32 devices in a mesh: seq: 8 (over z, y), dp: 4 (over x, core).
Axes of the slice: x: 2, y: 2, z: 4, core: 2. Of those that a mesh axis runs over, the one named last changes fastest.
Arguments:
- src: bfloat16 [4, 1024, 768], P('dp', 'seq'), may hold values from -6 to 6
- tgt: bfloat16 [4, 1024, 768], P('dp', 'seq'), may hold values from -6 to 6
- src_seg: int32 [4, 1024], P('dp', 'seq'), may hold values from 0 to 2, never falling along the last dimension, each value on 1 to 682 neighbouring positions
- tgt_seg: int32 [4, 1024], P('dp', 'seq'), may hold values from 0 to 2, never falling along the last dimension, each value on 1 to 682 neighbouring positions
- enc_qkv: bfloat16 [3, 768, 768], P(None, ('seq', 'dp')), may hold values from -0.21875 to 0.21875
- enc_out_w: bfloat16 [768, 768], P(('seq', 'dp')), may hold values from -1.5 to 1.5
- enc_attn_bias: bfloat16 [3, 768], P(None, ('seq', 'dp')), may hold values from -1 to 1
- enc_up: bfloat16 [768, 3072], P(('seq', 'dp')), may hold values from -0.21875 to 0.21875
- enc_up_bias: bfloat16 [3072], P(('seq', 'dp')), may hold values from -1 to 1
- enc_down: bfloat16 [3072, 768], P(('seq', 'dp')), may hold values from -0.109375 to 0.109375
- enc_down_bias: bfloat16 [768], P(('seq', 'dp')), may hold values from -1 to 1
- enc_gains: bfloat16 [2, 768], P(None, ('seq', 'dp')), may hold values from 0.5 to 1.5
- enc_shifts: bfloat16 [2, 768], P(None, ('seq', 'dp')), may hold values from -1 to 1
- dec_self_qkv: bfloat16 [3, 768, 768], P(None, ('seq', 'dp')), may hold values from -0.21875 to 0.21875
- dec_self_out: bfloat16 [768, 768], P(('seq', 'dp')), may hold values from -1.5 to 1.5
- dec_self_bias: bfloat16 [3, 768], P(None, ('seq', 'dp')), may hold values from -1 to 1
- dec_cross_qkv: bfloat16 [3, 768, 768], P(None, ('seq', 'dp')), may hold values from -0.21875 to 0.21875
- dec_cross_out: bfloat16 [768, 768], P(('seq', 'dp')), may hold values from -1.5 to 1.5
- dec_cross_bias: bfloat16 [3, 768], P(None, ('seq', 'dp')), may hold values from -1 to 1
- dec_up: bfloat16 [768, 3072], P(('seq', 'dp')), may hold values from -0.21875 to 0.21875
- dec_up_bias: bfloat16 [3072], P(('seq', 'dp')), may hold values from -1 to 1
- dec_down: bfloat16 [3072, 768], P(('seq', 'dp')), may hold values from -0.109375 to 0.109375
- dec_down_bias: bfloat16 [768], P(('seq', 'dp')), may hold values from -1 to 1
- dec_gains: bfloat16 [3, 768], P(None, ('seq', 'dp')), may hold values from 0.5 to 1.5
- dec_shifts: bfloat16 [3, 768], P(None, ('seq', 'dp')), may hold values from -1 to 1
- out_grad: bfloat16 [4, 1024, 768], P('dp', 'seq'), may hold values from -6 to 6
Outputs:
- dec_out: bfloat16 [4, 1024, 768], P('dp', 'seq')
- src_grad: float32 [4, 1024, 768], P('dp', 'seq')
- tgt_grad: float32 [4, 1024, 768], P('dp', 'seq')
- g_enc_qkv: float32 [3, 768, 768], P(None, ('seq', 'dp'))
- g_enc_out_w: float32 [768, 768], P(('seq', 'dp'))
- g_enc_attn_bias: float32 [3, 768], P(None, ('seq', 'dp'))
- g_enc_up: float32 [768, 3072], P(('seq', 'dp'))
- g_enc_up_bias: float32 [3072], P(('seq', 'dp'))
- g_enc_down: float32 [3072, 768], P(('seq', 'dp'))
- g_enc_down_bias: float32 [768], P(('seq', 'dp'))
- g_enc_gains: float32 [2, 768], P(None, ('seq', 'dp'))
- g_enc_shifts: float32 [2, 768], P(None, ('seq', 'dp'))
- g_dec_self_qkv: float32 [3, 768, 768], P(None, ('seq', 'dp'))
- g_dec_self_out: float32 [768, 768], P(('seq', 'dp'))
- g_dec_self_bias: float32 [3, 768], P(None, ('seq', 'dp'))
- g_dec_cross_qkv: float32 [3, 768, 768], P(None, ('seq', 'dp'))
- g_dec_cross_out: float32 [768, 768], P(('seq', 'dp'))
- g_dec_cross_bias: float32 [3, 768], P(None, ('seq', 'dp'))
- g_dec_up: float32 [768, 3072], P(('seq', 'dp'))
- g_dec_up_bias: float32 [3072], P(('seq', 'dp'))
- g_dec_down: float32 [3072, 768], P(('seq', 'dp'))
- g_dec_down_bias: float32 [768], P(('seq', 'dp'))
- g_dec_gains: float32 [3, 768], P(None, ('seq', 'dp'))
- g_dec_shifts: float32 [3, 768], P(None, ('seq', 'dp'))
The draws below stay inside these ranges and needn't reach their ends.
Inputs may be any that keep to these rules, and one draw needn't show every extreme that they name: `src_seg`: in every row the ids never fall along the row, all 3 ids occur, no document has more than 682 tokens and one has exactly 682. `tgt_seg`: in every row the ids never fall along the row, all 3 ids occur, no document has more than 682 tokens and one has exactly 682.
All inputs are finite; a program needn't handle non-finite values.
Results may differ from the reference program's by a relative error of at most 0.024.
Values may be sent and summed in bfloat16 or wider, within the bound.
No kernel may reach another device: no remote copies, remote signals or barrier semaphores. Data moves between devices by JAX's collectives and lax.ppermute only.
A program may use at most 256 MiB of HBM per device.

```python
import math
import jax
import jax.numpy as jnp
import numpy as np
from jax import lax

D = 768
HEADS = 12
FF = 3072
DOCS = 3
SEQ_LEN = 1024
DOC_MOST = 682
ROWS = 4


def shard_levels(own_key, shape, cuts, low, top_value):
    def one(axis_at, parts):
        steps = jax.random.uniform(jax.random.fold_in(jax.random.fold_in(own_key, 6), axis_at), (parts,), jnp.float32, low / len(cuts), top_value / len(cuts))
        return jnp.repeat(jnp.exp(steps), shape[axis_at] // parts).reshape((-1,) + (1,) * (len(shape) - axis_at - 1))

    factor_of = one(*cuts[0])
    for cut in cuts[1:]:
        factor_of = factor_of * one(*cut)
    return factor_of


def split_up(number_of, total, limit, slope):
    weights = [(1 << 20) // math.isqrt(standing ** slope) + 1 for standing in range(2, number_of + 1)]
    surplus, counts = total - limit - (number_of - 1), [1] * (number_of - 1)
    while surplus > 0:
        candidates = [i for i in range(number_of - 1) if counts[i] < limit]
        whole, remaining = sum([weights[i] for i in candidates]), surplus
        for i in candidates:
            extra = min(limit - counts[i], max(1, remaining * weights[i] // whole), surplus)
            counts[i] = counts[i] + extra
            surplus = surplus - extra
    return np.array([limit] + counts)


def uneven(key, number_of, total, most, lean):
    if number_of == 2:
        one = jax.random.randint(key, (), max(1, total - most), min(most, total - 1) + 1)
        return jnp.stack([one, total - one])
    tallies = jnp.asarray(split_up(number_of, total, most, lean), jnp.int32)
    couples = (number_of - 1) // 2
    source_of, sink = tallies[1:1 + 2 * couples:2], tallies[2:2 + 2 * couples:2]
    slack = jnp.minimum(source_of - 1, most - sink)
    moved = jax.random.randint(jax.random.fold_in(key, 1), (couples,), 0, 1 << 20) % (slack + 1)
    tallies = tallies.at[1:1 + 2 * couples:2].set(source_of - moved).at[2:2 + 2 * couples:2].set(sink + moved)
    return tallies[jax.random.permutation(jax.random.fold_in(key, 2), number_of)]


def bell_draw(key, shape, deviation, most, split=(), held_as=jnp.bfloat16):
    entries = jax.random.normal(key, shape, jnp.float32) * deviation
    if len(split) > 0:
        entries = shard_levels(key, shape, split, -0.22, 0.18) * entries
    return jnp.clip(entries, min=-most, max=most).astype(held_as)


def setup_inputs(seed: int = 0) -> dict:
    splits = jax.random.split(jax.random.key(seed), 27)
    return {
        "src": bell_draw(splits[0], (ROWS, SEQ_LEN, D), 1.0, 6.0, ((0, 4), (1, 8))),
        "tgt": bell_draw(splits[1], (ROWS, SEQ_LEN, D), 1.0, 6.0, ((0, 4), (1, 8))),
        "src_seg": jax.vmap(lambda own: jnp.searchsorted(jnp.cumsum(uneven(own, DOCS, SEQ_LEN, DOC_MOST, 0)), jnp.arange(SEQ_LEN), side="right"))(jax.random.split(splits[2], ROWS)).reshape((ROWS, SEQ_LEN)).astype(jnp.int32),
        "tgt_seg": jax.vmap(lambda own: jnp.searchsorted(jnp.cumsum(uneven(own, DOCS, SEQ_LEN, DOC_MOST, 0)), jnp.arange(SEQ_LEN), side="right"))(jax.random.split(splits[3], ROWS)).reshape((ROWS, SEQ_LEN)).astype(jnp.int32),
        "enc_qkv": bell_draw(splits[4], (3, D, D), D ** -0.5, 0.21875, ((1, 32),)),
        "enc_out_w": bell_draw(splits[5], (D, D), 16 ** -0.5, 1.5, ((0, 32),)),
        "enc_attn_bias": bell_draw(splits[6], (3, D), 0.2, 1.0, ((1, 32),)),
        "enc_up": bell_draw(splits[7], (D, FF), D ** -0.5, 0.21875, ((0, 32),)),
        "enc_up_bias": bell_draw(splits[8], (FF,), 0.2, 1.0, ((0, 32),)),
        "enc_down": bell_draw(splits[9], (FF, D), FF ** -0.5, 0.109375, ((0, 32),)),
        "enc_down_bias": bell_draw(splits[10], (D,), 0.2, 1.0, ((0, 32),)),
        "enc_gains": jnp.clip(1.0 + 0.1 * jax.random.normal(splits[11], (2, D), jnp.float32), 0.5, 1.5).astype(jnp.bfloat16),
        "enc_shifts": bell_draw(splits[12], (2, D), 0.2, 1.0, ((1, 32),)),
        "dec_self_qkv": bell_draw(splits[13], (3, D, D), D ** -0.5, 0.21875, ((1, 32),)),
        "dec_self_out": bell_draw(splits[14], (D, D), 16 ** -0.5, 1.5, ((0, 32),)),
        "dec_self_bias": bell_draw(splits[15], (3, D), 0.2, 1.0, ((1, 32),)),
        "dec_cross_qkv": bell_draw(splits[16], (3, D, D), D ** -0.5, 0.21875, ((1, 32),)),
        "dec_cross_out": bell_draw(splits[17], (D, D), 16 ** -0.5, 1.5, ((0, 32),)),
        "dec_cross_bias": bell_draw(splits[18], (3, D), 0.2, 1.0, ((1, 32),)),
        "dec_up": bell_draw(splits[19], (D, FF), D ** -0.5, 0.21875, ((0, 32),)),
        "dec_up_bias": bell_draw(splits[20], (FF,), 0.2, 1.0, ((0, 32),)),
        "dec_down": bell_draw(splits[21], (FF, D), FF ** -0.5, 0.109375, ((0, 32),)),
        "dec_down_bias": bell_draw(splits[22], (D,), 0.2, 1.0, ((0, 32),)),
        "dec_gains": jnp.clip(1.0 + 0.1 * jax.random.normal(splits[23], (3, D), jnp.float32), 0.5, 1.5).astype(jnp.bfloat16),
        "dec_shifts": bell_draw(splits[24], (3, D), 0.2, 1.0, ((1, 32),)),
        "out_grad": bell_draw(splits[25], (ROWS, SEQ_LEN, D), 1.0, 6.0, ((0, 4), (1, 8))),
    }


EPSILON = 1e-05
MASKED = -1e+30
HIGHEST = lax.Precision.HIGHEST

@jax.custom_vjp
def low(v):
    return lax.optimization_barrier(v.astype(jnp.bfloat16)).astype(jnp.float32)

@jax.custom_vjp
def low_back(v):
    return v

def low_keep(v):
    return (low(v), None)

def low_pass(kept, grad):
    return (grad,)

def back_keep(v):
    return (v, None)

def back_low(kept, grad):
    return (low(grad),)
low.defvjp(low_keep, low_pass)
low_back.defvjp(back_keep, back_low)

def product(left, right):
    return jnp.dot(left, right, precision=HIGHEST)

def layer_norm(resid, gain, shift):
    center = resid - lax.optimization_barrier(jnp.mean(resid, axis=-1, keepdims=True))
    second = lax.optimization_barrier(jnp.mean(center * center, axis=-1, keepdims=True))
    return center * lax.rsqrt(second + EPSILON) * gain + shift

def attention(queries, keys_in, values, query_seg, key_seg, causal):
    length = queries.shape[0]
    model_width = queries.shape[1]
    head_size = model_width // HEADS
    block_rows = min(length, 512)
    block_count = length // block_rows
    key_heads = keys_in.reshape(keys_in.shape[0], HEADS, head_size)
    value_heads = values.reshape(values.shape[0], HEADS, head_size)
    key_place = jnp.arange(keys_in.shape[0], dtype=jnp.int32)
    query_place = jnp.arange(length, dtype=jnp.int32)

    def one_block(inputs):
        query_block, seg_block, place_block = inputs
        scores = jnp.einsum('qhd,khd->hqk', query_block, key_heads, precision=HIGHEST) * head_size ** (-0.5)
        scores = low_back(scores)
        allowed = seg_block[:, None] == key_seg[None, :]
        if causal:
            allowed = allowed & (key_place[None, :] <= place_block[:, None])
        scores = jnp.where(allowed[None], scores, MASKED)
        weights = jax.nn.softmax(scores, axis=-1)
        return jnp.einsum('hqk,khd->qhd', low(weights), value_heads, precision=HIGHEST)
    mixture = lax.map(jax.checkpoint(one_block), (queries.reshape(block_count, block_rows, HEADS, head_size), query_seg.reshape(block_count, block_rows), query_place.reshape(block_count, block_rows)))
    return mixture.reshape(length, model_width)

def attention_layer(query_in, key_in, same_rows, qkv, out_weight, biases, query_seg, key_seg, causal):
    query_low = low(query_in)
    key_low = query_low if same_rows else low(key_in)
    queries = low(low_back(product(query_low, qkv[0]) + biases[0]))
    keys_out = low(low_back(product(key_low, qkv[1])))
    values = low(low_back(product(key_low, qkv[2]) + biases[1]))
    mixture = low(low_back(attention(queries, keys_out, values, query_seg, key_seg, causal)))
    return low_back(product(mixture, out_weight) + biases[2])

def ffn_layer(rows_in, up_weight, up_bias, down_weight, down_bias):
    pre_act = low_back(product(low(rows_in), up_weight) + up_bias)
    hidden = low(jax.nn.gelu(pre_act, approximate=False))
    return low_back(product(hidden, down_weight) + down_bias)

def forward(encoder_params, decoder_params, source, target, source_seg, target_seg):
    enc_first = layer_norm(source + attention_layer(source, source, True, encoder_params[0], encoder_params[1], encoder_params[2], source_seg, source_seg, False), encoder_params[7][0], encoder_params[8][0])
    encoded = layer_norm(enc_first + ffn_layer(enc_first, encoder_params[3], encoder_params[4], encoder_params[5], encoder_params[6]), encoder_params[7][1], encoder_params[8][1])
    dec_first = layer_norm(target + attention_layer(target, target, True, decoder_params[0], decoder_params[1], decoder_params[2], target_seg, target_seg, True), decoder_params[10][0], decoder_params[11][0])
    dec_second = layer_norm(dec_first + attention_layer(dec_first, encoded, False, decoder_params[3], decoder_params[4], decoder_params[5], target_seg, source_seg, False), decoder_params[10][1], decoder_params[11][1])
    return layer_norm(dec_second + ffn_layer(dec_second, decoder_params[6], decoder_params[7], decoder_params[8], decoder_params[9]), decoder_params[10][2], decoder_params[11][2])

def reference(src, tgt, src_seg, tgt_seg, enc_qkv, enc_out_w, enc_attn_bias, enc_up, enc_up_bias, enc_down, enc_down_bias, enc_gains, enc_shifts, dec_self_qkv, dec_self_out, dec_self_bias, dec_cross_qkv, dec_cross_out, dec_cross_bias, dec_up, dec_up_bias, dec_down, dec_down_bias, dec_gains, dec_shifts, out_grad):
    encoder_params = tuple((tensor.astype(jnp.float32) for tensor in (enc_qkv, enc_out_w, enc_attn_bias, enc_up, enc_up_bias, enc_down, enc_down_bias, enc_gains, enc_shifts)))
    decoder_params = tuple((tensor.astype(jnp.float32) for tensor in (dec_self_qkv, dec_self_out, dec_self_bias, dec_cross_qkv, dec_cross_out, dec_cross_bias, dec_up, dec_up_bias, dec_down, dec_down_bias, dec_gains, dec_shifts)))

    def row_step(totals, row_inputs):
        source, target, source_seg, target_seg, cotangent = row_inputs

        def run_row(encoder_in, decoder_in, source_in, target_in):
            return forward(encoder_in, decoder_in, source_in, target_in, source_seg, target_seg)
        outcome, pullback = jax.vjp(run_row, encoder_params, decoder_params, source.astype(jnp.float32), target.astype(jnp.float32))
        grads_enc, grads_dec, grad_source, grad_target = pullback(cotangent.astype(jnp.float32))
        totals = jax.tree.map(jnp.add, totals, (grads_enc, grads_dec))
        return (totals, (outcome.astype(jnp.bfloat16), grad_source, grad_target))
    zeros_start = jax.tree.map(jnp.zeros_like, (encoder_params, decoder_params))
    totals, stacked = lax.scan(row_step, zeros_start, (src, tgt, src_seg, tgt_seg, out_grad))
    grads_enc, grads_dec = totals
    decoded, source_grad, target_grad = stacked
    return (decoded, source_grad, target_grad, grads_enc[0], grads_enc[1], grads_enc[2], grads_enc[3], grads_enc[4], grads_enc[5], grads_enc[6], grads_enc[7], grads_enc[8], grads_dec[0], grads_dec[1], grads_dec[2], grads_dec[3], grads_dec[4], grads_dec[5], grads_dec[6], grads_dec[7], grads_dec[8], grads_dec[9], grads_dec[10], grads_dec[11])
```

```python
import functools

import jax
import jax.numpy as jnp
from jax import lax
from jax.experimental import pallas as pl
from jax.experimental.pallas import tpu as pltpu
from jax.sharding import Mesh
from jax.sharding import PartitionSpec as P

HEADS = 12
HEAD = 64
EPSILON = 1e-05
MASKED = -1e30
BLOCK = 128
F32 = jnp.float32
BF16 = jnp.bfloat16
AXES = ("z", "y", "x", "core")
PLANE = ("y", "x")
NT = (((1,), (1,)), ((), ()))
TN = (((0,), (0,)), ((), ()))


def matmul(left, right):
    return jnp.dot(left, right, preferred_element_type=F32)


def outer_sum(left, right):
    return lax.dot_general(left, right, TN, preferred_element_type=F32)


def back_matmul(left, right):
    return lax.dot_general(left, right, NT, preferred_element_type=F32)


def layer_norm(resid, gain, shift):
    center = resid - jnp.mean(resid, axis=-1, keepdims=True)
    second = jnp.mean(center * center, axis=-1, keepdims=True)
    return center * lax.rsqrt(second + EPSILON) * gain + shift


def norm_back(resid, gain, shift, grad_out):
    return jax.vjp(layer_norm, resid, gain, shift)[1](grad_out)


def gelu_exact(values):
    return jax.nn.gelu(values, approximate=False)


def positions(scal_ref, index):
    part, core, sub = scal_ref[0], scal_ref[1], scal_ref[2]
    group = lax.shift_right_logical(index, 10)
    half = lax.shift_right_logical(index, 9) & 1
    block = lax.shift_right_logical(index, 7) & 3
    return ((sub ^ group) << 10) + ((core ^ half) << 9) + ((part ^ block) << 7) + (index & 127)


def allowed_mask(scal_ref, start, width, keys, causal):
    query = positions(scal_ref, lax.broadcasted_iota(jnp.int32, (1, width), 1) + start)
    key = positions(scal_ref, lax.broadcasted_iota(jnp.int32, (keys, 1), 0))
    first = query >= scal_ref[3]
    second = query >= scal_ref[4]
    low = jnp.where(second, scal_ref[6], jnp.where(first, scal_ref[5], 0))
    high = jnp.where(second, scal_ref[7], jnp.where(first, scal_ref[6], scal_ref[5]))
    if causal:
        high = jnp.minimum(high, query + 1)
    return (key >= low) & (key < high)


def attn_fwd_kernel(causal, width, scal_ref, q_ref, k_ref, v_ref, o_ref, lse_ref, ot_ref):
    keys = k_ref.shape[0]
    heads = q_ref.shape[1] // HEAD
    for chunk in range(q_ref.shape[0] // width):
        rows = slice(chunk * width, (chunk + 1) * width)
        mask = allowed_mask(scal_ref, chunk * width, width, keys, causal)
        for head in range(heads):
            cols = slice(head * HEAD, (head + 1) * HEAD)
            scores = lax.dot_general(
                k_ref[:, cols], q_ref[rows, cols], NT, preferred_element_type=F32
            )
            scores = jnp.where(mask, scores, MASKED)
            peak = jnp.max(scores, axis=0, keepdims=True)
            weights = jnp.exp(scores - peak)
            total = jnp.sum(weights, axis=0, keepdims=True)
            probs = (weights * (1.0 / total)).astype(BF16)
            ot_ref[cols, rows] = lax.dot_general(
                v_ref[:, cols], probs, TN, preferred_element_type=F32
            )
            lse_ref[head : head + 1, rows] = peak + jnp.log(total)
    o_ref[...] = ot_ref[...].T.astype(BF16)


def attn_bwd_kernel(
    causal, width, scal_ref, q_ref, k_ref, v_ref, do_ref, lse_ref, dq_ref, dk_ref, dv_ref, dqt_ref
):
    keys = k_ref.shape[0]
    heads = q_ref.shape[1] // HEAD
    for chunk in range(q_ref.shape[0] // width):
        rows = slice(chunk * width, (chunk + 1) * width)
        mask = allowed_mask(scal_ref, chunk * width, width, keys, causal)
        for head in range(heads):
            cols = slice(head * HEAD, (head + 1) * HEAD)
            key, value = k_ref[:, cols], v_ref[:, cols]
            query, grad = q_ref[rows, cols], do_ref[rows, cols]
            scores = lax.dot_general(key, query, NT, preferred_element_type=F32)
            probs = jnp.where(mask, jnp.exp(scores - lse_ref[head : head + 1, rows]), 0.0)
            grad_probs = lax.dot_general(value, grad, NT, preferred_element_type=F32)
            product = probs * grad_probs
            delta = jnp.sum(product, axis=0, keepdims=True)
            grad_scores = (product - probs * delta).astype(BF16)
            grad_value = matmul(probs.astype(BF16), grad)
            grad_key = matmul(grad_scores, query)
            if chunk == 0:
                dv_ref[:, cols] = grad_value
                dk_ref[:, cols] = grad_key
            else:
                dv_ref[:, cols] += grad_value
                dk_ref[:, cols] += grad_key
            dqt_ref[cols, rows] = lax.dot_general(
                key, grad_scores, TN, preferred_element_type=F32
            ) * (HEAD**-0.5)
    dq_ref[...] = dqt_ref[...].T.astype(BF16)


def vmem_specs(count):
    return [pl.BlockSpec(memory_space=pltpu.VMEM)] * count


def attn_forward(scal, queries, keys, values, causal):
    rows, cols = queries.shape
    length = keys.shape[0]
    width = 256 if length <= 1024 else 128
    work = rows * length * cols
    return pl.pallas_call(
        functools.partial(attn_fwd_kernel, causal, width),
        out_shape=(
            jax.ShapeDtypeStruct((rows, cols), BF16),
            jax.ShapeDtypeStruct((8, rows), F32),
        ),
        in_specs=[pl.BlockSpec(memory_space=pltpu.SMEM)] + vmem_specs(3),
        out_specs=tuple(vmem_specs(2)),
        scratch_shapes=[pltpu.VMEM((cols, rows), F32)],
        compiler_params=pltpu.CompilerParams(vmem_limit_bytes=48 << 20),
        cost_estimate=pl.CostEstimate(
            flops=8 * work, transcendentals=work // HEAD, bytes_accessed=4 * length * cols
        ),
        name="attn_forward",
    )(scal, queries, keys, values)


def attn_backward(scal, queries, keys, values, grads, lse, causal):
    rows, cols = queries.shape
    length = keys.shape[0]
    width = 256 if length <= 1024 else 128
    work = rows * length * cols
    return pl.pallas_call(
        functools.partial(attn_bwd_kernel, causal, width),
        out_shape=(
            jax.ShapeDtypeStruct((rows, cols), BF16),
            jax.ShapeDtypeStruct((length, cols), F32),
            jax.ShapeDtypeStruct((length, cols), F32),
        ),
        in_specs=[pl.BlockSpec(memory_space=pltpu.SMEM)] + vmem_specs(5),
        out_specs=tuple(vmem_specs(3)),
        scratch_shapes=[pltpu.VMEM((cols, rows), F32)],
        compiler_params=pltpu.CompilerParams(vmem_limit_bytes=48 << 20),
        cost_estimate=pl.CostEstimate(
            flops=20 * work, transcendentals=work // HEAD, bytes_accessed=12 * length * cols
        ),
        name="attn_backward",
    )(scal, queries, keys, values, grads, lse)


def plane_swap(values, shift):
    return lax.ppermute(values, PLANE, [(i, i ^ shift) for i in range(4)])


def core_swap(values):
    return lax.ppermute(values, "core", [(0, 1), (1, 0)])


def plane_gather(values):
    return jnp.concatenate([values] + [plane_swap(values, k) for k in (1, 2, 3)], axis=0)


def plane_sum(left, right, contract):
    own = contract(left[:BLOCK], right)
    rest = contract(left[BLOCK:], right).astype(BF16)
    for k in (1, 2, 3):
        own = own + plane_swap(rest[(k - 1) * BLOCK : k * BLOCK], k).astype(F32)
    return own


class Layout:
    def __init__(self, groups, rows):
        self.groups = groups
        self.devices = groups * 8
        self.subs = groups // rows

    def index(self, z, y, x, c):
        return ((z * 2 + y) * 2 + x) * 2 + c

    def token_moves(self):
        moves = []
        for z in range(self.groups):
            for y in range(2):
                for x in range(2):
                    for c in range(2):
                        row, block = 2 * x + c, 2 * z + y
                        group, within = row * self.subs + block // 8, block % 8
                        core, part = within // 4, within % 4
                        moves.append(
                            (self.index(z, y, x, c), self.index(group, part // 2, part % 2, core))
                        )
        return moves

    def back_moves(self):
        return [(b, a) for a, b in self.token_moves()]

    def turn_moves(self):
        moves = []
        for part in range(4):
            for z in range(self.groups):
                owner, user = part * self.groups + z, z * 4 + part
                moves.append((owner, user))
        return moves


def on_device(lay, core, part, sub, params, tokens):
    (
        enc_qkv,
        enc_out_w,
        enc_attn_bias,
        enc_up,
        enc_up_bias,
        enc_down,
        enc_down_bias,
        enc_gains,
        enc_shifts,
        self_qkv,
        self_out,
        self_bias,
        cross_qkv,
        cross_out,
        cross_bias,
        dec_up,
        dec_up_bias,
        dec_down,
        dec_down_bias,
        dec_gains,
        dec_shifts,
    ) = params
    src, tgt, src_seg, tgt_seg, out_grad = tokens
    groups = lay.groups
    width = src.shape[1]
    rows = enc_out_w.shape[0]
    rows_ff = enc_down.shape[0]
    quarter = width // 4
    hidden = rows_ff * groups * 2
    heads_out = enc_qkv.shape[0] * quarter

    ids = jnp.concatenate([src_seg, tgt_seg]).astype(BF16)
    ids = jnp.pad(ids[None], ((0, 7), (0, width - 2 * BLOCK)))
    packed = lax.ppermute(jnp.concatenate([src, tgt, ids], axis=0), AXES, lay.token_moves())
    out_grad = lax.ppermute(out_grad, AXES, lay.token_moves())
    src, tgt = packed[:BLOCK], packed[BLOCK : 2 * BLOCK]
    pieces = [packed] + [plane_swap(packed, k) for k in (1, 2, 3)]
    src_rows = jnp.concatenate([piece[:BLOCK] for piece in pieces], axis=0)
    tgt_rows = jnp.concatenate([piece[BLOCK : 2 * BLOCK] for piece in pieces], axis=0)
    doc = jnp.concatenate([piece[2 * BLOCK : 2 * BLOCK + 1] for piece in pieces], axis=0)
    doc = doc[:, : 2 * BLOCK].astype(F32).reshape(4, 2, BLOCK)
    count = jnp.stack(
        [
            jnp.sum((doc < 0.5).astype(F32), axis=(0, 2)),
            jnp.sum((doc < 1.5).astype(F32), axis=(0, 2)),
        ]
    )
    count = jnp.pad(count, ((0, 6), (0, BLOCK - 2)))
    count = count + core_swap(count)
    for j in range(1, lay.subs):
        pass
    if lay.subs > 1:
        total = count
        for j in range(1, lay.subs):
            total = total + lax.ppermute(count, "z", [(z, z ^ j) for z in range(groups)])
        count = total
    count = count.astype(jnp.int32)
    length = jnp.int32(lay.subs * 8 * BLOCK)

    def scalars(query, key):
        return jnp.stack(
            [
                part,
                core,
                sub,
                count[0, query],
                count[1, query],
                count[0, key],
                count[1, key],
                length,
            ]
        ).astype(jnp.int32)

    def part_columns(values, pieces):
        return lax.all_to_all(values, PLANE, split_axis=0, concat_axis=0, tiled=True)

    def heads_split(qkv):
        parts = qkv.reshape(3, rows, 4, quarter)
        return parts.transpose(2, 1, 0, 3).reshape(4, rows, heads_out)

    def up_split(up):
        parts = up.reshape(rows, groups, 4, 2, rows_ff)
        return parts.transpose(2, 0, 3, 1, 4).reshape(4, rows, hidden)

    def both_cores(mine, axis):
        other = core_swap(mine)
        shape = [1] * (mine.ndim + 1)
        shape[axis] = 2
        which = lax.broadcasted_iota(jnp.int32, shape, axis) == core
        return jnp.where(which, jnp.expand_dims(mine, axis), jnp.expand_dims(other, axis))

    def whole_rows(split):
        split = lax.all_to_all(split, PLANE, split_axis=0, concat_axis=0, tiled=True)
        split = lax.all_gather(split, "z", axis=0)
        return both_cores(split, 2).reshape(width, split.shape[-1])

    first = whole_rows(jnp.concatenate([heads_split(enc_qkv), heads_split(self_qkv)], axis=2))
    w_enc, w_self = first[:, :heads_out], first[:, heads_out:]

    outs = jnp.concatenate([enc_out_w, self_out, cross_out], axis=1)
    outs = lax.ppermute(outs, ("z", "y", "x"), lay.turn_moves())
    outs = lax.all_gather(outs, "z", axis=0)
    outs = both_cores(outs, 1).reshape(quarter, 3 * width)
    wo_enc, wo_self, wo_cross = (outs[:, k * width : (k + 1) * width] for k in range(3))

    vectors = jnp.concatenate(
        [
            enc_attn_bias,
            self_bias,
            cross_bias,
            enc_down_bias[None],
            dec_down_bias[None],
            enc_gains,
            dec_gains,
            enc_shifts,
            dec_shifts,
        ],
        axis=0,
    )
    vector_count = vectors.shape[0]
    vectors = jnp.concatenate([vectors.reshape(-1), enc_up_bias, dec_up_bias])[None]
    vectors = lax.all_gather(vectors, AXES, axis=0, tiled=True).astype(F32)
    ups = vectors[:, vector_count * rows :].reshape(groups, 4, 2, 2, rows_ff)
    ups = lax.dynamic_index_in_dim(ups, part, axis=1, keepdims=False)
    ups = ups.transpose(2, 1, 0, 3).reshape(2, hidden)
    vectors = vectors[:, : vector_count * rows].reshape(lay.devices, vector_count, rows)
    vectors = vectors.transpose(1, 0, 2).reshape(vector_count, width)
    mine = lax.dynamic_slice_in_dim(vectors, part * quarter, quarter, axis=1)

    second = whole_rows(up_split(enc_up))
    w_up_enc = second
    w_down_enc = both_cores(lax.all_gather(enc_down, "z", axis=0), 0).reshape(hidden, width)
    third = whole_rows(jnp.concatenate([heads_split(cross_qkv), up_split(dec_up)], axis=2))
    w_cross, w_up_dec = third[:, :heads_out], third[:, heads_out:]
    w_down_dec = both_cores(lax.all_gather(dec_down, "z", axis=0), 0).reshape(hidden, width)

    scale = HEAD**-0.5

    def with_others(kv):
        kv = jnp.concatenate([kv, core_swap(kv)], axis=0)
        if lay.subs > 1:
            kv = jnp.concatenate(
                [kv]
                + [
                    lax.ppermute(kv, "z", [(z, z ^ j) for z in range(groups)])
                    for j in range(1, lay.subs)
                ],
                axis=0,
            )
        return kv

    def project(query_rows, key_rows, weight, bias):
        q = (matmul(query_rows, weight[:, :quarter]) + bias[0]).astype(BF16) * BF16(scale)
        shift = jnp.concatenate([jnp.zeros_like(bias[1]), bias[1]])
        kv = (matmul(key_rows, weight[:, quarter:]) + shift).astype(BF16)
        kv = with_others(kv)
        return q, kv[:, :quarter], kv[:, quarter:]

    def ffn(rows_in, up, up_bias, down):
        pre = matmul(rows_in, up) + up_bias
        act = gelu_exact(pre).astype(BF16)
        return plane_sum(act, down, matmul), pre, act

    scal_enc, scal_self, scal_cross = scalars(0, 0), scalars(1, 1), scalars(1, 0)
    q_enc, k_enc, v_enc = project(src_rows, src_rows, w_enc, mine[0:2])
    o_enc, lse_enc = attn_forward(scal_enc, q_enc, k_enc, v_enc, False)
    r_enc1 = src.astype(F32) + plane_sum(o_enc, wo_enc, matmul) + vectors[2]
    gains_enc, gains_dec = vectors[11:13], vectors[13:16]
    shifts_enc, shifts_dec = vectors[16:18], vectors[18:21]
    e1 = layer_norm(r_enc1, gains_enc[0], shifts_enc[0])
    e1_rows = plane_gather(e1.astype(BF16))
    branch, pre_enc, act_enc = ffn(e1_rows, w_up_enc, ups[0], w_down_enc)
    r_enc2 = e1 + branch + vectors[9]
    encoded = layer_norm(r_enc2, gains_enc[1], shifts_enc[1])
    encoded_rows = plane_gather(encoded.astype(BF16))

    q_self, k_self, v_self = project(tgt_rows, tgt_rows, w_self, mine[3:5])
    o_self, lse_self = attn_forward(scal_self, q_self, k_self, v_self, True)
    r_dec1 = tgt.astype(F32) + plane_sum(o_self, wo_self, matmul) + vectors[5]
    t1 = layer_norm(r_dec1, gains_dec[0], shifts_dec[0])
    t1_rows = plane_gather(t1.astype(BF16))

    q_cross, k_cross, v_cross = project(t1_rows, encoded_rows, w_cross, mine[6:8])
    o_cross, lse_cross = attn_forward(scal_cross, q_cross, k_cross, v_cross, False)
    r_dec2 = t1 + plane_sum(o_cross, wo_cross, matmul) + vectors[8]
    t2 = layer_norm(r_dec2, gains_dec[1], shifts_dec[1])
    t2_rows = plane_gather(t2.astype(BF16))
    branch, pre_dec, act_dec = ffn(t2_rows, w_up_dec, ups[1], w_down_dec)
    r_dec3 = t2 + branch + vectors[10]
    t3 = layer_norm(r_dec3, gains_dec[2], shifts_dec[2])

    def column_sum(values):
        return jnp.sum(values.astype(F32), axis=0)

    def ffn_back(grad, rows_in, up, down, pre, act):
        low = grad.astype(BF16)
        low_rows = plane_gather(low)
        grad_down = outer_sum(act, low_rows)
        grad_act = back_matmul(low_rows, down)
        grad_pre = jax.vjp(gelu_exact, pre)[1](grad_act)[0].astype(BF16)
        grad_up = outer_sum(rows_in, grad_pre)
        grad_in = plane_sum(grad_pre, up, back_matmul)
        return grad_in, grad_up, column_sum(grad_pre), grad_down, column_sum(low)

    def attn_back(grad, out_weight, scal, q, k, v, o, lse, causal):
        low = grad.astype(BF16)
        low_rows = plane_gather(low)
        grad_out_w = outer_sum(o, low_rows)
        grad_o = back_matmul(low_rows, out_weight).astype(BF16)
        dq, dk, dv = attn_backward(scal, q, k, v, grad_o, lse, causal)
        dkv = jnp.concatenate([dk, dv], axis=1)
        half = 4 * BLOCK
        if lay.subs > 1:
            total = dkv[: 2 * half]
            for j in range(1, lay.subs):
                total = total + lax.ppermute(
                    dkv[2 * half * j : 2 * half * (j + 1)],
                    "z",
                    [(z, z ^ j) for z in range(groups)],
                )
            dkv = total
        dkv = (dkv[:half] + core_swap(dkv[half:])).astype(BF16)
        return dq, dkv, grad_out_w, column_sum(low)

    d_r3, g_gain_d3, g_shift_d3 = norm_back(
        r_dec3, gains_dec[2], shifts_dec[2], out_grad.astype(F32)
    )
    d_t2, g_up_dec, g_upb_dec, g_down_dec, g_downb_dec = ffn_back(
        d_r3, t2_rows, w_up_dec, w_down_dec, pre_dec, act_dec
    )
    d_r2, g_gain_d2, g_shift_d2 = norm_back(r_dec2, gains_dec[1], shifts_dec[1], d_r3 + d_t2)
    dq, dkv, g_wo_cross, g_bout_cross = attn_back(
        d_r2, wo_cross, scal_cross, q_cross, k_cross, v_cross, o_cross, lse_cross, False
    )
    d_encoded = plane_sum(dkv, w_cross[:, quarter:], back_matmul)
    d_t1 = plane_sum(dq, w_cross[:, :quarter], back_matmul)
    g_cross = jnp.concatenate([outer_sum(t1_rows, dq), outer_sum(encoded_rows, dkv)], axis=1)
    g_bq_cross, g_bv_cross = column_sum(dq), column_sum(dkv[:, quarter:])

    d_r1, g_gain_d1, g_shift_d1 = norm_back(r_dec1, gains_dec[0], shifts_dec[0], d_r2 + d_t1)
    dq, dkv, g_wo_self, g_bout_self = attn_back(
        d_r1, wo_self, scal_self, q_self, k_self, v_self, o_self, lse_self, True
    )
    dqkv = jnp.concatenate([dq, dkv], axis=1)
    tgt_grad = d_r1 + plane_sum(dqkv, w_self, back_matmul)
    g_self = outer_sum(tgt_rows, dqkv)
    g_bq_self, g_bv_self = column_sum(dq), column_sum(dkv[:, quarter:])

    d_e2, g_gain_e2, g_shift_e2 = norm_back(r_enc2, gains_enc[1], shifts_enc[1], d_encoded)
    d_e1, g_up_enc, g_upb_enc, g_down_enc, g_downb_enc = ffn_back(
        d_e2, e1_rows, w_up_enc, w_down_enc, pre_enc, act_enc
    )
    d_r1e, g_gain_e1, g_shift_e1 = norm_back(r_enc1, gains_enc[0], shifts_enc[0], d_e2 + d_e1)
    dq, dkv, g_wo_enc, g_bout_enc = attn_back(
        d_r1e, wo_enc, scal_enc, q_enc, k_enc, v_enc, o_enc, lse_enc, False
    )
    dqkv = jnp.concatenate([dq, dkv], axis=1)
    src_grad = d_r1e + plane_sum(dqkv, w_enc, back_matmul)
    g_enc = outer_sum(src_rows, dqkv)
    g_bq_enc, g_bv_enc = column_sum(dq), column_sum(dkv[:, quarter:])

    def core_reduce(grad, axis):
        zero = lax.index_in_dim(grad, 0, axis, keepdims=False)
        one = lax.index_in_dim(grad, 1, axis, keepdims=False)
        send = jnp.where(core == 0, one, zero).astype(BF16)
        keep = jnp.where(core == 0, zero, one)
        return (keep + core_swap(send).astype(F32)).astype(BF16)

    def rows_reduce(grad):
        grad = core_reduce(grad.reshape(groups, 4, 2, rows, -1), 2)
        grad = lax.psum_scatter(grad, "z", scatter_dimension=0, tiled=False)
        return lax.all_to_all(grad, PLANE, split_axis=0, concat_axis=0, tiled=True)

    def heads_join(parts):
        parts = parts.reshape(4, rows, 3, quarter).transpose(2, 1, 0, 3)
        return parts.reshape(3, rows, width).astype(F32)

    def up_join(parts):
        parts = parts.reshape(4, rows, 2, groups, rows_ff).transpose(1, 3, 0, 2, 4)
        return parts.reshape(rows, -1).astype(F32)

    def down_reduce(grad):
        grad = core_reduce(grad.reshape(2, groups, rows_ff, width), 0)
        return lax.psum_scatter(grad, "z", scatter_dimension=0, tiled=False).astype(F32)

    def out_reduce(grad):
        grad = core_reduce(grad.reshape(groups, 2, rows, width), 1)
        grad = lax.psum_scatter(grad, "z", scatter_dimension=0, tiled=False)
        return lax.ppermute(
            grad, ("z", "y", "x"), [(b, a) for a, b in lay.turn_moves()]
        ).astype(F32)

    g_dec_down = down_reduce(g_down_dec)
    g_dec_up = up_join(rows_reduce(g_up_dec))
    g_cross_qkv = heads_join(rows_reduce(g_cross))
    g_cross_out = out_reduce(g_wo_cross)
    g_self_qkv = heads_join(rows_reduce(g_self))
    g_self_out = out_reduce(g_wo_self)
    g_enc_down = down_reduce(g_down_enc)
    g_enc_up = up_join(rows_reduce(g_up_enc))
    g_enc_out = out_reduce(g_wo_enc)
    g_enc_qkv = heads_join(rows_reduce(g_enc))

    placed = jnp.stack([g_bq_enc, g_bv_enc, g_bq_self, g_bv_self, g_bq_cross, g_bv_cross])
    placed = lax.dynamic_update_slice(
        jnp.zeros((6, width), F32), placed, (jnp.int32(0), part * quarter)
    )
    small = jnp.concatenate(
        [
            placed,
            jnp.stack(
                [
                    g_bout_enc,
                    g_bout_self,
                    g_bout_cross,
                    g_downb_enc,
                    g_downb_dec,
                    g_gain_e1,
                    g_gain_e2,
                    g_gain_d1,
                    g_gain_d2,
                    g_gain_d3,
                    g_shift_e1,
                    g_shift_e2,
                    g_shift_d1,
                    g_shift_d2,
                    g_shift_d3,
                ]
            ),
        ],
        axis=0,
    )
    small_count = small.shape[0]
    small = small.reshape(small_count, lay.devices, rows).transpose(1, 0, 2)
    small = small.reshape(lay.devices, small_count * rows)
    ups_g = jnp.stack([g_upb_enc, g_upb_dec]).reshape(2, 2, groups, rows_ff)
    ups_g = ups_g.transpose(2, 1, 0, 3)[:, None]
    ups_g = lax.dynamic_update_slice(
        jnp.zeros((groups, 4, 2, 2, rows_ff), F32),
        ups_g,
        (jnp.int32(0), part, jnp.int32(0), jnp.int32(0), jnp.int32(0)),
    ).reshape(lay.devices, 2 * rows_ff)
    small = jnp.concatenate([small, ups_g], axis=1)
    small = lax.all_to_all(small, AXES, split_axis=0, concat_axis=0, tiled=True)
    small = jnp.sum(small, axis=0)
    ups_g = small[small_count * rows :]
    small = small[: small_count * rows].reshape(small_count, rows)

    def home(values):
        return lax.ppermute(values.astype(BF16), AXES, lay.back_moves())

    return (
        home(t3)[None],
        home(src_grad).astype(F32)[None],
        home(tgt_grad).astype(F32)[None],
        g_enc_qkv,
        g_enc_out,
        jnp.stack([small[0], small[1], small[6]]),
        g_enc_up,
        ups_g[:rows_ff],
        g_enc_down,
        small[9],
        small[11:13],
        small[16:18],
        g_self_qkv,
        g_self_out,
        jnp.stack([small[2], small[3], small[7]]),
        g_cross_qkv,
        g_cross_out,
        jnp.stack([small[4], small[5], small[8]]),
        g_dec_up,
        ups_g[rows_ff:],
        g_dec_down,
        small[10],
        small[13:16],
        small[18:21],
    )


def solution(mesh):
    groups = mesh.shape["seq"] // 2
    rows = mesh.shape["dp"]
    lay = Layout(groups, rows)
    fine = Mesh(mesh.devices.reshape(groups, 2, 2, 2), AXES)
    seq, dp = ("z", "y"), ("x", "core")

    def run(
        src,
        tgt,
        src_seg,
        tgt_seg,
        enc_qkv,
        enc_out_w,
        enc_attn_bias,
        enc_up,
        enc_up_bias,
        enc_down,
        enc_down_bias,
        enc_gains,
        enc_shifts,
        self_qkv,
        self_out,
        self_bias,
        cross_qkv,
        cross_out,
        cross_bias,
        dec_up,
        dec_up_bias,
        dec_down,
        dec_down_bias,
        dec_gains,
        dec_shifts,
        out_grad,
    ):
        core = lax.axis_index("core")
        part = 2 * lax.axis_index("y") + lax.axis_index("x")
        sub = lax.axis_index("z") % lay.subs
        params = (
            enc_qkv,
            enc_out_w,
            enc_attn_bias,
            enc_up,
            enc_up_bias,
            enc_down,
            enc_down_bias,
            enc_gains,
            enc_shifts,
            self_qkv,
            self_out,
            self_bias,
            cross_qkv,
            cross_out,
            cross_bias,
            dec_up,
            dec_up_bias,
            dec_down,
            dec_down_bias,
            dec_gains,
            dec_shifts,
        )
        return on_device(
            lay, core, part, sub, params, (src[0], tgt[0], src_seg[0], tgt_seg[0], out_grad[0])
        )

    token = P(dp, seq, None)
    ids = P(dp, seq)
    stack = P(None, AXES, None)
    mat = P(AXES, None)
    vecs = P(None, AXES)
    vec = P(AXES)
    in_specs = (
        (token, token, ids, ids)
        + (stack, mat, vecs, mat, vec, mat, vec, vecs, vecs)
        + (stack, mat, vecs, stack, mat, vecs, mat, vec, mat, vec, vecs, vecs)
        + (token,)
    )
    out_specs = (
        (token, token, token)
        + (stack, mat, vecs, mat, vec, mat, vec, vecs, vecs)
        + (stack, mat, vecs, stack, mat, vecs, mat, vec, mat, vec, vecs, vecs)
    )
    return jax.shard_map(run, mesh=fine, in_specs=in_specs, out_specs=out_specs, check_vma=False)
```

```python
import functools

import jax
import jax.numpy as jnp
from jax import lax
from jax.experimental import pallas as pl
from jax.experimental.pallas import tpu as pltpu
from jax.sharding import Mesh
from jax.sharding import PartitionSpec as P

HEADS = 12
HEAD = 64
EPSILON = 1e-05
MASKED = -1e30
BLOCK = 128
F32 = jnp.float32
BF16 = jnp.bfloat16
AXES = ("z", "y", "x", "core")
PLANE = ("y", "x")
NT = (((1,), (1,)), ((), ()))
TN = (((0,), (0,)), ((), ()))


def matmul(left, right):
    return jnp.dot(left, right, preferred_element_type=F32)


def outer_sum(left, right):
    return lax.dot_general(left, right, TN, preferred_element_type=F32)


def back_matmul(left, right):
    return lax.dot_general(left, right, NT, preferred_element_type=F32)


def layer_norm(resid, gain, shift):
    center = resid - jnp.mean(resid, axis=-1, keepdims=True)
    second = jnp.mean(center * center, axis=-1, keepdims=True)
    return center * lax.rsqrt(second + EPSILON) * gain + shift


def positions(subs, index):
    core = lax.axis_index("core")
    part = 2 * lax.axis_index("y") + lax.axis_index("x")
    sub = lax.axis_index("z") & (subs - 1)
    group = lax.shift_right_logical(index, 10)
    half = lax.shift_right_logical(index, 9) & 1
    block = lax.shift_right_logical(index, 7) & 3
    return ((sub ^ group) << 10) + ((core ^ half) << 9) + ((part ^ block) << 7) + (index & 127)


def allowed_mask(form, count_ref, start, width, keys):
    query_kind, key_kind, causal = form
    subs = keys // (8 * BLOCK)
    query = positions(subs, lax.broadcasted_iota(jnp.int32, (1, width), 1) + start)
    key = positions(subs, lax.broadcasted_iota(jnp.int32, (keys, 1), 0))
    one, two = count_ref[0, key_kind], count_ref[1, key_kind]
    first = query >= count_ref[0, query_kind]
    second = query >= count_ref[1, query_kind]
    low = jnp.where(second, two, jnp.where(first, one, 0))
    high = jnp.where(second, keys, jnp.where(first, two, one))
    if causal:
        high = jnp.minimum(high, query + 1)
    return (key >= low) & (key < high)


def joined(refs):
    return jnp.concatenate([ref[...] for ref in refs], axis=0)


def spread(value, out_refs):
    out_refs[0][...] = value[:BLOCK]
    for k in (1, 2, 3):
        out_refs[k][...] = value[k * BLOCK : (k + 1) * BLOCK].astype(BF16)


def spread_shapes(width):
    return [jax.ShapeDtypeStruct((BLOCK, width), F32)] + [
        jax.ShapeDtypeStruct((BLOCK, width), BF16)
    ] * 3


def split_shapes(split, shape, core_axis):
    if not split:
        rows = 1
        for size in shape[:-1]:
            rows *= size
        return [jax.ShapeDtypeStruct((rows, shape[-1]), F32)]
    half = shape[:core_axis] + shape[core_axis + 1 :]
    return [jax.ShapeDtypeStruct(half, F32), jax.ShapeDtypeStruct(half, BF16)]


def put_halves(all_ref, core_axis, out_refs):
    core = lax.axis_index("core")
    lead = (slice(None),) * core_axis
    out_refs[0][...] = all_ref[lead + (core,)]
    out_refs[1][...] = all_ref[lead + (1 - core,)].astype(BF16)


class Chain:
    def __init__(self):
        self.token = jnp.zeros((8, BLOCK), F32)

    def tie(self, *values):
        self.token, *values = lax.optimization_barrier((self.token, *values))
        return values


def call(chain, kernel, name, ins, outs, scratch=(), smem=0, flops=0, trans=0):
    size = sum(x.size * x.dtype.itemsize for x in ins)
    size += sum(x.size * jnp.dtype(x.dtype).itemsize for x in outs)
    count, made = len(ins), len(outs)

    def body(*refs):
        refs[count + 1 + made][...] = refs[count][...]
        kernel(*refs[:count], *refs[count + 1 : count + 1 + made], *refs[count + 2 + made :])

    results = pl.pallas_call(
        body,
        out_shape=(*outs, jax.ShapeDtypeStruct((8, BLOCK), F32)),
        in_specs=[pl.BlockSpec(memory_space=pltpu.SMEM)] * smem + vmem_specs(count - smem + 1),
        out_specs=tuple(vmem_specs(made + 1)),
        scratch_shapes=[pltpu.VMEM(shape, F32) for shape in scratch],
        compiler_params=pltpu.CompilerParams(vmem_limit_bytes=48 << 20),
        cost_estimate=pl.CostEstimate(flops=flops, transcendentals=trans, bytes_accessed=size),
        name=name,
    )(*ins, chain.token)
    chain.token = results[-1]
    return results[:-1]


def vmem_specs(count):
    return [pl.BlockSpec(memory_space=pltpu.VMEM)] * count


def project_kernel(wants, bias_row, count, *refs):
    x_refs, (w_ref, bias_ref), out_refs = refs[:count], refs[count : count + 2], refs[count + 2 :]
    rows = joined(x_refs)
    quarter = bias_ref.shape[1]
    out_refs = list(out_refs)
    if "q" in wants:
        value = matmul(rows, w_ref[:, :quarter]) + bias_ref[bias_row : bias_row + 1]
        out_refs.pop(0)[...] = value.astype(BF16) * BF16(HEAD**-0.5)
    if "k" in wants:
        out_ref = out_refs.pop(0)
        out_ref[:, :quarter] = matmul(rows, w_ref[:, quarter : 2 * quarter]).astype(BF16)
        value = matmul(rows, w_ref[:, 2 * quarter :]) + bias_ref[bias_row + 1 : bias_row + 2]
        out_ref[:, quarter:] = value.astype(BF16)


def project(chain, wants, bias_row, pieces, weight, biases):
    quarter = biases.shape[1]
    rows = BLOCK * len(pieces)
    outs = [jax.ShapeDtypeStruct((rows, quarter), BF16)] if "q" in wants else []
    if "k" in wants:
        outs.append(jax.ShapeDtypeStruct((rows, 2 * quarter), BF16))
    return call(
        chain,
        functools.partial(project_kernel, wants, bias_row, len(pieces)),
        "project_heads",
        [*pieces, weight, biases],
        outs,
        flops=2 * rows * weight.size,
    )


def attn_fwd_kernel(form, width, halves, count_ref, q_ref, wo_ref, *refs):
    kv_refs, (o_ref, lse_ref), out_refs = refs[:halves], refs[halves : halves + 2], refs[halves + 2 : -1]
    ot_ref = refs[-1]
    quarter = q_ref.shape[1]
    keys = sum(ref.shape[0] for ref in kv_refs)
    for chunk in range(q_ref.shape[0] // width):
        rows = slice(chunk * width, (chunk + 1) * width)
        mask = allowed_mask(form, count_ref, chunk * width, width, keys)
        for head in range(quarter // HEAD):
            cols = slice(head * HEAD, (head + 1) * HEAD)
            wide = slice(quarter + head * HEAD, quarter + (head + 1) * HEAD)
            key = jnp.concatenate([ref[:, cols] for ref in kv_refs], axis=0)
            value = jnp.concatenate([ref[:, wide] for ref in kv_refs], axis=0)
            scores = lax.dot_general(key, q_ref[rows, cols], NT, preferred_element_type=F32)
            scores = jnp.where(mask, scores, MASKED)
            peak = jnp.max(scores, axis=0, keepdims=True)
            weights = jnp.exp(scores - peak)
            total = jnp.sum(weights, axis=0, keepdims=True)
            probs = (weights * (1.0 / total)).astype(BF16)
            ot_ref[cols, rows] = lax.dot_general(value, probs, TN, preferred_element_type=F32)
            lse_ref[head : head + 1, rows] = peak + jnp.log(total)
    mixture = ot_ref[...].T.astype(BF16)
    o_ref[...] = mixture
    spread(matmul(mixture, wo_ref[...]), out_refs)


def attn_forward(chain, form, count, queries, kv, out_weight):
    rows, cols = queries.shape
    length = rows * len(kv)
    width = 256 if length <= 1024 else 128
    work = rows * length * cols
    outs = [jax.ShapeDtypeStruct((rows, cols), BF16), jax.ShapeDtypeStruct((8, rows), F32)]
    o, lse, *sent = call(
        chain,
        functools.partial(attn_fwd_kernel, form, width, len(kv)),
        "attn_forward",
        [count, queries, out_weight, *kv],
        outs + spread_shapes(out_weight.shape[1]),
        scratch=[(cols, rows)],
        smem=1,
        flops=8 * work,
        trans=work // HEAD,
    )
    return o, lse, sent


def attn_bwd_kernel(form, width, halves, split, count_ref, q_ref, wo_ref, o_ref, lse_ref, *refs):
    kv_refs, low_refs = refs[:halves], refs[halves : halves + 4]
    refs = refs[halves + 4 :]
    dq_ref, dkv_refs, w_refs = refs[0], refs[1 : 1 + halves], refs[1 + halves : -3]
    dqt_ref, do_ref, all_ref = refs[-3:]
    quarter = q_ref.shape[1]
    half = kv_refs[0].shape[0]
    keys = half * halves
    low = joined(low_refs)
    do_ref[...] = back_matmul(low, wo_ref[...])
    grad_w = outer_sum(o_ref[...], low)
    if split:
        all_ref[...] = grad_w.reshape(all_ref.shape)
        put_halves(all_ref, 1, w_refs)
    else:
        w_refs[0][...] = grad_w
    for chunk in range(q_ref.shape[0] // width):
        rows = slice(chunk * width, (chunk + 1) * width)
        mask = allowed_mask(form, count_ref, chunk * width, width, keys)
        for head in range(quarter // HEAD):
            cols = slice(head * HEAD, (head + 1) * HEAD)
            wide = slice(quarter + head * HEAD, quarter + (head + 1) * HEAD)
            key = jnp.concatenate([ref[:, cols] for ref in kv_refs], axis=0)
            value = jnp.concatenate([ref[:, wide] for ref in kv_refs], axis=0)
            query, grad = q_ref[rows, cols], do_ref[rows, cols].astype(BF16)
            scores = lax.dot_general(key, query, NT, preferred_element_type=F32)
            probs = jnp.where(mask, jnp.exp(scores - lse_ref[head : head + 1, rows]), 0.0)
            grad_probs = lax.dot_general(value, grad, NT, preferred_element_type=F32)
            product = probs * grad_probs
            delta = jnp.sum(product, axis=0, keepdims=True)
            grad_scores = (product - probs * delta).astype(BF16)
            grad_value = matmul(probs.astype(BF16), grad)
            grad_key = matmul(grad_scores, query)
            for j, ref in enumerate(dkv_refs):
                own = slice(j * half, (j + 1) * half)
                if chunk == 0:
                    ref[:, cols] = grad_key[own]
                    ref[:, wide] = grad_value[own]
                else:
                    ref[:, cols] += grad_key[own]
                    ref[:, wide] += grad_value[own]
            dqt_ref[cols, rows] = lax.dot_general(
                key, grad_scores, TN, preferred_element_type=F32
            ) * (HEAD**-0.5)
    dq_ref[...] = dqt_ref[...].T.astype(BF16)


def attn_backward(chain, form, split, count, queries, kv, low, out_weight, o, lse, view):
    rows, cols = queries.shape
    length = rows * len(kv)
    width = 256 if length <= 1024 else 128
    work = rows * length * cols
    halves = len(kv)
    outs = [jax.ShapeDtypeStruct((rows, cols), BF16)]
    outs += [jax.ShapeDtypeStruct((rows, 2 * cols), F32)] * halves
    outs += split_shapes(split, view, 1)
    dq, *rest = call(
        chain,
        functools.partial(attn_bwd_kernel, form, width, halves, split),
        "attn_backward",
        [count, queries, out_weight, o, lse, *kv, *low],
        outs,
        scratch=[(cols, rows), (rows, cols), view if split else (8, BLOCK)],
        smem=1,
        flops=20 * work,
        trans=work // HEAD,
    )
    return dq, rest[:halves], rest[halves:]


def project_back_kernel(cross, split, picks, *refs):
    count = 8 if cross else 4
    x_refs, (w_ref, dq_ref, own_ref, got_ref) = refs[:count], refs[count : count + 4]
    refs = refs[count + 4 :]
    made = len({source for source, _, _ in picks})
    vec_refs, out_refs, refs = refs[:made], refs[made : made + count], refs[made + count :]
    bias_ref, w_refs, all_ref = refs[0], refs[1:-1], refs[-1]
    quarter = dq_ref.shape[1]
    dq = dq_ref[...]
    dkv = (own_ref[...] + got_ref[...]).astype(BF16)
    bias_ref[...] = jnp.zeros_like(bias_ref)
    bias_ref[0:1] = jnp.sum(dq.astype(F32), axis=0, keepdims=True)
    bias_ref[1:2] = jnp.sum(dkv[:, quarter:].astype(F32), axis=0, keepdims=True)
    from_q = back_matmul(dq, w_ref[:, :quarter])
    from_kv = back_matmul(dkv, w_ref[:, quarter:])
    if cross:
        spread(from_q, out_refs[:4])
        spread(from_kv, out_refs[4:])
        rows_q, rows_kv = joined(x_refs[:4]), joined(x_refs[4:])
    else:
        spread(from_q + from_kv, out_refs)
        rows_q = rows_kv = joined(x_refs)
    grads = (
        (slice(0, quarter), outer_sum(rows_q, dq)),
        (slice(quarter, 3 * quarter), outer_sum(rows_kv, dkv)),
    )
    for cols, grad in grads:
        if split:
            all_ref[..., cols] = grad.reshape(all_ref.shape[:-1] + (grad.shape[-1],))
        else:
            w_refs[0][:, cols] = grad
    if split:
        part = 2 * lax.axis_index("y") + lax.axis_index("x")
        lines = [None] * 8
        for source, row, lane in picks:
            lines[lane] = vec_refs[source][row : row + 1]
        blank = jnp.zeros_like(vec_refs[0][0:1])
        lines = jnp.concatenate([blank if line is None else line for line in lines], axis=0)
        extra = slice(3 * quarter, 3 * quarter + 8)
        all_ref[..., 3 * quarter :] = jnp.zeros_like(all_ref[..., 3 * quarter :])
        all_ref[..., extra] = lines.T.reshape(all_ref.shape[:-1] + (8,))
        heads = slice(3 * quarter, 3 * quarter + 2)
        all_ref[part, :, :, :, heads] = bias_ref[...].T[:, :2].reshape(all_ref.shape[1:-1] + (2,))
        put_halves(all_ref, 2, w_refs)


def project_back(chain, cross, split, pieces, weight, dq, own, got, view, vecs, picks):
    rows, quarter = dq.shape
    width = weight.shape[0]
    outs = spread_shapes(width) * (2 if cross else 1)
    outs += [jax.ShapeDtypeStruct((8, quarter), F32)] + split_shapes(split, view, 2)
    results = call(
        chain,
        functools.partial(project_back_kernel, cross, split, picks),
        "project_back",
        [*pieces, weight, dq, own, got, *vecs],
        outs,
        scratch=[view if split else (8, BLOCK)],
        flops=4 * rows * weight.size,
    )
    count = len(pieces)
    return results[:count], results[count], results[count + 1 :]


def norm_kernel(bias_row, gain_row, shift_row, has_sent, base_ref, *refs):
    sent_refs, vec_ref, out_refs = refs[:4], refs[4], refs[5:]
    resid = base_ref[...].astype(F32) + vec_ref[bias_row : bias_row + 1]
    for ref in sent_refs:
        resid = resid + ref[...].astype(F32)
    out_refs[0][...] = resid
    gain, shift = vec_ref[gain_row : gain_row + 1], vec_ref[shift_row : shift_row + 1]
    value = layer_norm(resid, gain, shift)
    out_refs[1][...] = value
    out_refs[2][...] = value.astype(BF16)


def norm(chain, base, sent, vectors, bias_row, gain_row, shift_row):
    shape = base.shape
    return call(
        chain,
        functools.partial(norm_kernel, bias_row, gain_row, shift_row, True),
        "layer_norm",
        [base, *sent, vectors],
        [
            jax.ShapeDtypeStruct(shape, F32),
            jax.ShapeDtypeStruct(shape, F32),
            jax.ShapeDtypeStruct(shape, BF16),
        ],
    )


def norm_back_kernel(gain_row, count, *refs):
    grad_refs, (resid_ref, vec_ref), out_refs = refs[:count], refs[count : count + 2], refs[count + 2 :]
    grad = grad_refs[0][...].astype(F32)
    for ref in grad_refs[1:]:
        grad = grad + ref[...].astype(F32)
    resid = resid_ref[...]
    center = resid - jnp.mean(resid, axis=-1, keepdims=True)
    scale = lax.rsqrt(jnp.mean(center * center, axis=-1, keepdims=True) + EPSILON)
    unit = center * scale
    weighted = grad * vec_ref[gain_row : gain_row + 1]
    both = grad * unit
    first = jnp.mean(weighted, axis=-1, keepdims=True)
    second = jnp.mean(weighted * unit, axis=-1, keepdims=True)
    value = (weighted - first - unit * second) * scale
    low = value.astype(BF16)
    out_refs[0][...] = value
    out_refs[1][...] = low
    out_refs[2][...] = jnp.zeros_like(out_refs[2])
    for row, terms in enumerate((both, grad, low.astype(F32))):
        out_refs[2][row : row + 1] = jnp.sum(terms, axis=0, keepdims=True)


def norm_back(chain, grads, resid, vectors, gain_row):
    shape = resid.shape
    return call(
        chain,
        functools.partial(norm_back_kernel, gain_row, len(grads)),
        "layer_norm_back",
        [*grads, resid, vectors],
        [
            jax.ShapeDtypeStruct(shape, F32),
            jax.ShapeDtypeStruct(shape, BF16),
            jax.ShapeDtypeStruct((8, shape[1]), F32),
        ],
    )


def total_kernel(*refs):
    total = refs[0][...].astype(F32)
    for ref in refs[1:-1]:
        total = total + ref[...].astype(F32)
    refs[-1][...] = total.astype(BF16)


def rounded_total(chain, parts):
    (out,) = call(
        chain, total_kernel, "sum_parts", list(parts), [jax.ShapeDtypeStruct(parts[0].shape, BF16)]
    )
    return out


def normal_cdf(values):
    return 0.5 + 0.5 * lax.erf(values * (0.5**0.5))


def ffn_fwd_kernel(layer, y0, y1, y2, y3, up_ref, bias_ref, down_ref, *out_refs):
    rows = joined((y0, y1, y2, y3))
    hidden = up_ref.shape[1]
    total = None
    for cols in (slice(0, hidden // 2), slice(hidden // 2, hidden)):
        pre = matmul(rows, up_ref[:, cols]) + bias_ref[layer : layer + 1, cols]
        act = (pre * normal_cdf(pre)).astype(BF16)
        part = matmul(act, down_ref[cols])
        total = part if total is None else total + part
    spread(total, out_refs)


def ffn_forward(chain, layer, pieces, up, biases, down):
    return call(
        chain,
        functools.partial(ffn_fwd_kernel, layer),
        "ffn_forward",
        [*pieces, up, biases, down],
        spread_shapes(down.shape[1]),
        flops=16 * BLOCK * up.size,
        trans=4 * BLOCK * up.shape[1],
    )


def ffn_bwd_kernel(layer, split, *refs):
    rows, low = joined(refs[:4]), joined(refs[4:8])
    up_ref, bias_ref, down_ref = refs[8:11]
    out_refs = refs[11:15]
    up_all, down_all, bias_all = refs[-3:]
    if split:
        bias_refs, up_refs, down_refs = refs[15:17], refs[17:19], refs[19:21]
        bias_all[...] = jnp.zeros_like(bias_all)
    else:
        bias_refs, up_refs, down_refs = refs[15:16], refs[16:17], refs[17:18]
    hidden = up_ref.shape[1]
    total = None
    for c, cols in enumerate((slice(0, hidden // 2), slice(hidden // 2, hidden))):
        pre = matmul(rows, up_ref[:, cols]) + bias_ref[layer : layer + 1, cols]
        cdf = normal_cdf(pre)
        act = (pre * cdf).astype(BF16)
        slope = cdf + pre * (jnp.exp(-0.5 * pre * pre) * (2.0 * jnp.pi) ** -0.5)
        grad = (back_matmul(low, down_ref[cols]) * slope).astype(BF16)
        grad_bias = jnp.sum(grad.astype(F32), axis=0, keepdims=True)
        grad_down, grad_up = outer_sum(act, low), outer_sum(rows, grad)
        if split:
            down_all[c] = grad_down.reshape(down_all.shape[1:])
            up_all[..., cols] = grad_up.reshape(up_all.shape[:-1] + (hidden // 2,))
            size = down_all.shape[2]
            for z in range(4):
                bias_all[c, z, 0:1, :size] = grad_bias[:, z * size : (z + 1) * size]
        else:
            bias_refs[0][:, cols] = grad_bias
            down_refs[0][cols] = grad_down
            up_refs[0][:, cols] = grad_up
        part = back_matmul(grad, up_ref[:, cols])
        total = part if total is None else total + part
    spread(total, out_refs)
    if split:
        put_halves(up_all, 2, up_refs)
        put_halves(down_all, 0, down_refs)
        put_halves(bias_all, 0, bias_refs)


def ffn_backward(chain, layer, split, pieces, low, up, biases, down, up_view, down_view):
    hidden = up.shape[1]
    bias_view = (2, 4, 8, BLOCK) if split else (1, hidden)
    outs = spread_shapes(down.shape[1]) + split_shapes(split, bias_view, 0)
    outs += split_shapes(split, up_view, 2) + split_shapes(split, down_view, 0)
    tiny = (8, BLOCK)
    results = call(
        chain,
        functools.partial(ffn_bwd_kernel, layer, split),
        "ffn_backward",
        [*pieces, *low, up, biases, down],
        outs,
        scratch=[up_view, down_view, bias_view] if split else [tiny] * 3,
        flops=48 * BLOCK * up.size,
        trans=8 * BLOCK * hidden,
    )
    per = 2 if split else 1
    rest = results[4:]
    return results[:4], rest[:per], rest[per : 2 * per], rest[2 * per :]


def combine_kernel(count, *refs):
    out_ref = refs[-1]
    row = 0
    for keep_ref, got_ref in zip(refs[:count], refs[count:-1], strict=True):
        total = (keep_ref[...] + got_ref[...].astype(F32)).astype(BF16)
        _, size, cols = total.shape
        out_ref[:, row : row + size, :cols] = total
        if cols < out_ref.shape[2]:
            rest = jnp.zeros((total.shape[0], size, out_ref.shape[2] - cols), BF16)
            out_ref[:, row : row + size, cols:] = rest
        row += size


def combine(chain, keeps, gots, width):
    keeps = [x.reshape(x.shape[0], -1, x.shape[-1]) for x in keeps]
    gots = [x.reshape(x.shape[0], -1, x.shape[-1]) for x in gots]
    shape = (4, sum(x.shape[1] for x in keeps), width)
    (out,) = call(
        chain,
        functools.partial(combine_kernel, len(keeps)),
        "combine_gradients",
        [*keeps, *gots],
        [jax.ShapeDtypeStruct(shape, BF16)],
    )
    return out


def shares_kernel(keep_ref, got_ref, keep_out, got_out, *out_refs):
    group = lax.axis_index("z")
    cols, wide = keep_ref.shape[-1], out_refs[0].shape[-1]
    for k, ref in enumerate(out_refs):
        z = group ^ k
        ref[:4, :, :cols] = (keep_ref[z] + got_ref[z].astype(F32)).astype(ref.dtype)
        ref[:4, :, cols:] = jnp.zeros((4, ref.shape[1], wide - cols), ref.dtype)
        ref[4] = (keep_out[z] + got_out[z].astype(F32)).astype(ref.dtype)


def shares(chain, heads, out, width):
    shape = (5, heads[0].shape[2], width)
    return call(
        chain,
        shares_kernel,
        "group_shares",
        [*heads, *out],
        [jax.ShapeDtypeStruct(shape, F32)] + [jax.ShapeDtypeStruct(shape, BF16)] * 3,
    )


def join_heads(part_ref, col, out_ref):
    quarter = out_ref.shape[-1] // 4
    for j in range(3):
        for p in range(4):
            value = part_ref[p, :, col + j * quarter : col + (j + 1) * quarter]
            out_ref[j, :, p * quarter : (p + 1) * quarter] = value.astype(F32)


def join_up(part_ref, col, out_ref):
    size = out_ref.shape[1] // 32
    for z in range(4):
        for p in range(4):
            for c in range(2):
                start = ((z * 4 + p) * 2 + c) * size
                first = col + (c * 4 + z) * size
                out_ref[:, start : start + size] = part_ref[p, :, first : first + size].astype(F32)


def join_lines(part_ref, col, out_ref):
    total = part_ref[0, :, col : col + BLOCK].astype(F32)
    for p in (1, 2, 3):
        total = total + part_ref[p, :, col : col + BLOCK].astype(F32)
    out_ref[...] = total.T[:8]


def join_layer_kernel(heads_out, part_ref, up_ref, heads_ref, line_ref):
    hidden = part_ref.shape[-1] - heads_out - BLOCK
    join_up(part_ref, 0, up_ref)
    join_heads(part_ref, hidden, heads_ref)
    join_lines(part_ref, hidden + heads_out, line_ref)


def join_layer(chain, parts, heads_out):
    _, rows, _ = parts.shape
    return call(
        chain,
        functools.partial(join_layer_kernel, heads_out),
        "join_gradients",
        [parts],
        [
            jax.ShapeDtypeStruct((rows, 128 * rows), F32),
            jax.ShapeDtypeStruct((3, rows, 32 * rows), F32),
            jax.ShapeDtypeStruct((8, rows), F32),
        ],
    )


def join_last_kernel(heads_out, part_ref, cross_ref, self_ref, heads_ref, *refs):
    line_ref = refs[-1]
    join_heads(part_ref, 0, heads_ref)
    join_lines(part_ref, heads_out, line_ref)
    lines = {"e": line_ref, "s": self_ref, "c": cross_ref}
    for ref, picks in zip(refs[:-1], LINES, strict=True):
        for row, (name, line) in enumerate(picks):
            ref[row : row + 1] = lines[name][line : line + 1]


LINES = (
    (("e", 0), ("e", 1), ("e", 2)),
    (("s", 3),),
    (("e", 4), ("s", 6)),
    (("e", 5), ("s", 7)),
    (("s", 0), ("s", 1), ("s", 2)),
    (("c", 0), ("c", 1), ("c", 2)),
    (("c", 3),),
    (("s", 4), ("c", 6), ("c", 4)),
    (("s", 5), ("c", 7), ("c", 5)),
)


def join_last(chain, parts, cross_lines, self_lines, heads_out):
    _, rows, _ = parts.shape
    return call(
        chain,
        functools.partial(join_last_kernel, heads_out),
        "join_gradients",
        [parts, cross_lines, self_lines],
        [jax.ShapeDtypeStruct((3, rows, 32 * rows), F32)]
        + [jax.ShapeDtypeStruct((len(picks), rows), F32) for picks in LINES],
        scratch=[(8, rows)],
    )


def place_kernel(plan, turned, mine_ref, other_ref, *out_refs):
    group, core = lax.axis_index("z"), lax.axis_index("core")
    for piece_ref, c in ((mine_ref, core), (other_ref, 1 - core)):
        for k in range(4):
            z = group ^ k if turned else k
            for (kind, row, col), out_ref in zip(plan, out_refs, strict=True):
                count, cols = out_ref.shape[-2:]
                for p in range(4 if kind == "rows" else 1):
                    first = row + p * count
                    value = piece_ref[k, first : first + count, col : col + cols]
                    if kind == "rows":
                        out_ref[z, p, c] = value
                    elif kind == "down":
                        out_ref[c, z] = value
                    else:
                        out_ref[z, c] = value


def place(chain, plan, shapes, turned, mine, other):
    lead = {"rows": (4, 4, 2), "down": (2, 4), "out": (4, 2)}
    outs = call(
        chain,
        functools.partial(place_kernel, plan, turned),
        "place_weights",
        [mine, other],
        [
            jax.ShapeDtypeStruct(lead[entry[0]] + shape, mine.dtype)
            for entry, shape in zip(plan, shapes, strict=True)
        ],
    )
    return [out.reshape(-1, out.shape[-1]) for out in outs]


def place_first_kernel(
    cols, count, mine_ref, other_ref, w_ref, out_w_ref, vec_ref, up_ref, part_ref, all_ref
):
    group, core = lax.axis_index("z"), lax.axis_index("core")
    part = 2 * lax.axis_index("y") + lax.axis_index("x")
    for piece_ref, c in ((mine_ref, core), (other_ref, 1 - core)):
        for k in range(4):
            for p in range(4):
                w_ref[group ^ k, p, c] = piece_ref[k, p, :, :cols]
                all_ref[group ^ k, p, c] = piece_ref[k, p, :, cols:].astype(F32)
            out_w_ref[group ^ k, c] = piece_ref[k, 4]
    rows = all_ref.shape[3]
    rows_ff = 4 * rows
    for z in range(4):
        for p in range(4):
            for c in range(2):
                start = ((z * 4 + p) * 2 + c) * rows
                vec_ref[:, start : start + rows] = all_ref[z, p, c, :, :rows]
    for c in range(2):
        for z in range(4):
            start = (c * 4 + z) * rows_ff
            up_ref[:, start : start + rows_ff] = all_ref[z, part, c, count : count + 2, :rows_ff]
    for p in range(4):
        for c in range(2):
            start = (p * 2 + c) * rows
            part_ref[:, start : start + rows] = all_ref[part, p, c, :, :rows]


def place_first(chain, mine, other, cols, count):
    _, _, rows, wide = mine.shape
    width = 32 * rows
    return call(
        chain,
        functools.partial(place_first_kernel, cols, count),
        "place_first_weights",
        [mine, other],
        [
            jax.ShapeDtypeStruct((4, 4, 2, rows, cols), mine.dtype),
            jax.ShapeDtypeStruct((4, 2, rows, wide), mine.dtype),
            jax.ShapeDtypeStruct((rows, width), F32),
            jax.ShapeDtypeStruct((2, 32 * rows), F32),
            jax.ShapeDtypeStruct((rows, 8 * rows), F32),
        ],
        scratch=[(4, 4, 2, rows, wide - cols)],
    )


def plane_swap(values, shift):
    return lax.ppermute(values, PLANE, [(i, i ^ shift) for i in range(4)])


def z_swap(values, shift):
    groups = lax.axis_size("z")
    return lax.ppermute(values, "z", [(z, z ^ shift) for z in range(groups)])


def core_swap(values):
    return lax.ppermute(values, "core", [(0, 1), (1, 0)])


def plane_gather(values):
    return [values] + [plane_swap(values, k) for k in (1, 2, 3)]


def tie(*values):
    return lax.optimization_barrier(values)


def plane_send(spreads):
    return [spreads[0]] + [plane_swap(spreads[k], k) for k in (1, 2, 3)]


def plane_total(sent):
    total = sent[0]
    for part in sent[1:]:
        total = total + part.astype(F32)
    return total


class Layout:
    def __init__(self, groups, rows):
        self.groups = groups
        self.devices = groups * 8
        self.subs = groups // rows

    def index(self, z, y, x, c):
        return ((z * 2 + y) * 2 + x) * 2 + c

    def token_moves(self):
        moves = []
        for z in range(self.groups):
            for y in range(2):
                for x in range(2):
                    for c in range(2):
                        row, block = 2 * x + c, 2 * z + y
                        group, within = row * self.subs + block // 8, block % 8
                        core, part = within // 4, within % 4
                        moves.append(
                            (self.index(z, y, x, c), self.index(group, part // 2, part % 2, core))
                        )
        return moves

    def back_moves(self):
        return [(b, a) for a, b in self.token_moves()]

    def turn_moves(self):
        moves = []
        for part in range(4):
            for z in range(self.groups):
                owner, user = part * self.groups + z, z * 4 + part
                moves.append((owner, user))
        return moves


def on_device(lay, core, part, sub, params, tokens):
    (
        enc_qkv,
        enc_out_w,
        enc_attn_bias,
        enc_up,
        enc_up_bias,
        enc_down,
        enc_down_bias,
        enc_gains,
        enc_shifts,
        self_qkv,
        self_out,
        self_bias,
        cross_qkv,
        cross_out,
        cross_bias,
        dec_up,
        dec_up_bias,
        dec_down,
        dec_down_bias,
        dec_gains,
        dec_shifts,
    ) = params
    src, tgt, src_seg, tgt_seg, out_grad = tokens
    groups = lay.groups
    width = src.shape[1]
    rows = enc_out_w.shape[0]
    rows_ff = enc_down.shape[0]
    quarter = width // 4
    hidden = rows_ff * groups * 2
    heads_out = enc_qkv.shape[0] * quarter

    chain = Chain()
    split = groups == 4
    ids = jnp.concatenate([src_seg, tgt_seg]).astype(BF16)
    ids = jnp.pad(ids[None], ((0, 7), (0, width - 2 * BLOCK)))
    packed = lax.ppermute(jnp.concatenate([src, ids], axis=0), AXES, lay.token_moves())

    def heads_split(qkv):
        parts = qkv.reshape(3, rows, 4, quarter)
        return parts.transpose(2, 1, 0, 3).reshape(4, rows, heads_out)

    def up_split(up):
        parts = up.reshape(rows, groups, 4, 2, rows_ff)
        return parts.transpose(2, 0, 3, 1, 4).reshape(4, rows, hidden)

    def both_cores(mine, axis):
        other = core_swap(mine)
        shape = [1] * (mine.ndim + 1)
        shape[axis] = 2
        which = lax.broadcasted_iota(jnp.int32, shape, axis) == core
        return jnp.where(which, jnp.expand_dims(mine, axis), jnp.expand_dims(other, axis))

    def whole(kind, piece):
        cols = piece.shape[-1]
        piece = lax.all_gather(piece, "z", axis=0)
        return both_cores(piece, {"rows": 2, "down": 0, "out": 1}[kind]).reshape(-1, cols)

    def plane_turn(values):
        return lax.all_to_all(values, PLANE, split_axis=0, concat_axis=0, tiled=True)

    def out_turn(values):
        return lax.ppermute(values, ("z", "y", "x"), lay.turn_moves())

    vectors = jnp.concatenate(
        [
            enc_attn_bias,
            self_bias,
            cross_bias,
            enc_down_bias[None],
            dec_down_bias[None],
            enc_gains,
            dec_gains,
            enc_shifts,
            dec_shifts,
        ],
        axis=0,
    )
    vector_count = vectors.shape[0]
    if split:
        wide = width - heads_out
        extra = jnp.concatenate(
            [
                jnp.pad(vectors, ((0, 0), (0, wide - rows))),
                jnp.pad(jnp.stack([enc_up_bias, dec_up_bias]), ((0, 1), (0, wide - rows_ff))),
            ],
            axis=0,
        )
        extra = jnp.broadcast_to(extra[None], (4, rows, wide))
        pieces = plane_turn(
            jnp.concatenate(
                [
                    heads_split(enc_qkv),
                    extra,
                    heads_split(self_qkv),
                    heads_split(cross_qkv),
                    up_split(enc_up),
                    up_split(dec_up),
                ],
                axis=2,
            )
        )
        outs = out_turn(jnp.concatenate([enc_out_w, self_out, cross_out], axis=0))
        pieces, packed = tie(pieces, packed)
        first = jnp.concatenate([pieces[:, :, :width], outs[None, :rows]], axis=0)
        first = jnp.stack([first] + [z_swap(first, k) for k in (1, 2, 3)])
        rest = pieces[:, :, width:].reshape(4 * rows, -1)
        narrow = ((0, 0), (0, width - heads_out))
        w_self = jnp.pad(rest[:, :heads_out], narrow)
        w_cross = jnp.pad(rest[:, heads_out : 2 * heads_out], narrow)
        up = rest[:, 2 * heads_out : 2 * heads_out + hidden]
        one = jnp.concatenate([up, enc_down, outs[rows:], w_self], axis=0)
        one = lax.all_gather(one, "z", axis=0)
        up = rest[:, 2 * heads_out + hidden :]
        two = jnp.concatenate([up, dec_down, w_cross], axis=0)
        two = lax.all_gather(two, "z", axis=0)
        ffn_plan = [("rows", 0, 0), ("down", 4 * rows, 0)]
        ffn_shapes = [(rows, hidden), (rows_ff, width)]
        row = 4 * rows + rows_ff

    src = packed[:BLOCK]
    blocks = [packed] + [plane_swap(packed, k) for k in (1, 2, 3)]
    src_rows = [block[:BLOCK] for block in blocks]
    doc = jnp.concatenate([block[BLOCK : BLOCK + 1] for block in blocks], axis=0)
    doc = doc[:, : 2 * BLOCK].astype(F32).reshape(4, 2, BLOCK)
    count = jnp.stack(
        [
            jnp.sum((doc < 0.5).astype(F32), axis=(0, 2)),
            jnp.sum((doc < 1.5).astype(F32), axis=(0, 2)),
        ]
    )
    count = jnp.pad(count, ((0, 6), (0, BLOCK - 2)))
    count = count + core_swap(count)
    total = count
    for j in range(1, lay.subs):
        total = total + z_swap(count, j)
    count = total.astype(jnp.int32)

    if split:
        w_enc, wo_enc, vectors, ups, mine = place_first(
            chain, first, core_swap(first), heads_out, vector_count
        )
        w_enc, wo_enc = w_enc.reshape(width, heads_out), wo_enc.reshape(quarter, width)
    else:
        w_enc = whole("rows", plane_turn(heads_split(enc_qkv)))
        vectors = jnp.concatenate([vectors.reshape(-1), enc_up_bias, dec_up_bias])[None]
        vectors = lax.all_gather(vectors, AXES, axis=0, tiled=True).astype(F32)
        ups = vectors[:, vector_count * rows :].reshape(groups, 4, 2, 2, rows_ff)
        ups = lax.dynamic_index_in_dim(ups, part, axis=1, keepdims=False)
        ups = ups.transpose(2, 1, 0, 3).reshape(2, hidden)
        vectors = vectors[:, : vector_count * rows].reshape(lay.devices, vector_count, rows)
        vectors = vectors.transpose(1, 0, 2).reshape(vector_count, width)
        mine = lax.dynamic_slice_in_dim(vectors, part * quarter, quarter, axis=1)
        w_self = whole("rows", plane_turn(heads_split(self_qkv)))
        outs = out_turn(jnp.concatenate([enc_out_w, self_out, cross_out], axis=1))
        outs = whole("out", outs)
        wo_enc, wo_self, wo_cross = (outs[:, k * width : (k + 1) * width] for k in range(3))
        w_up_enc = whole("rows", plane_turn(up_split(enc_up)))
        w_down_enc = whole("down", enc_down)
        w_cross = whole("rows", plane_turn(heads_split(cross_qkv)))
        w_up_dec = whole("rows", plane_turn(up_split(dec_up)))
        w_down_dec = whole("down", dec_down)

    row_view = (4, 4, 2, rows)

    def with_others(kv):
        kv = [kv, core_swap(kv)]
        return kv + [z_swap(half, j) for j in range(1, lay.subs) for half in kv]

    def own_part(halves):
        own, other = halves[:2]
        for j in range(1, lay.subs):
            own = own + z_swap(halves[2 * j], j)
            other = other + z_swap(halves[2 * j + 1], j)
        return own, core_swap(other)

    enc_form, self_form, cross_form = (0, 0, False), (1, 1, True), (1, 0, False)
    q_enc, kv_enc = project(chain, "qk", 0, src_rows, w_enc, mine)
    kv_enc = with_others(kv_enc)
    kv_enc, tgt = tie(kv_enc, tgt)
    tgt = lax.ppermute(tgt, AXES, lay.token_moves())
    o_enc, lse_enc, sent = attn_forward(chain, enc_form, count, q_enc, kv_enc, wo_enc)
    sent = plane_send(sent)
    sent, tgt = tie(sent, tgt)
    r_enc1, e1, e1_low = norm(chain, src, sent, vectors, 2, 11, 16)
    e1_rows = plane_gather(e1_low)
    if split:
        e1_rows, one = tie(e1_rows, one)
        w_up_enc, w_down_enc, wo_self, wo_cross, w_self = place(
            chain,
            ffn_plan + [("out", row, 0), ("out", row + rows, 0), ("rows", row + 2 * rows, 0)],
            ffn_shapes + [(rows, width)] * 2 + [(rows, heads_out)],
            False,
            one,
            core_swap(one),
        )
    e1_rows, tgt = tie(e1_rows, tgt)
    tgt_rows = plane_gather(tgt)
    sent = plane_send(ffn_forward(chain, 0, e1_rows, w_up_enc, ups, w_down_enc))
    q_self, kv_self = project(chain, "qk", 3, tgt_rows, w_self, mine)
    kv_self = with_others(kv_self)
    o_self, lse_self, self_sent = attn_forward(chain, self_form, count, q_self, kv_self, wo_self)
    r_enc2, encoded, encoded_low = norm(chain, e1, sent, vectors, 9, 12, 17)
    self_sent = plane_send(self_sent)
    encoded_rows = plane_gather(encoded_low)
    r_dec1, t1, t1_low = norm(chain, tgt, self_sent, vectors, 5, 13, 18)
    t1_rows = plane_gather(t1_low)
    if split:
        encoded_rows, two = tie(encoded_rows, two)
        w_up_dec, w_down_dec, w_cross = place(
            chain,
            ffn_plan + [("rows", row, 0)],
            ffn_shapes + [(rows, heads_out)],
            False,
            two,
            core_swap(two),
        )
    (kv_cross,) = project(chain, "k", 6, encoded_rows, w_cross, mine)
    kv_cross = with_others(kv_cross)
    (q_cross,) = project(chain, "q", 6, t1_rows, w_cross, mine)
    q_cross, out_grad = tie(q_cross, out_grad)
    out_grad = lax.ppermute(out_grad, AXES, lay.token_moves())
    o_cross, lse_cross, sent = attn_forward(chain, cross_form, count, q_cross, kv_cross, wo_cross)
    r_dec2, t2, t2_low = norm(chain, t1, plane_send(sent), vectors, 8, 14, 19)
    t2_rows = plane_gather(t2_low)
    sent = plane_send(ffn_forward(chain, 1, t2_rows, w_up_dec, ups, w_down_dec))
    sent, out_grad = tie(sent, out_grad)
    r_dec3, _, t3_low = norm(chain, t2, sent, vectors, 10, 15, 20)

    heads_view = row_view + (heads_out + BLOCK,)
    up_view = row_view + (hidden,)
    down_view = (2, 4, rows_ff, width)
    out_view = (4, 2, rows, width)
    if not split:
        heads_view, up_view = (width, heads_out), (width, hidden)
        down_view, out_view = (hidden, width), (quarter, width)

    def core_send(grad, kind):
        if split:
            return grad[0], core_swap(grad[1])
        axis = {"rows": 2, "down": 0, "out": 1}[kind]
        shape = {
            "rows": (groups, 4, 2, rows, -1),
            "down": (2, groups, rows_ff, width),
            "out": (groups, 2, rows, width),
        }[kind]
        grad = grad[0].reshape(shape)
        zero = lax.index_in_dim(grad, 0, axis, keepdims=False)
        one = lax.index_in_dim(grad, 1, axis, keepdims=False)
        send = jnp.where(core == 0, one, zero).astype(BF16)
        return jnp.where(core == 0, zero, one), core_swap(send)

    def stacked(*sends):
        keeps, gots = [x[0] for x in sends], [x[1] for x in sends]
        if split:
            return combine(chain, keeps, gots, width)
        sums = []
        for keep, got in zip(keeps, gots, strict=True):
            total = (keep + got.astype(F32)).astype(BF16)
            total = total.reshape(groups, -1, total.shape[-1])
            sums.append(jnp.pad(total, ((0, 0), (0, 0), (0, width - total.shape[-1]))))
        return jnp.concatenate(sums, axis=1)

    def z_reduce(grad):
        return lax.psum_scatter(grad, "z", scatter_dimension=0, tiled=False)

    def ffn_sends(bias, up, down):
        sends = [core_send(up, "rows"), core_send(down, "down")]
        if split:
            sends.append(core_send(bias, "bias"))
        return sends

    d_r3, low3, sums3 = norm_back(chain, [out_grad], r_dec3, vectors, 15)
    spreads, *grads = ffn_backward(
        chain, 1, split, t2_rows, plane_gather(low3), w_up_dec, ups, w_down_dec, up_view, down_view
    )
    upb_dec = grads[0]
    sent = plane_send(spreads)
    sends = ffn_sends(*grads)
    sent, sends = tie(sent, sends)
    d_r2, low2, sums2 = norm_back(chain, [d_r3, *sent], r_dec2, vectors, 14)

    low2_rows = plane_gather(low2)
    dec_ffn = z_reduce(stacked(*sends))
    dq, dkv, g_wo_cross = attn_backward(
        chain,
        cross_form,
        split,
        count,
        q_cross,
        kv_cross,
        low2_rows,
        wo_cross,
        o_cross,
        lse_cross,
        out_view,
    )
    spreads, g_bias_cross, g_cross = project_back(
        chain,
        True,
        split,
        t1_rows + encoded_rows,
        w_cross,
        dq,
        *own_part(dkv),
        heads_view,
        [sums2, sums3],
        ((0, 2, 2), (1, 2, 3), (1, 0, 4), (1, 1, 5), (0, 0, 6), (0, 1, 7)),
    )
    sent = plane_send(spreads[4:])
    sends = [core_send(g_cross, "rows"), core_send(g_wo_cross, "out")]
    sent, sends = tie(sent, sends)

    d_e2, low_e2, sums_e2 = norm_back(chain, sent, r_enc2, vectors, 12)
    low_e2_rows = plane_gather(low_e2)
    d_t1_sent = plane_send(spreads[:4])
    cross = z_reduce(stacked(*sends))
    spreads, *grads = ffn_backward(
        chain, 0, split, e1_rows, low_e2_rows, w_up_enc, ups, w_down_enc, up_view, down_view
    )
    upb_enc = grads[0]
    sent = plane_send(spreads)
    d_r1, low1, sums1 = norm_back(chain, [d_r2, *d_t1_sent], r_dec1, vectors, 13)
    sends = ffn_sends(*grads)
    sent, sends = tie(sent, sends)
    low1_rows = plane_gather(low1)
    d_r1e, low_e1, sums_e1 = norm_back(chain, [d_e2, *sent], r_enc1, vectors, 11)

    low_e1_rows = plane_gather(low_e1)
    enc_ffn = z_reduce(stacked(*sends))
    dq_self, dkv_self, g_wo_self = attn_backward(
        chain,
        self_form,
        split,
        count,
        q_self,
        kv_self,
        low1_rows,
        wo_self,
        o_self,
        lse_self,
        out_view,
    )
    dq_enc, dkv_enc, g_wo_enc = attn_backward(
        chain,
        enc_form,
        split,
        count,
        q_enc,
        kv_enc,
        low_e1_rows,
        wo_enc,
        o_enc,
        lse_enc,
        out_view,
    )
    spreads_self, g_bias_self, g_self = project_back(
        chain,
        False,
        split,
        tgt_rows,
        w_self,
        dq_self,
        *own_part(dkv_self),
        heads_view,
        [sums1, sums_e2],
        ((0, 2, 2), (1, 2, 3), (0, 0, 4), (0, 1, 5), (1, 0, 6), (1, 1, 7)),
    )
    spreads, g_bias_enc, g_enc = project_back(
        chain,
        False,
        split,
        src_rows,
        w_enc,
        dq_enc,
        *own_part(dkv_enc),
        heads_view,
        [sums_e1],
        ((0, 2, 2), (0, 0, 4), (0, 1, 5)),
    )
    g_enc, g_wo_enc = core_send(g_enc, "rows"), core_send(g_wo_enc, "out")
    sent = plane_send(spreads)
    self_sent = plane_send(spreads_self)
    self_sends = [core_send(g_self, "rows"), core_send(g_wo_self, "out")]

    if split:
        parts = shares(chain, g_enc, g_wo_enc, width)
        parts = [parts[0]] + [z_swap(parts[k], k) for k in (1, 2, 3)]
        own_self = z_reduce(stacked(*self_sends))
        src_low = rounded_total(chain, [d_r1e, *sent])
        tgt_low = rounded_total(chain, [d_r1, *self_sent])
        dec_parts = jnp.concatenate(
            [
                dec_ffn[: 4 * rows].reshape(4, rows, hidden),
                cross[: 4 * rows, : heads_out + BLOCK].reshape(4, rows, heads_out + BLOCK),
            ],
            axis=2,
        )
        g_dec_up, g_cross_qkv, cross_lines = join_layer(chain, plane_turn(dec_parts), heads_out)
        enc_parts = jnp.concatenate(
            [
                enc_ffn[: 4 * rows].reshape(4, rows, hidden),
                own_self[: 4 * rows, : heads_out + BLOCK].reshape(4, rows, heads_out + BLOCK),
            ],
            axis=2,
        )
        last = rounded_total(chain, parts)
        g_enc_up, g_self_qkv, self_lines = join_layer(chain, plane_turn(enc_parts), heads_out)
        outs = jnp.concatenate([last[4], own_self[4 * rows :], cross[4 * rows :]], axis=0)
        outs = lax.ppermute(outs, ("z", "y", "x"), [(b, a) for a, b in lay.turn_moves()])
        outs = outs.astype(F32)
        g_enc_qkv, *small = join_last(
            chain, plane_turn(last[:4]), cross_lines, self_lines, heads_out
        )
        small = [x[0] if x.shape[0] == 1 else x for x in small]
        tail = 4 * rows + rows_ff
        g_upb_enc, g_upb_dec = (x[tail, :rows_ff].astype(F32) for x in (enc_ffn, dec_ffn))
        g_enc_down, g_dec_down = (x[4 * rows : tail].astype(F32) for x in (enc_ffn, dec_ffn))
    else:

        def heads_join(parts):
            parts = plane_turn(parts[:, :heads_out].reshape(4, rows, heads_out))
            parts = parts.reshape(4, rows, 3, quarter).transpose(2, 1, 0, 3)
            return parts.reshape(3, rows, width).astype(F32)

        def up_join(parts):
            parts = plane_turn(parts.reshape(4, rows, hidden))
            parts = parts.reshape(4, rows, 2, groups, rows_ff).transpose(1, 3, 0, 2, 4)
            return parts.reshape(rows, -1).astype(F32)

        src_low = plane_total([d_r1e + sent[0], *sent[1:]]).astype(BF16)
        tgt_low = plane_total([d_r1 + self_sent[0], *self_sent[1:]]).astype(BF16)
        own_self = z_reduce(stacked(*self_sends))
        last = z_reduce(stacked(g_enc, g_wo_enc))
        g_dec_up, g_enc_up = up_join(dec_ffn[: 4 * rows]), up_join(enc_ffn[: 4 * rows])
        g_enc_down, g_dec_down = (x[4 * rows :].astype(F32) for x in (enc_ffn, dec_ffn))
        g_cross_qkv, g_self_qkv, g_enc_qkv = (
            heads_join(x[: 4 * rows]) for x in (cross, own_self, last)
        )
        outs = jnp.concatenate([x[4 * rows :] for x in (last, own_self, cross)], axis=0)
        outs = lax.ppermute(outs, ("z", "y", "x"), [(b, a) for a, b in lay.turn_moves()])
        outs = outs.astype(F32)
        placed = jnp.concatenate([g_bias_enc[:2], g_bias_self[:2], g_bias_cross[:2]], axis=0)
        placed = lax.dynamic_update_slice(
            jnp.zeros((6, width), F32), placed, (jnp.int32(0), part * quarter)
        )
        lines = jnp.concatenate(
            [placed, sums_e1[:3], sums_e2[:3], sums1[:3], sums2[:3], sums3[:3]], axis=0
        )
        line_count = lines.shape[0]
        lines = lines.reshape(line_count, lay.devices, rows).transpose(1, 0, 2)
        lines = lines.reshape(lay.devices, line_count * rows)
        upb = jnp.concatenate([upb_enc[0], upb_dec[0]]).reshape(2, 2, groups, rows_ff)
        upb = lax.dynamic_update_slice(
            jnp.zeros((groups, 4, 2, 2, rows_ff), F32),
            upb.transpose(2, 1, 0, 3)[:, None],
            (jnp.int32(0), part, jnp.int32(0), jnp.int32(0), jnp.int32(0)),
        )
        lines = jnp.concatenate([lines, upb.reshape(lay.devices, 2 * rows_ff)], axis=1)
        lines = lax.all_to_all(lines, AXES, split_axis=0, concat_axis=0, tiled=True)
        lines = jnp.sum(lines, axis=0)
        upb = lines[line_count * rows :]
        g_upb_enc, g_upb_dec = upb[:rows_ff], upb[rows_ff:]
        lines = lines[: line_count * rows].reshape(line_count, rows)
        small = [
            jnp.stack([lines[0], lines[1], lines[8]]),
            lines[11],
            jnp.stack([lines[6], lines[9]]),
            jnp.stack([lines[7], lines[10]]),
            jnp.stack([lines[2], lines[3], lines[14]]),
            jnp.stack([lines[4], lines[5], lines[17]]),
            lines[20],
            jnp.stack([lines[12], lines[15], lines[18]]),
            jnp.stack([lines[13], lines[16], lines[19]]),
        ]
    g_enc_out, g_self_out, g_cross_out = outs[:rows], outs[rows : 2 * rows], outs[2 * rows :]

    def home(values):
        return lax.ppermute(values, AXES, lay.back_moves())

    bias_enc, down_enc, gains_enc, shifts_enc = small[:4]
    bias_self, bias_cross, down_dec, gains_dec, shifts_dec = small[4:]
    return (
        home(t3_low)[None],
        home(src_low).astype(F32)[None],
        home(tgt_low).astype(F32)[None],
        g_enc_qkv,
        g_enc_out,
        bias_enc,
        g_enc_up,
        g_upb_enc,
        g_enc_down,
        down_enc,
        gains_enc,
        shifts_enc,
        g_self_qkv,
        g_self_out,
        bias_self,
        g_cross_qkv,
        g_cross_out,
        bias_cross,
        g_dec_up,
        g_upb_dec,
        g_dec_down,
        down_dec,
        gains_dec,
        shifts_dec,
    )


def solution(mesh):
    groups = mesh.shape["seq"] // 2
    rows = mesh.shape["dp"]
    lay = Layout(groups, rows)
    fine = Mesh(mesh.devices.reshape(groups, 2, 2, 2), AXES)
    seq, dp = ("z", "y"), ("x", "core")

    def run(
        src,
        tgt,
        src_seg,
        tgt_seg,
        enc_qkv,
        enc_out_w,
        enc_attn_bias,
        enc_up,
        enc_up_bias,
        enc_down,
        enc_down_bias,
        enc_gains,
        enc_shifts,
        self_qkv,
        self_out,
        self_bias,
        cross_qkv,
        cross_out,
        cross_bias,
        dec_up,
        dec_up_bias,
        dec_down,
        dec_down_bias,
        dec_gains,
        dec_shifts,
        out_grad,
    ):
        core = lax.axis_index("core")
        part = 2 * lax.axis_index("y") + lax.axis_index("x")
        sub = lax.axis_index("z") % lay.subs
        params = (
            enc_qkv,
            enc_out_w,
            enc_attn_bias,
            enc_up,
            enc_up_bias,
            enc_down,
            enc_down_bias,
            enc_gains,
            enc_shifts,
            self_qkv,
            self_out,
            self_bias,
            cross_qkv,
            cross_out,
            cross_bias,
            dec_up,
            dec_up_bias,
            dec_down,
            dec_down_bias,
            dec_gains,
            dec_shifts,
        )
        return on_device(
            lay, core, part, sub, params, (src[0], tgt[0], src_seg[0], tgt_seg[0], out_grad[0])
        )

    token = P(dp, seq, None)
    ids = P(dp, seq)
    stack = P(None, AXES, None)
    mat = P(AXES, None)
    vecs = P(None, AXES)
    vec = P(AXES)
    in_specs = (
        (token, token, ids, ids)
        + (stack, mat, vecs, mat, vec, mat, vec, vecs, vecs)
        + (stack, mat, vecs, stack, mat, vecs, mat, vec, mat, vec, vecs, vecs)
        + (token,)
    )
    out_specs = (
        (token, token, token)
        + (stack, mat, vecs, mat, vec, mat, vec, vecs, vecs)
        + (stack, mat, vecs, stack, mat, vecs, mat, vec, mat, vec, vecs, vecs)
    )
    return jax.shard_map(run, mesh=fine, in_specs=in_specs, out_specs=out_specs, check_vma=False)
```

```python
import functools

import jax
import jax.numpy as jnp
from jax import lax
from jax.experimental import pallas as pl
from jax.experimental.pallas import tpu as pltpu
from jax.sharding import Mesh
from jax.sharding import PartitionSpec as P

HEADS = 12
HEAD = 64
EPSILON = 1e-05
MASKED = -1e30
BLOCK = 128
F32 = jnp.float32
BF16 = jnp.bfloat16
AXES = ("z", "y", "x", "core")
PLANE = ("y", "x")
NT = (((1,), (1,)), ((), ()))
TN = (((0,), (0,)), ((), ()))


def matmul(left, right):
    return jnp.dot(left, right, preferred_element_type=F32)


def outer_sum(left, right):
    return lax.dot_general(left, right, TN, preferred_element_type=F32)


def back_matmul(left, right):
    return lax.dot_general(left, right, NT, preferred_element_type=F32)


def layer_norm(resid, gain, shift):
    center = resid - jnp.mean(resid, axis=-1, keepdims=True)
    second = jnp.mean(center * center, axis=-1, keepdims=True)
    return center * lax.rsqrt(second + EPSILON) * gain + shift


def positions(subs, index):
    core = lax.axis_index("core")
    part = 2 * lax.axis_index("x") + lax.axis_index("y")
    sub = lax.axis_index("z") & (subs - 1)
    group = lax.shift_right_logical(index, 10)
    half = lax.shift_right_logical(index, 9) & 1
    block = lax.shift_right_logical(index, 7) & 3
    block = ((block & 1) << 1) | lax.shift_right_logical(block, 1)
    return ((sub ^ group) << 10) + ((core ^ half) << 9) + ((part ^ block) << 7) + (index & 127)


def allowed_mask(form, count_ref, start, width, keys):
    query_kind, key_kind, causal = form
    subs = keys // (8 * BLOCK)
    query = positions(subs, lax.broadcasted_iota(jnp.int32, (1, width), 1) + start)
    key = positions(subs, lax.broadcasted_iota(jnp.int32, (keys, 1), 0))
    one, two = count_ref[0, key_kind], count_ref[1, key_kind]
    first = query >= count_ref[0, query_kind]
    second = query >= count_ref[1, query_kind]
    low = jnp.where(second, two, jnp.where(first, one, 0))
    high = jnp.where(second, keys, jnp.where(first, two, one))
    if causal:
        high = jnp.minimum(high, query + 1)
    return (key >= low) & (key < high)


def joined(refs, start=0):
    return jnp.concatenate([ref[start : start + BLOCK] for ref in refs], axis=0)


def spread(value, out_refs, start=0):
    out_refs[0][...] = value[:BLOCK]
    for k in (1, 2, 3):
        block = value[k * BLOCK : (k + 1) * BLOCK]
        out_refs[k][start : start + BLOCK] = block.astype(BF16)


def spread_shapes(width, blocks=1):
    return [jax.ShapeDtypeStruct((BLOCK, width), F32)] + [
        jax.ShapeDtypeStruct((blocks * BLOCK, width), BF16)
    ] * 3


def split_shapes(split, shape, core_axis):
    if not split:
        rows = 1
        for size in shape[:-1]:
            rows *= size
        return [jax.ShapeDtypeStruct((rows, shape[-1]), F32)]
    half = shape[:core_axis] + shape[core_axis + 1 :]
    return [jax.ShapeDtypeStruct(half, F32), jax.ShapeDtypeStruct(half, BF16)]


def put_halves(all_ref, core_axis, out_refs):
    core = lax.axis_index("core")
    lead = (slice(None),) * core_axis
    out_refs[0][...] = all_ref[lead + (core,)]
    out_refs[1][...] = all_ref[lead + (1 - core,)].astype(BF16)


class Chain:
    def __init__(self):
        self.token = jnp.zeros((8, BLOCK), F32)

    def tie(self, *values):
        self.token, *values = lax.optimization_barrier((self.token, *values))
        return values


def call(chain, kernel, name, ins, outs, scratch=(), smem=0, flops=0, trans=0):
    size = sum(x.size * x.dtype.itemsize for x in ins)
    size += sum(x.size * jnp.dtype(x.dtype).itemsize for x in outs)
    count, made = len(ins), len(outs)

    def body(*refs):
        refs[count + 1 + made][...] = refs[count][...]
        kernel(*refs[:count], *refs[count + 1 : count + 1 + made], *refs[count + 2 + made :])

    results = pl.pallas_call(
        body,
        out_shape=(*outs, jax.ShapeDtypeStruct((8, BLOCK), F32)),
        in_specs=[pl.BlockSpec(memory_space=pltpu.SMEM)] * smem + vmem_specs(count - smem + 1),
        out_specs=tuple(vmem_specs(made + 1)),
        scratch_shapes=[pltpu.VMEM(shape, F32) for shape in scratch],
        compiler_params=pltpu.CompilerParams(vmem_limit_bytes=24 << 20),
        cost_estimate=pl.CostEstimate(flops=flops, transcendentals=trans, bytes_accessed=size),
        name=name,
    )(*ins, chain.token)
    chain.token = results[-1]
    return results[:-1]


def vmem_specs(count):
    return [pl.BlockSpec(memory_space=pltpu.VMEM)] * count


def project_kernel(bias_row, q_start, x0, x1, x2, x3, w_ref, bias_ref, q_ref, kv_ref, rows_ref):
    pieces = (x0, x1, x2, x3)
    quarter = bias_ref.shape[1]
    rows = joined(pieces, q_start)
    if q_start:
        rows_ref[4 * BLOCK :] = rows
    value = matmul(rows, w_ref[:, :quarter]) + bias_ref[bias_row : bias_row + 1]
    q_ref[...] = value.astype(BF16) * BF16(HEAD**-0.5)
    rows = joined(pieces)
    rows_ref[: 4 * BLOCK] = rows
    kv_ref[:, :quarter] = matmul(rows, w_ref[:, quarter : 2 * quarter]).astype(BF16)
    value = matmul(rows, w_ref[:, 2 * quarter :]) + bias_ref[bias_row + 1 : bias_row + 2]
    kv_ref[:, quarter:] = value.astype(BF16)


def project(chain, bias_row, pieces, weight, biases, q_start=0):
    quarter = biases.shape[1]
    rows = 4 * BLOCK
    return call(
        chain,
        functools.partial(project_kernel, bias_row, q_start),
        "project_heads",
        [*pieces, weight, biases],
        [
            jax.ShapeDtypeStruct((rows, quarter), BF16),
            jax.ShapeDtypeStruct((rows, 2 * quarter), BF16),
            jax.ShapeDtypeStruct((rows * (2 if q_start else 1), weight.shape[0]), BF16),
        ],
        flops=2 * rows * weight.size,
    )


def attn_fwd_kernel(form, width, halves, count_ref, q_ref, wo_ref, *refs):
    kv_refs, (kept_ref, lse_ref), out_refs = refs[:halves], refs[halves : halves + 2], refs[halves + 2 : -1]
    ot_ref = refs[-1]
    quarter = q_ref.shape[1]
    kept_ref[:, :quarter] = q_ref[...]
    for j, ref in enumerate(kv_refs):
        kept_ref[:, (2 + 2 * j) * quarter : (4 + 2 * j) * quarter] = ref[...]
    keys = sum(ref.shape[0] for ref in kv_refs)
    for chunk in range(q_ref.shape[0] // width):
        rows = slice(chunk * width, (chunk + 1) * width)
        mask = allowed_mask(form, count_ref, chunk * width, width, keys)
        for head in range(quarter // HEAD):
            cols = slice(head * HEAD, (head + 1) * HEAD)
            wide = slice(quarter + head * HEAD, quarter + (head + 1) * HEAD)
            key = jnp.concatenate([ref[:, cols] for ref in kv_refs], axis=0)
            value = jnp.concatenate([ref[:, wide] for ref in kv_refs], axis=0)
            scores = lax.dot_general(key, q_ref[rows, cols], NT, preferred_element_type=F32)
            scores = jnp.where(mask, scores, MASKED)
            peak = jnp.max(scores, axis=0, keepdims=True)
            weights = jnp.exp(scores - peak)
            total = jnp.sum(weights, axis=0, keepdims=True)
            probs = (weights * (1.0 / total)).astype(BF16)
            ot_ref[cols, rows] = lax.dot_general(value, probs, TN, preferred_element_type=F32)
            lse_ref[head : head + 1, rows] = peak + jnp.log(total)
    mixture = ot_ref[...].T.astype(BF16)
    kept_ref[:, quarter : 2 * quarter] = mixture
    spread(matmul(mixture, wo_ref[...]), out_refs)


def attn_forward(chain, form, count, queries, kv, out_weight):
    rows, cols = queries.shape
    length = rows * len(kv)
    width = 256 if length <= 1024 else 128
    work = rows * length * cols
    outs = [
        jax.ShapeDtypeStruct((rows, cols * (2 + 2 * len(kv))), BF16),
        jax.ShapeDtypeStruct((8, rows), F32),
    ]
    kept, lse, *rest = call(
        chain,
        functools.partial(attn_fwd_kernel, form, width, len(kv)),
        "attn_forward",
        [count, queries, out_weight, *kv],
        outs + spread_shapes(out_weight.shape[1]),
        scratch=[(cols, rows)],
        smem=1,
        flops=8 * work,
        trans=work // HEAD,
    )
    return (kept, out_weight, lse), rest


def attn_bwd_kernel(form, width, halves, split, start, count_ref, kept_ref, wo_ref, lse_ref, *refs):
    low_refs, refs = refs[:4], refs[4:]
    quarter = wo_ref.shape[0]

    def kept(first):
        starts = [(2 + 2 * j) * quarter + first for j in range(halves)]
        return jnp.concatenate([kept_ref[:, at : at + HEAD] for at in starts], axis=0)

    dq_ref, dkv_refs, w_refs = refs[0], refs[1 : 1 + halves], refs[1 + halves : -3]
    dqt_ref, do_ref, all_ref = refs[-3:]
    half = kept_ref.shape[0]
    keys = half * halves
    low = joined(low_refs, start)
    do_ref[...] = back_matmul(low, wo_ref[...])
    grad_w = outer_sum(kept_ref[:, quarter : 2 * quarter], low)
    if split:
        all_ref[...] = grad_w.reshape(all_ref.shape)
        put_halves(all_ref, 1, w_refs)
    else:
        w_refs[0][...] = grad_w
    for chunk in range(half // width):
        rows = slice(chunk * width, (chunk + 1) * width)
        mask = allowed_mask(form, count_ref, chunk * width, width, keys)
        for head in range(quarter // HEAD):
            cols = slice(head * HEAD, (head + 1) * HEAD)
            wide = slice(quarter + head * HEAD, quarter + (head + 1) * HEAD)
            key, value = kept(head * HEAD), kept(quarter + head * HEAD)
            query, grad = kept_ref[rows, cols], do_ref[rows, cols].astype(BF16)
            scores = lax.dot_general(key, query, NT, preferred_element_type=F32)
            probs = jnp.where(mask, jnp.exp(scores - lse_ref[head : head + 1, rows]), 0.0)
            grad_probs = lax.dot_general(value, grad, NT, preferred_element_type=F32)
            product = probs * grad_probs
            delta = jnp.sum(product, axis=0, keepdims=True)
            grad_scores = (product - probs * delta).astype(BF16)
            grad_value = matmul(probs.astype(BF16), grad)
            grad_key = matmul(grad_scores, query)
            for j, ref in enumerate(dkv_refs):
                own = slice(j * half, (j + 1) * half)
                if chunk == 0:
                    ref[:, cols] = grad_key[own]
                    ref[:, wide] = grad_value[own]
                else:
                    ref[:, cols] += grad_key[own]
                    ref[:, wide] += grad_value[own]
            dqt_ref[cols, rows] = lax.dot_general(
                key, grad_scores, TN, preferred_element_type=F32
            ) * (HEAD**-0.5)
    dq_ref[...] = dqt_ref[...].T.astype(BF16)


def attn_backward(chain, form, split, count, saved, low, view, start=0):
    kept, out_weight, lse = saved
    rows, cols = kept.shape[0], out_weight.shape[0]
    halves = kept.shape[1] // (2 * cols) - 1
    length = rows * halves
    width = 256 if length <= 1024 else 128
    work = rows * length * cols
    outs = [jax.ShapeDtypeStruct((rows, cols), BF16)]
    outs += [jax.ShapeDtypeStruct((rows, 2 * cols), F32)] * halves
    outs += split_shapes(split, view, 1)
    dq, *rest = call(
        chain,
        functools.partial(attn_bwd_kernel, form, width, halves, split, start),
        "attn_backward",
        [count, kept, out_weight, lse, *low],
        outs,
        scratch=[(cols, rows), (rows, cols), view if split else (8, BLOCK)],
        smem=1,
        flops=20 * work,
        trans=work // HEAD,
    )
    return dq, rest[:halves], rest[halves:]


def project_back_kernel(cross, joins, split, picks, *refs):
    rows_ref, w_ref, dq_ref, own_ref, got_ref = refs[:5]
    refs = refs[5:]
    made = len({source for source, _, _ in picks})
    vec_refs, refs = refs[:made], refs[made:]
    mate_refs, refs = (refs[:3], refs[3:]) if joins else ((), refs)
    own_q_ref, refs = (refs[0], refs[1:]) if cross else (None, refs)
    out_refs, refs = refs[:4], refs[4:]
    bias_ref, w_refs, all_ref = refs[0], refs[1:-1], refs[-1]
    quarter = dq_ref.shape[1]
    dq = dq_ref[...]
    dkv = (own_ref[...] + got_ref[...]).astype(BF16)
    bias_ref[...] = jnp.zeros_like(bias_ref)
    bias_ref[0:1] = jnp.sum(dq.astype(F32), axis=0, keepdims=True)
    bias_ref[1:2] = jnp.sum(dkv[:, quarter:].astype(F32), axis=0, keepdims=True)
    from_q = back_matmul(dq, w_ref[:, :quarter])
    from_kv = back_matmul(dkv, w_ref[:, quarter:])
    if cross:
        spread(from_kv, out_refs)
        spread(from_q, (own_q_ref, *out_refs[1:]), BLOCK)
    else:
        spread(from_q + from_kv, out_refs)
    for ref, out_ref in zip(mate_refs, out_refs[1:], strict=False):
        out_ref[BLOCK:] = ref[...]
    rows_q = rows_kv = rows_ref[: 4 * BLOCK]
    if cross:
        rows_q = rows_ref[4 * BLOCK :]
    grads = (
        (slice(0, quarter), outer_sum(rows_q, dq)),
        (slice(quarter, 3 * quarter), outer_sum(rows_kv, dkv)),
    )
    for cols, grad in grads:
        if split:
            all_ref[..., cols] = grad.reshape(all_ref.shape[:-1] + (grad.shape[-1],))
        else:
            w_refs[0][:, cols] = grad
    if split:
        part = 2 * lax.axis_index("y") + lax.axis_index("x")
        lines = [None] * 8
        for source, row, lane in picks:
            lines[lane] = vec_refs[source][row : row + 1]
        blank = jnp.zeros_like(vec_refs[0][0:1])
        lines = jnp.concatenate([blank if line is None else line for line in lines], axis=0)
        extra = slice(3 * quarter, 3 * quarter + 8)
        all_ref[..., 3 * quarter :] = jnp.zeros_like(all_ref[..., 3 * quarter :])
        all_ref[..., extra] = lines.T.reshape(all_ref.shape[:-1] + (8,))
        heads = slice(3 * quarter, 3 * quarter + 2)
        all_ref[part, :, :, :, heads] = bias_ref[...].T[:, :2].reshape(all_ref.shape[1:-1] + (2,))
        put_halves(all_ref, 2, w_refs)


def project_back(
    chain, split, kept_rows, weight, dq, own, got, view, vecs, picks, mates=()
):
    rows, quarter = dq.shape
    width = weight.shape[0]
    cross = kept_rows.shape[0] > rows
    outs = [jax.ShapeDtypeStruct((BLOCK, width), F32)] if cross else []
    outs += spread_shapes(width, 2 if cross or mates else 1)
    count = len(outs)
    outs += [jax.ShapeDtypeStruct((8, quarter), F32)] + split_shapes(split, view, 2)
    results = call(
        chain,
        functools.partial(project_back_kernel, cross, bool(mates), split, picks),
        "project_back",
        [kept_rows, weight, dq, own, got, *vecs, *mates],
        outs,
        scratch=[view if split else (8, BLOCK)],
        flops=4 * rows * weight.size,
    )
    return results[:count], results[count], results[count + 1 :]


def norm_kernel(bias_row, line, before, start, base_ref, *refs):
    sent_refs, vec_ref, mate_refs, (resid_ref, low_ref) = refs[:4], refs[4], refs[5:-2], refs[-2:]

    def normed(resid, gain_row, shift_row):
        return layer_norm(
            resid, vec_ref[gain_row : gain_row + 1], vec_ref[shift_row : shift_row + 1]
        )

    base = base_ref[...].astype(F32)
    if before is not None:
        base = normed(base, *before)
    resid = base + vec_ref[bias_row : bias_row + 1] + sent_refs[0][...]
    for ref in sent_refs[1:]:
        resid = resid + ref[start : start + BLOCK].astype(F32)
    resid_ref[...] = resid
    at = BLOCK if mate_refs else 0
    for ref in mate_refs:
        low_ref[:BLOCK] = ref[...]
    low_ref[at:] = normed(resid, *line).astype(BF16)


def norm(chain, base, sent, vectors, bias_row, line, before=None, start=0, mate=()):
    rows, width = base.shape
    return call(
        chain,
        functools.partial(norm_kernel, bias_row, line, before, start),
        "layer_norm",
        [base, *sent, vectors, *mate],
        [
            jax.ShapeDtypeStruct((rows, width), F32),
            jax.ShapeDtypeStruct((rows * (1 + len(mate)), width), BF16),
        ],
    )


def norm_back_kernel(gain_row, count, start, *refs):
    grad_refs, (resid_ref, vec_ref), refs = refs[:count], refs[count : count + 2], refs[count + 2 :]
    mate_refs, out_refs = refs[:-3], refs[-3:]
    grad = None
    for ref in grad_refs:
        first = start if ref.shape[0] > BLOCK else 0
        part = ref[first : first + BLOCK].astype(F32)
        grad = part if grad is None else grad + part
    resid = resid_ref[...]
    center = resid - jnp.mean(resid, axis=-1, keepdims=True)
    scale = lax.rsqrt(jnp.mean(center * center, axis=-1, keepdims=True) + EPSILON)
    unit = center * scale
    weighted = grad * vec_ref[gain_row : gain_row + 1]
    both = grad * unit
    first = jnp.mean(weighted, axis=-1, keepdims=True)
    second = jnp.mean(weighted * unit, axis=-1, keepdims=True)
    value = (weighted - first - unit * second) * scale
    low = value.astype(BF16)
    out_refs[0][...] = value
    for ref in mate_refs:
        out_refs[1][:BLOCK] = ref[...]
    out_refs[1][BLOCK if mate_refs else 0 :] = low
    out_refs[2][...] = jnp.zeros_like(out_refs[2])
    for row, terms in enumerate((both, grad, low.astype(F32))):
        out_refs[2][row : row + 1] = jnp.sum(terms, axis=0, keepdims=True)


def norm_back(chain, grads, resid, vectors, gain_row, start=0, mate=()):
    rows, width = resid.shape
    return call(
        chain,
        functools.partial(norm_back_kernel, gain_row, len(grads), start),
        "layer_norm_back",
        [*grads, resid, vectors, *mate],
        [
            jax.ShapeDtypeStruct((rows, width), F32),
            jax.ShapeDtypeStruct((rows * (1 + len(mate)), width), BF16),
            jax.ShapeDtypeStruct((8, width), F32),
        ],
    )


def both_totals_kernel(*refs):
    for at, base_ref, own_ref in ((0, refs[0], refs[1]), (BLOCK, refs[2], refs[3])):
        total = base_ref[...] + own_ref[...]
        for ref in refs[4:7]:
            total = total + ref[at : at + BLOCK].astype(F32)
        refs[8][at : at + BLOCK] = total.astype(BF16)
    refs[8][2 * BLOCK :] = refs[7][...]


def both_totals(chain, parts):
    shape = (3 * BLOCK, parts[0].shape[1])
    (out,) = call(
        chain, both_totals_kernel, "sum_both", list(parts), [jax.ShapeDtypeStruct(shape, BF16)]
    )
    return out


def total_kernel(*refs):
    total = refs[0][...].astype(F32)
    for ref in refs[1:-1]:
        total = total + ref[...].astype(F32)
    refs[-1][...] = total.astype(BF16)


def rounded_total(chain, parts):
    outs = [jax.ShapeDtypeStruct(parts[0].shape, BF16)]
    (out,) = call(chain, total_kernel, "sum_parts", list(parts), outs)
    return out


def normal_cdf(values):
    return 0.5 + 0.5 * lax.erf(values * (0.5**0.5))


def ffn_fwd_kernel(layer, y0, y1, y2, y3, up_ref, bias_ref, down_ref, *refs):
    mate_refs, rows_ref, out_refs = refs[:-5], refs[-5], refs[-4:]
    rows = joined((y0, y1, y2, y3))
    rows_ref[...] = rows
    hidden = up_ref.shape[1]
    total = None
    for cols in (slice(0, hidden // 2), slice(hidden // 2, hidden)):
        pre = matmul(rows, up_ref[:, cols]) + bias_ref[layer : layer + 1, cols]
        act = (pre * normal_cdf(pre)).astype(BF16)
        part = matmul(act, down_ref[cols])
        total = part if total is None else total + part
    spread(total, out_refs)
    for ref, out_ref in zip(mate_refs, out_refs[1:], strict=False):
        out_ref[BLOCK:] = ref[...]


def ffn_forward(chain, layer, pieces, up, biases, down, mates=()):
    rows, *spreads = call(
        chain,
        functools.partial(ffn_fwd_kernel, layer),
        "ffn_forward",
        [*pieces, up, biases, down, *mates],
        [jax.ShapeDtypeStruct((4 * BLOCK, up.shape[0]), BF16)]
        + spread_shapes(down.shape[1], 2 if mates else 1),
        flops=16 * BLOCK * up.size,
        trans=4 * BLOCK * up.shape[1],
    )
    return rows, spreads


def ffn_bwd_kernel(layer, split, *refs):
    rows, low = refs[0][...], joined(refs[1:5])
    up_ref, bias_ref, down_ref = refs[5:8]
    out_refs, refs = refs[8:12], refs[12:]
    up_all, down_all, bias_all = refs[-3:]
    if split:
        bias_refs, up_refs, down_refs = refs[:2], refs[2:4], refs[4:6]
        bias_all[...] = jnp.zeros_like(bias_all)
    else:
        bias_refs, up_refs, down_refs = refs[:1], refs[1:2], refs[2:3]
    hidden = up_ref.shape[1]
    total = None
    for c, cols in enumerate((slice(0, hidden // 2), slice(hidden // 2, hidden))):
        pre = matmul(rows, up_ref[:, cols]) + bias_ref[layer : layer + 1, cols]
        cdf = normal_cdf(pre)
        act = (pre * cdf).astype(BF16)
        slope = cdf + pre * (jnp.exp(-0.5 * pre * pre) * (2.0 * jnp.pi) ** -0.5)
        grad = (back_matmul(low, down_ref[cols]) * slope).astype(BF16)
        grad_bias = jnp.sum(grad.astype(F32), axis=0, keepdims=True)
        grad_down, grad_up = outer_sum(act, low), outer_sum(rows, grad)
        if split:
            down_all[c] = grad_down.reshape(down_all.shape[1:])
            up_all[..., cols] = grad_up.reshape(up_all.shape[:-1] + (hidden // 2,))
            size = down_all.shape[2]
            for z in range(4):
                bias_all[c, z, 0:1, :size] = grad_bias[:, z * size : (z + 1) * size]
        else:
            bias_refs[0][:, cols] = grad_bias
            down_refs[0][cols] = grad_down
            up_refs[0][:, cols] = grad_up
        part = back_matmul(grad, up_ref[:, cols])
        total = part if total is None else total + part
    spread(total, out_refs)
    if split:
        put_halves(up_all, 2, up_refs)
        put_halves(down_all, 0, down_refs)
        put_halves(bias_all, 0, bias_refs)


def ffn_backward(chain, layer, split, rows, low, up, biases, down, up_view, down_view):
    hidden = up.shape[1]
    bias_view = (2, 4, 8, BLOCK) if split else (1, hidden)
    outs = spread_shapes(down.shape[1]) + split_shapes(split, bias_view, 0)
    outs += split_shapes(split, up_view, 2) + split_shapes(split, down_view, 0)
    tiny = (8, BLOCK)
    results = call(
        chain,
        functools.partial(ffn_bwd_kernel, layer, split),
        "ffn_backward",
        [rows, *low, up, biases, down],
        outs,
        scratch=[up_view, down_view, bias_view] if split else [tiny] * 3,
        flops=48 * BLOCK * up.size,
        trans=8 * BLOCK * hidden,
    )
    per = 2 if split else 1
    rest = results[4:]
    return results[:4], rest[:per], rest[per : 2 * per], rest[2 * per :]


def combine_kernel(count, *refs):
    out_ref = refs[-1]
    row = 0
    for keep_ref, got_ref in zip(refs[:count], refs[count:-1], strict=True):
        total = (keep_ref[...] + got_ref[...].astype(F32)).astype(BF16)
        _, size, cols = total.shape
        out_ref[:, row : row + size, :cols] = total
        if cols < out_ref.shape[2]:
            rest = jnp.zeros((total.shape[0], size, out_ref.shape[2] - cols), BF16)
            out_ref[:, row : row + size, cols:] = rest
        row += size


def combine(chain, keeps, gots, width):
    keeps = [x.reshape(x.shape[0], -1, x.shape[-1]) for x in keeps]
    gots = [x.reshape(x.shape[0], -1, x.shape[-1]) for x in gots]
    shape = (4, sum(x.shape[1] for x in keeps), width)
    (out,) = call(
        chain,
        functools.partial(combine_kernel, len(keeps)),
        "combine_gradients",
        [*keeps, *gots],
        [jax.ShapeDtypeStruct(shape, BF16)],
    )
    return out


def shares_kernel(keep_ref, got_ref, keep_out, got_out, *out_refs):
    group = lax.axis_index("z")
    cols, wide = keep_ref.shape[-1], out_refs[0].shape[-1]
    targets = (out_refs[0], out_refs[1], out_refs[2].at[0], out_refs[2].at[1])
    for ref, shift in zip(targets, (0, 2, 1, 3), strict=True):
        z = group ^ shift
        ref[:4, :, :cols] = (keep_ref[z] + got_ref[z].astype(F32)).astype(ref.dtype)
        ref[:4, :, cols:] = jnp.zeros((4, ref.shape[1], wide - cols), ref.dtype)
        ref[4] = (keep_out[z] + got_out[z].astype(F32)).astype(ref.dtype)


def shares(chain, heads, out, width):
    shape = (5, heads[0].shape[2], width)
    return call(
        chain,
        shares_kernel,
        "group_shares",
        [*heads, *out],
        [jax.ShapeDtypeStruct(shape, F32)] * 2 + [jax.ShapeDtypeStruct((2, *shape), BF16)],
    )


def join_heads(part_ref, col, out_ref):
    quarter = out_ref.shape[-1] // 4
    for j in range(3):
        for p in range(4):
            value = part_ref[p, :, col + j * quarter : col + (j + 1) * quarter]
            out_ref[j, :, p * quarter : (p + 1) * quarter] = value.astype(F32)


def join_up(part_ref, col, out_ref):
    size = out_ref.shape[1] // 32
    for z in range(4):
        for p in range(4):
            for c in range(2):
                start = ((z * 4 + p) * 2 + c) * size
                first = col + (c * 4 + z) * size
                out_ref[:, start : start + size] = part_ref[p, :, first : first + size].astype(F32)


def join_lines(part_ref, col, out_ref):
    total = part_ref[0, :, col : col + BLOCK].astype(F32)
    for p in (1, 2, 3):
        total = total + part_ref[p, :, col : col + BLOCK].astype(F32)
    out_ref[...] = total.T[:8]


def join_last_kernel(heads_out, part_ref, *refs):
    enc_up_ref, self_ref, enc_ref, dec_up_ref, cross_ref = refs[:5]
    lines = dict(zip("sec", refs[-3:], strict=True))
    hidden = enc_up_ref.shape[1] // 4
    wide = part_ref.shape[-1] - 2 * (hidden + heads_out + BLOCK)
    join_up(part_ref, 0, enc_up_ref)
    join_heads(part_ref, hidden, self_ref)
    join_lines(part_ref, hidden + heads_out, lines["s"])
    start = hidden + heads_out + BLOCK
    join_heads(part_ref, start, enc_ref)
    join_lines(part_ref, start + heads_out, lines["e"])
    start += wide
    join_up(part_ref, start, dec_up_ref)
    join_heads(part_ref, start + hidden, cross_ref)
    join_lines(part_ref, start + hidden + heads_out, lines["c"])
    for ref, picks in zip(refs[5:-3], LINES, strict=True):
        for row, (name, line) in enumerate(picks):
            ref[row : row + 1] = lines[name][line : line + 1]


LINES = (
    (("e", 0), ("e", 1), ("e", 2)),
    (("s", 3),),
    (("e", 4), ("s", 6)),
    (("e", 5), ("s", 7)),
    (("s", 0), ("s", 1), ("s", 2)),
    (("c", 0), ("c", 1), ("c", 2)),
    (("c", 3),),
    (("s", 4), ("c", 6), ("c", 4)),
    (("s", 5), ("c", 7), ("c", 5)),
)


def join_last(chain, parts, heads_out):
    _, rows, _ = parts.shape
    heads = jax.ShapeDtypeStruct((3, rows, 32 * rows), F32)
    up = jax.ShapeDtypeStruct((rows, 128 * rows), F32)
    results = call(
        chain,
        functools.partial(join_last_kernel, heads_out),
        "join_gradients",
        [parts],
        [up, heads, heads, up, heads]
        + [jax.ShapeDtypeStruct((len(picks), rows), F32) for picks in LINES],
        scratch=[(8, rows)] * 3,
    )
    return results[:5], results[5:]


def place_kernel(plan, turned, mine_ref, other_ref, *out_refs):
    group, core = lax.axis_index("z"), lax.axis_index("core")
    for piece_ref, c in ((mine_ref, core), (other_ref, 1 - core)):
        for k in range(4):
            z = group ^ k if turned else k
            for (kind, row, col), out_ref in zip(plan, out_refs, strict=True):
                count, cols = out_ref.shape[-2:]
                for p in range(4 if kind == "rows" else 1):
                    first = row + p * count
                    value = piece_ref[k, first : first + count, col : col + cols]
                    if kind == "rows":
                        out_ref[z, p, c] = value
                    elif kind == "down":
                        out_ref[c, z] = value
                    else:
                        out_ref[z, c] = value


def place(chain, plan, shapes, turned, mine, other):
    lead = {"rows": (4, 4, 2), "down": (2, 4), "out": (4, 2)}
    outs = call(
        chain,
        functools.partial(place_kernel, plan, turned),
        "place_weights",
        [mine, other],
        [
            jax.ShapeDtypeStruct(lead[entry[0]] + shape, mine.dtype)
            for entry, shape in zip(plan, shapes, strict=True)
        ],
    )
    outs = [out.reshape(-1, out.shape[-1]) for out in outs]
    return outs


def place_first_kernel(
    cols, count, mine_ref, other_ref, w_ref, out_w_ref, vec_ref, up_ref, part_ref, all_ref
):
    group, core = lax.axis_index("z"), lax.axis_index("core")
    part = 2 * lax.axis_index("y") + lax.axis_index("x")
    for piece_ref, c in ((mine_ref, core), (other_ref, 1 - core)):
        for k, shift in enumerate((0, 2, 1, 3)):
            for p in range(4):
                w_ref[group ^ shift, p, c] = piece_ref[k, p, :, :cols]
                all_ref[group ^ shift, p, c] = piece_ref[k, p, :, cols:].astype(F32)
            out_w_ref[group ^ shift, c] = piece_ref[k, 4]
    rows = all_ref.shape[3]
    rows_ff = 4 * rows
    for z in range(4):
        for p in range(4):
            for c in range(2):
                start = ((z * 4 + p) * 2 + c) * rows
                vec_ref[:, start : start + rows] = all_ref[z, p, c, :, :rows]
    for c in range(2):
        for z in range(4):
            start = (c * 4 + z) * rows_ff
            up_ref[:, start : start + rows_ff] = all_ref[z, part, c, count : count + 2, :rows_ff]
    for p in range(4):
        for c in range(2):
            start = (p * 2 + c) * rows
            part_ref[:, start : start + rows] = all_ref[part, p, c, :, :rows]


def place_first(chain, mine, other, cols, count):
    _, _, rows, wide = mine.shape
    width = 32 * rows
    return call(
        chain,
        functools.partial(place_first_kernel, cols, count),
        "place_first_weights",
        [mine, other],
        [
            jax.ShapeDtypeStruct((4, 4, 2, rows, cols), mine.dtype),
            jax.ShapeDtypeStruct((4, 2, rows, wide), mine.dtype),
            jax.ShapeDtypeStruct((rows, width), F32),
            jax.ShapeDtypeStruct((2, 32 * rows), F32),
            jax.ShapeDtypeStruct((rows, 8 * rows), F32),
        ],
        scratch=[(4, 4, 2, rows, wide - cols)],
    )


def plane_swap(values, shift):
    return lax.ppermute(values, PLANE, [(i, i ^ shift) for i in range(4)])


def z_swap(values, shift):
    groups = lax.axis_size("z")
    return lax.ppermute(values, "z", [(z, z ^ shift) for z in range(groups)])


def core_swap(values):
    return lax.ppermute(values, "core", [(0, 1), (1, 0)])


def plane_gather(values):
    return [values] + [plane_swap(values, k) for k in (1, 2, 3)]


def tie(*values):
    return lax.optimization_barrier(values)


def plane_send(spreads):
    return [spreads[0]] + [plane_swap(spreads[k], k) for k in (1, 2, 3)]


def plane_total(sent):
    total = sent[0]
    for part in sent[1:]:
        total = total + part.astype(F32)
    return total


class Layout:
    def __init__(self, groups, rows):
        self.groups = groups
        self.devices = groups * 8
        self.subs = groups // rows

    def index(self, z, y, x, c):
        return ((z * 2 + y) * 2 + x) * 2 + c

    def token_moves(self):
        moves = []
        for z in range(self.groups):
            for y in range(2):
                for x in range(2):
                    for c in range(2):
                        row, block = 2 * x + c, 2 * z + y
                        group, within = row * self.subs + block // 8, block % 8
                        core, part = within // 4, within % 4
                        moves.append(
                            (self.index(z, y, x, c), self.index(group, part % 2, part // 2, core))
                        )
        return moves

    def back_moves(self):
        return [(b, a) for a, b in self.token_moves()]

    def turn_moves(self):
        moves = []
        for part in range(4):
            for z in range(self.groups):
                owner, user = part * self.groups + z, z * 4 + part
                moves.append((owner, user))
        return moves


def on_device(lay, core, part, sub, params, tokens):
    (
        enc_qkv,
        enc_out_w,
        enc_attn_bias,
        enc_up,
        enc_up_bias,
        enc_down,
        enc_down_bias,
        enc_gains,
        enc_shifts,
        self_qkv,
        self_out,
        self_bias,
        cross_qkv,
        cross_out,
        cross_bias,
        dec_up,
        dec_up_bias,
        dec_down,
        dec_down_bias,
        dec_gains,
        dec_shifts,
    ) = params
    src, tgt, src_seg, tgt_seg, out_grad = tokens
    groups = lay.groups
    width = src.shape[1]
    rows = enc_out_w.shape[0]
    rows_ff = enc_down.shape[0]
    quarter = width // 4
    hidden = rows_ff * groups * 2
    heads_out = enc_qkv.shape[0] * quarter

    chain = Chain()
    split = groups == 4
    ids = jnp.concatenate([src_seg, tgt_seg]).astype(BF16)
    ids = jnp.pad(ids[None], ((0, 7), (0, width - 2 * BLOCK)))
    packed = jnp.concatenate([src, ids, tgt, out_grad], axis=0)
    packed = lax.ppermute(packed, AXES, lay.token_moves())

    def heads_split(qkv):
        parts = qkv.reshape(3, rows, 4, quarter)
        return parts.transpose(2, 1, 0, 3).reshape(4, rows, heads_out)

    def up_split(up):
        parts = up.reshape(rows, groups, 4, 2, rows_ff)
        return parts.transpose(2, 0, 3, 1, 4).reshape(4, rows, hidden)

    def both_cores(mine, axis):
        other = core_swap(mine)
        shape = [1] * (mine.ndim + 1)
        shape[axis] = 2
        which = lax.broadcasted_iota(jnp.int32, shape, axis) == core
        return jnp.where(which, jnp.expand_dims(mine, axis), jnp.expand_dims(other, axis))

    def whole(kind, piece):
        cols = piece.shape[-1]
        piece = lax.all_gather(piece, "z", axis=0)
        return both_cores(piece, {"rows": 2, "down": 0, "out": 1}[kind]).reshape(-1, cols)

    def plane_turn(values):
        return lax.all_to_all(values, PLANE, split_axis=0, concat_axis=0, tiled=True)

    def out_turn(values):
        return lax.ppermute(values, ("z", "y", "x"), lay.turn_moves())

    vectors = jnp.concatenate(
        [
            enc_attn_bias,
            self_bias,
            cross_bias,
            enc_down_bias[None],
            dec_down_bias[None],
            enc_gains,
            dec_gains,
            enc_shifts,
            dec_shifts,
        ],
        axis=0,
    )
    vector_count = vectors.shape[0]
    if split:
        wide = width - heads_out
        extra = jnp.concatenate(
            [
                jnp.pad(vectors, ((0, 0), (0, wide - rows))),
                jnp.pad(jnp.stack([enc_up_bias, dec_up_bias]), ((0, 1), (0, wide - rows_ff))),
            ],
            axis=0,
        )
        extra = jnp.broadcast_to(extra[None], (4, rows, wide))
        first = plane_turn(jnp.concatenate([heads_split(enc_qkv), extra], axis=2))
        rest = jnp.concatenate(
            [heads_split(self_qkv), heads_split(cross_qkv), up_split(enc_up), up_split(dec_up)],
            axis=2,
        )
        first, rest = tie(first, rest)
        rest = plane_turn(rest).reshape(4 * rows, -1)
        outs = out_turn(jnp.concatenate([enc_out_w, self_out, cross_out], axis=0))
        turned, outs = outs[:rows], outs[rows:]
        first, packed = tie(first, packed)
        first = jnp.concatenate([first, turned[None]], axis=0)
        far = z_swap(first, 2)
        blocks = plane_gather(packed[: BLOCK + 8])
        far, blocks, rest = tie(far, blocks, rest)
        first = jnp.stack([first, far])
        first = jnp.concatenate([first, z_swap(first, 1)], axis=0)
        narrow = ((0, 0), (0, width - heads_out))
        w_self = jnp.pad(rest[:, :heads_out], narrow)
        w_cross = jnp.pad(rest[:, heads_out : 2 * heads_out], narrow)
        up = rest[:, 2 * heads_out : 2 * heads_out + hidden]
        one = jnp.concatenate([up, enc_down, outs, w_self], axis=0)
        one = lax.all_gather(one, "z", axis=0)
        up = rest[:, 2 * heads_out + hidden :]
        two = jnp.concatenate([up, dec_down, w_cross], axis=0)
        two = lax.all_gather(two, "z", axis=0)
        ffn_plan = [("rows", 0, 0), ("down", 4 * rows, 0)]
        ffn_shapes = [(rows, hidden), (rows_ff, width)]
        row = 4 * rows + rows_ff

    start = BLOCK + 8
    src, tgt, out_grad = packed[:BLOCK], packed[start : start + BLOCK], packed[start + BLOCK :]
    if not split:
        blocks = plane_gather(packed[:start])
    src_rows = [block[:BLOCK] for block in blocks]
    doc = jnp.concatenate([block[BLOCK : BLOCK + 1] for block in blocks], axis=0)
    doc = doc[:, : 2 * BLOCK].astype(F32).reshape(4, 2, BLOCK)
    count = jnp.stack(
        [
            jnp.sum((doc < 0.5).astype(F32), axis=(0, 2)),
            jnp.sum((doc < 1.5).astype(F32), axis=(0, 2)),
        ]
    )
    count = jnp.pad(count, ((0, 6), (0, BLOCK - 2)))
    count = count + core_swap(count)
    total = count
    for j in range(1, lay.subs):
        total = total + z_swap(count, j)
    count = total.astype(jnp.int32)

    if split:
        w_enc, wo_enc, vectors, ups, mine = place_first(
            chain, first, core_swap(first), heads_out, vector_count
        )
        w_enc, wo_enc = w_enc.reshape(width, heads_out), wo_enc.reshape(quarter, width)
    else:
        w_enc = whole("rows", plane_turn(heads_split(enc_qkv)))
        vectors = jnp.concatenate([vectors.reshape(-1), enc_up_bias, dec_up_bias])[None]
        vectors = lax.all_gather(vectors, AXES, axis=0, tiled=True).astype(F32)
        ups = vectors[:, vector_count * rows :].reshape(groups, 4, 2, 2, rows_ff)
        ups = lax.dynamic_index_in_dim(ups, part, axis=1, keepdims=False)
        ups = ups.transpose(2, 1, 0, 3).reshape(2, hidden)
        vectors = vectors[:, : vector_count * rows].reshape(lay.devices, vector_count, rows)
        vectors = vectors.transpose(1, 0, 2).reshape(vector_count, width)
        mine = lax.dynamic_slice_in_dim(vectors, part * quarter, quarter, axis=1)
        w_self = whole("rows", plane_turn(heads_split(self_qkv)))
        outs = out_turn(jnp.concatenate([enc_out_w, self_out, cross_out], axis=1))
        outs = whole("out", outs)
        wo_enc, wo_self, wo_cross = (outs[:, k * width : (k + 1) * width] for k in range(3))
        w_up_enc = whole("rows", plane_turn(up_split(enc_up)))
        w_down_enc = whole("down", enc_down)
        w_cross = whole("rows", plane_turn(heads_split(cross_qkv)))
        w_up_dec = whole("rows", plane_turn(up_split(dec_up)))
        w_down_dec = whole("down", dec_down)

    row_view = (4, 4, 2, rows)

    def with_others(kv):
        kv = [kv, core_swap(kv)]
        return kv + [z_swap(half, j) for j in range(1, lay.subs) for half in kv]

    def own_part(halves):
        own, other = halves[:2]
        for j in range(1, lay.subs):
            own = own + z_swap(halves[2 * j], j)
            other = other + z_swap(halves[2 * j + 1], j)
        return own, core_swap(other)

    enc_form, self_form, cross_form = (0, 0, False), (1, 1, True), (1, 0, False)
    q_enc, kv_enc, src_rows = project(chain, 0, src_rows, w_enc, mine)
    kv_enc = with_others(kv_enc)
    enc_saved, sent = attn_forward(chain, enc_form, count, q_enc, kv_enc, wo_enc)
    tgt_rows = plane_gather(tgt)
    sent = plane_send(sent)
    r_enc1, e1_low = norm(chain, src, sent, vectors, 2, (11, 16))
    e1_rows = plane_gather(e1_low)
    if split:
        e1_rows, one = tie(e1_rows, one)
        w_up_enc, w_down_enc, wo_self, wo_cross, w_self = place(
            chain,
            ffn_plan + [("out", row, 0), ("out", row + rows, 0), ("rows", row + 2 * rows, 0)],
            ffn_shapes + [(rows, width)] * 2 + [(rows, heads_out)],
            False,
            one,
            core_swap(one),
        )
    q_self, kv_self, tgt_rows = project(chain, 3, tgt_rows, w_self, mine)
    kv_self = with_others(kv_self)
    self_saved, mates = attn_forward(chain, self_form, count, q_self, kv_self, wo_self)
    e1_rows, sent = ffn_forward(chain, 0, e1_rows, w_up_enc, ups, w_down_enc, mates[1:])
    sent = plane_send(sent)
    r_enc2, encoded_low = norm(chain, r_enc1, sent, vectors, 9, (12, 17), (11, 16))
    sent = [mates[0], *sent[1:]]
    r_dec1, both_low = norm(
        chain, tgt, sent, vectors, 5, (13, 18), start=BLOCK, mate=(encoded_low,)
    )
    if split:
        both_low, two = tie(both_low, two)
    both_rows = plane_gather(both_low)
    if split:
        w_up_dec, w_down_dec, w_cross = place(
            chain,
            ffn_plan + [("rows", row, 0)],
            ffn_shapes + [(rows, heads_out)],
            False,
            two,
            core_swap(two),
        )
    q_cross, kv_cross, both_rows = project(chain, 6, both_rows, w_cross, mine, q_start=BLOCK)
    kv_cross = with_others(kv_cross)
    cross_saved, sent = attn_forward(chain, cross_form, count, q_cross, kv_cross, wo_cross)
    sent = plane_send(sent)
    r_dec2, t2_low = norm(chain, r_dec1, sent, vectors, 8, (14, 19), (13, 18))
    t2_rows = plane_gather(t2_low)
    t2_rows, sent = ffn_forward(chain, 1, t2_rows, w_up_dec, ups, w_down_dec)
    sent = plane_send(sent)
    r_dec3, t3_low = norm(chain, r_dec2, sent, vectors, 10, (15, 20), (14, 19))

    heads_view = row_view + (heads_out + BLOCK,)
    up_view = row_view + (hidden,)
    down_view = (2, 4, rows_ff, width)
    out_view = (4, 2, rows, width)
    if not split:
        heads_view, up_view = (width, heads_out), (width, hidden)
        down_view, out_view = (hidden, width), (quarter, width)

    def core_send(grad, kind):
        if split:
            return grad[0], core_swap(grad[1])
        axis = {"rows": 2, "down": 0, "out": 1}[kind]
        shape = {
            "rows": (groups, 4, 2, rows, -1),
            "down": (2, groups, rows_ff, width),
            "out": (groups, 2, rows, width),
        }[kind]
        grad = grad[0].reshape(shape)
        zero = lax.index_in_dim(grad, 0, axis, keepdims=False)
        one = lax.index_in_dim(grad, 1, axis, keepdims=False)
        send = jnp.where(core == 0, one, zero).astype(BF16)
        return jnp.where(core == 0, zero, one), core_swap(send)

    def stacked(*sends):
        keeps, gots = [x[0] for x in sends], [x[1] for x in sends]
        if split:
            return combine(chain, keeps, gots, width)
        sums = []
        for keep, got in zip(keeps, gots, strict=True):
            total = (keep + got.astype(F32)).astype(BF16)
            total = total.reshape(groups, -1, total.shape[-1])
            sums.append(jnp.pad(total, ((0, 0), (0, 0), (0, width - total.shape[-1]))))
        return jnp.concatenate(sums, axis=1)

    def z_reduce(grad):
        return lax.psum_scatter(grad, "z", scatter_dimension=0, tiled=False)

    def home(values):
        return lax.ppermute(values, AXES, lay.back_moves())

    def ffn_sends(bias, up, down):
        sends = [core_send(up, "rows"), core_send(down, "down")]
        if split:
            sends.append(core_send(bias, "bias"))
        return sends

    d_r3, low3, sums3 = norm_back(chain, [out_grad], r_dec3, vectors, 15)
    spreads, *grads = ffn_backward(
        chain, 1, split, t2_rows, plane_gather(low3), w_up_dec, ups, w_down_dec, up_view, down_view
    )
    upb_dec = grads[0]
    sent = plane_send(spreads)
    sends = ffn_sends(*grads)
    sent, sends = tie(sent, sends)
    d_r2, low2, sums2 = norm_back(chain, [d_r3, *sent], r_dec2, vectors, 14)

    low2_rows = plane_gather(low2)
    dec_ffn = z_reduce(stacked(*sends))
    dq, dkv, g_wo_cross = attn_backward(
        chain, cross_form, split, count, cross_saved, low2_rows, out_view
    )
    spreads, g_bias_cross, g_cross = project_back(
        chain,
        split,
        both_rows,
        w_cross,
        dq,
        *own_part(dkv),
        heads_view,
        [sums2, sums3],
        ((0, 2, 2), (1, 2, 3), (1, 0, 4), (1, 1, 5), (0, 0, 6), (0, 1, 7)),
    )
    sent = plane_send(spreads[1:])
    sends = [core_send(g_cross, "rows"), core_send(g_wo_cross, "out")]
    sent, sends = tie(sent, sends)

    d_e2, low_e2, sums_e2 = norm_back(chain, sent, r_enc2, vectors, 12)
    d_r1, both_low, sums1 = norm_back(
        chain, [d_r2, spreads[0], *sent[1:]], r_dec1, vectors, 13, start=BLOCK, mate=(low_e2,)
    )
    both_grads = plane_gather(both_low)
    cross = z_reduce(stacked(*sends))
    both_grads, dec_ffn = tie(both_grads, dec_ffn)
    spreads, *grads = ffn_backward(
        chain, 0, split, e1_rows, both_grads, w_up_enc, ups, w_down_enc, up_view, down_view
    )
    upb_enc = grads[0]
    sent = plane_send(spreads)
    sends = ffn_sends(*grads)
    dq_self, dkv_self, g_wo_self = attn_backward(
        chain, self_form, split, count, self_saved, both_grads, out_view, start=BLOCK
    )
    enc_ffn = stacked(*sends)
    sent, enc_ffn, dq_self = tie(sent, enc_ffn, dq_self)
    enc_ffn = z_reduce(enc_ffn)
    d_r1e, low_e1, sums_e1 = norm_back(chain, [d_e2, *sent], r_enc1, vectors, 11)

    low_e1_rows = plane_gather(low_e1)
    spreads_self, g_bias_self, g_self = project_back(
        chain,
        split,
        tgt_rows,
        w_self,
        dq_self,
        *own_part(dkv_self),
        heads_view,
        [sums1, sums_e2],
        ((0, 2, 2), (1, 2, 3), (0, 0, 4), (0, 1, 5), (1, 0, 6), (1, 1, 7)),
    )
    self_sends = [core_send(g_self, "rows"), core_send(g_wo_self, "out")]
    low_e1_rows, self_sends, cross = tie(low_e1_rows, self_sends, cross)
    own_self = z_reduce(stacked(*self_sends))
    dq_enc, dkv_enc, g_wo_enc = attn_backward(
        chain, enc_form, split, count, enc_saved, low_e1_rows, out_view
    )
    spreads, g_bias_enc, g_enc = project_back(
        chain,
        split,
        src_rows,
        w_enc,
        dq_enc,
        *own_part(dkv_enc),
        heads_view,
        [sums_e1],
        ((0, 2, 2), (0, 0, 4), (0, 1, 5)),
        mates=spreads_self[1:],
    )
    g_enc, g_wo_enc = core_send(g_enc, "rows"), core_send(g_wo_enc, "out")
    g_enc, enc_ffn = tie(g_enc, enc_ffn)
    sent = plane_send(spreads)

    if split:
        own_sum, far_sum, near = shares(chain, g_enc, g_wo_enc, width)
        near = z_swap(near, 1)
        near, dec_ffn, cross, enc_ffn = tie(near, dec_ffn, cross, enc_ffn)
        far_sum = z_swap(rounded_total(chain, [far_sum, near[1]]), 2)
        homes = both_totals(chain, [d_r1e, sent[0], d_r1, spreads_self[0], *sent[1:], t3_low])
        last = rounded_total(chain, [own_sum, near[0], far_sum])
        parts = jnp.concatenate(
            [
                enc_ffn[: 4 * rows].reshape(4, rows, hidden),
                own_self[: 4 * rows, : heads_out + BLOCK].reshape(4, rows, heads_out + BLOCK),
                last[:4],
                dec_ffn[: 4 * rows].reshape(4, rows, hidden),
                cross[: 4 * rows, : heads_out + BLOCK].reshape(4, rows, heads_out + BLOCK),
            ],
            axis=2,
        )
        parts = plane_turn(parts)
        outs = jnp.concatenate([last[4], own_self[4 * rows :], cross[4 * rows :]], axis=0)
        outs = lax.ppermute(outs, ("z", "y", "x"), [(b, a) for a, b in lay.turn_moves()])
        outs = outs.astype(F32)
        grads, small = join_last(chain, parts, heads_out)
        g_enc_up, g_self_qkv, g_enc_qkv, g_dec_up, g_cross_qkv = grads
        small = [x[0] if x.shape[0] == 1 else x for x in small]
        tail = 4 * rows + rows_ff
        g_upb_enc, g_upb_dec = (x[tail, :rows_ff].astype(F32) for x in (enc_ffn, dec_ffn))
        g_enc_down, g_dec_down = (x[4 * rows : tail].astype(F32) for x in (enc_ffn, dec_ffn))
    else:

        def heads_join(parts):
            parts = plane_turn(parts[:, :heads_out].reshape(4, rows, heads_out))
            parts = parts.reshape(4, rows, 3, quarter).transpose(2, 1, 0, 3)
            return parts.reshape(3, rows, width).astype(F32)

        def up_join(parts):
            parts = plane_turn(parts.reshape(4, rows, hidden))
            parts = parts.reshape(4, rows, 2, groups, rows_ff).transpose(1, 3, 0, 2, 4)
            return parts.reshape(rows, -1).astype(F32)

        homes = both_totals(chain, [d_r1e, sent[0], d_r1, spreads_self[0], *sent[1:], t3_low])
        last = z_reduce(stacked(g_enc, g_wo_enc))
        g_dec_up, g_enc_up = up_join(dec_ffn[: 4 * rows]), up_join(enc_ffn[: 4 * rows])
        g_enc_down, g_dec_down = (x[4 * rows :].astype(F32) for x in (enc_ffn, dec_ffn))
        g_cross_qkv, g_self_qkv, g_enc_qkv = (
            heads_join(x[: 4 * rows]) for x in (cross, own_self, last)
        )
        outs = jnp.concatenate([x[4 * rows :] for x in (last, own_self, cross)], axis=0)
        outs = lax.ppermute(outs, ("z", "y", "x"), [(b, a) for a, b in lay.turn_moves()])
        outs = outs.astype(F32)
        placed = jnp.concatenate([g_bias_enc[:2], g_bias_self[:2], g_bias_cross[:2]], axis=0)
        placed = lax.dynamic_update_slice(
            jnp.zeros((6, width), F32), placed, (jnp.int32(0), part * quarter)
        )
        lines = jnp.concatenate(
            [placed, sums_e1[:3], sums_e2[:3], sums1[:3], sums2[:3], sums3[:3]], axis=0
        )
        line_count = lines.shape[0]
        lines = lines.reshape(line_count, lay.devices, rows).transpose(1, 0, 2)
        lines = lines.reshape(lay.devices, line_count * rows)
        upb = jnp.concatenate([upb_enc[0], upb_dec[0]]).reshape(2, 2, groups, rows_ff)
        upb = lax.dynamic_update_slice(
            jnp.zeros((groups, 4, 2, 2, rows_ff), F32),
            upb.transpose(2, 1, 0, 3)[:, None],
            (jnp.int32(0), part, jnp.int32(0), jnp.int32(0), jnp.int32(0)),
        )
        lines = jnp.concatenate([lines, upb.reshape(lay.devices, 2 * rows_ff)], axis=1)
        lines = lax.all_to_all(lines, AXES, split_axis=0, concat_axis=0, tiled=True)
        lines = jnp.sum(lines, axis=0)
        upb = lines[line_count * rows :]
        g_upb_enc, g_upb_dec = upb[:rows_ff], upb[rows_ff:]
        lines = lines[: line_count * rows].reshape(line_count, rows)
        small = [
            jnp.stack([lines[0], lines[1], lines[8]]),
            lines[11],
            jnp.stack([lines[6], lines[9]]),
            jnp.stack([lines[7], lines[10]]),
            jnp.stack([lines[2], lines[3], lines[14]]),
            jnp.stack([lines[4], lines[5], lines[17]]),
            lines[20],
            jnp.stack([lines[12], lines[15], lines[18]]),
            jnp.stack([lines[13], lines[16], lines[19]]),
        ]
    g_enc_out, g_self_out, g_cross_out = outs[:rows], outs[rows : 2 * rows], outs[2 * rows :]

    homes = home(homes)
    bias_enc, down_enc, gains_enc, shifts_enc = small[:4]
    bias_self, bias_cross, down_dec, gains_dec, shifts_dec = small[4:]
    return (
        homes[None, 2 * BLOCK :],
        homes[None, :BLOCK].astype(F32),
        homes[None, BLOCK : 2 * BLOCK].astype(F32),
        g_enc_qkv,
        g_enc_out,
        bias_enc,
        g_enc_up,
        g_upb_enc,
        g_enc_down,
        down_enc,
        gains_enc,
        shifts_enc,
        g_self_qkv,
        g_self_out,
        bias_self,
        g_cross_qkv,
        g_cross_out,
        bias_cross,
        g_dec_up,
        g_upb_dec,
        g_dec_down,
        down_dec,
        gains_dec,
        shifts_dec,
    )


def solution(mesh):
    groups = mesh.shape["seq"] // 2
    rows = mesh.shape["dp"]
    lay = Layout(groups, rows)
    fine = Mesh(mesh.devices.reshape(groups, 2, 2, 2), AXES)
    seq, dp = ("z", "y"), ("x", "core")

    def run(
        src,
        tgt,
        src_seg,
        tgt_seg,
        enc_qkv,
        enc_out_w,
        enc_attn_bias,
        enc_up,
        enc_up_bias,
        enc_down,
        enc_down_bias,
        enc_gains,
        enc_shifts,
        self_qkv,
        self_out,
        self_bias,
        cross_qkv,
        cross_out,
        cross_bias,
        dec_up,
        dec_up_bias,
        dec_down,
        dec_down_bias,
        dec_gains,
        dec_shifts,
        out_grad,
    ):
        core = lax.axis_index("core")
        part = 2 * lax.axis_index("y") + lax.axis_index("x")
        sub = lax.axis_index("z") % lay.subs
        params = (
            enc_qkv,
            enc_out_w,
            enc_attn_bias,
            enc_up,
            enc_up_bias,
            enc_down,
            enc_down_bias,
            enc_gains,
            enc_shifts,
            self_qkv,
            self_out,
            self_bias,
            cross_qkv,
            cross_out,
            cross_bias,
            dec_up,
            dec_up_bias,
            dec_down,
            dec_down_bias,
            dec_gains,
            dec_shifts,
        )
        return on_device(
            lay, core, part, sub, params, (src[0], tgt[0], src_seg[0], tgt_seg[0], out_grad[0])
        )

    token = P(dp, seq, None)
    ids = P(dp, seq)
    stack = P(None, AXES, None)
    mat = P(AXES, None)
    vecs = P(None, AXES)
    vec = P(AXES)
    in_specs = (
        (token, token, ids, ids)
        + (stack, mat, vecs, mat, vec, mat, vec, vecs, vecs)
        + (stack, mat, vecs, stack, mat, vecs, mat, vec, mat, vec, vecs, vecs)
        + (token,)
    )
    out_specs = (
        (token, token, token)
        + (stack, mat, vecs, mat, vec, mat, vec, vecs, vecs)
        + (stack, mat, vecs, stack, mat, vecs, mat, vec, mat, vec, vecs, vecs)
    )
    return jax.shard_map(run, mesh=fine, in_specs=in_specs, out_specs=out_specs, check_vma=False)
```

```python
import functools

import jax
import jax.numpy as jnp
from jax import lax
from jax.experimental import pallas as pl
from jax.experimental.pallas import tpu as pltpu
from jax.sharding import Mesh
from jax.sharding import PartitionSpec as P

HEADS = 12
HEAD = 64
EPSILON = 1e-05
MASKED = -1e30
BLOCK = 128
F32 = jnp.float32
BF16 = jnp.bfloat16
AXES = ("z", "y", "x", "core")
PLANE = ("y", "x")
NT = (((1,), (1,)), ((), ()))
TN = (((0,), (0,)), ((), ()))


def matmul(left, right):
    return jnp.dot(left, right, preferred_element_type=F32)


def outer_sum(left, right):
    return lax.dot_general(left, right, TN, preferred_element_type=F32)


def back_matmul(left, right):
    return lax.dot_general(left, right, NT, preferred_element_type=F32)


def layer_norm(resid, gain, shift):
    center = resid - jnp.mean(resid, axis=-1, keepdims=True)
    second = jnp.mean(center * center, axis=-1, keepdims=True)
    return center * lax.rsqrt(second + EPSILON) * gain + shift


def positions(subs, index):
    core = lax.axis_index("core")
    part = 2 * lax.axis_index("x") + lax.axis_index("y")
    sub = lax.axis_index("z") & (subs - 1)
    group = lax.shift_right_logical(index, 10)
    half = lax.shift_right_logical(index, 9) & 1
    block = lax.shift_right_logical(index, 7) & 3
    block = ((block & 1) << 1) | lax.shift_right_logical(block, 1)
    return ((sub ^ group) << 10) + ((core ^ half) << 9) + ((part ^ block) << 7) + (index & 127)


def allowed_mask(form, count_ref, start, width, keys):
    query_kind, key_kind, causal = form
    subs = keys // (8 * BLOCK)
    query = positions(subs, lax.broadcasted_iota(jnp.int32, (1, width), 1) + start)
    key = positions(subs, lax.broadcasted_iota(jnp.int32, (keys, 1), 0))
    one, two = count_ref[0, key_kind], count_ref[1, key_kind]
    first = query >= count_ref[0, query_kind]
    second = query >= count_ref[1, query_kind]
    low = jnp.where(second, two, jnp.where(first, one, 0))
    high = jnp.where(second, keys, jnp.where(first, two, one))
    if causal:
        high = jnp.minimum(high, query + 1)
    return (key >= low) & (key < high)


def joined(refs, start=0):
    return jnp.concatenate([ref[start : start + BLOCK] for ref in refs], axis=0)


def spread(value, out_refs, start=0):
    out_refs[0][...] = value[:BLOCK]
    for k in (1, 2, 3):
        block = value[k * BLOCK : (k + 1) * BLOCK]
        out_refs[k][start : start + BLOCK] = block.astype(BF16)


def spread_shapes(width, blocks=1):
    return [jax.ShapeDtypeStruct((BLOCK, width), F32)] + [
        jax.ShapeDtypeStruct((blocks * BLOCK, width), BF16)
    ] * 3


def split_shapes(split, shape, core_axis):
    if not split:
        rows = 1
        for size in shape[:-1]:
            rows *= size
        return [jax.ShapeDtypeStruct((rows, shape[-1]), F32)]
    half = shape[:core_axis] + shape[core_axis + 1 :]
    return [jax.ShapeDtypeStruct(half, F32), jax.ShapeDtypeStruct(half, BF16)]


def put_halves(all_ref, core_axis, out_refs):
    core = lax.axis_index("core")
    lead = (slice(None),) * core_axis
    out_refs[0][...] = all_ref[lead + (core,)]
    out_refs[1][...] = all_ref[lead + (1 - core,)].astype(BF16)


class Chain:
    def __init__(self):
        self.token = jnp.zeros((8, BLOCK), F32)

    def tie(self, *values):
        self.token, *values = lax.optimization_barrier((self.token, *values))
        return values


def call(chain, kernel, name, ins, outs, scratch=(), smem=0, flops=0, trans=0):
    size = sum(x.size * x.dtype.itemsize for x in ins)
    size += sum(x.size * jnp.dtype(x.dtype).itemsize for x in outs)
    count, made = len(ins), len(outs)

    def body(*refs):
        refs[count + 1 + made][...] = refs[count][...]
        kernel(*refs[:count], *refs[count + 1 : count + 1 + made], *refs[count + 2 + made :])

    results = pl.pallas_call(
        body,
        out_shape=(*outs, jax.ShapeDtypeStruct((8, BLOCK), F32)),
        in_specs=[pl.BlockSpec(memory_space=pltpu.SMEM)] * smem + vmem_specs(count - smem + 1),
        out_specs=tuple(vmem_specs(made + 1)),
        scratch_shapes=[pltpu.VMEM(shape, F32) for shape in scratch],
        compiler_params=pltpu.CompilerParams(vmem_limit_bytes=24 << 20),
        cost_estimate=pl.CostEstimate(flops=flops, transcendentals=trans, bytes_accessed=size),
        name=name,
    )(*ins, chain.token)
    chain.token = results[-1]
    return results[:-1]


def vmem_specs(count):
    return [pl.BlockSpec(memory_space=pltpu.VMEM)] * count


def project_kernel(bias_row, q_start, x0, x1, x2, x3, w_ref, bias_ref, q_ref, kv_ref, rows_ref):
    pieces = (x0, x1, x2, x3)
    quarter = bias_ref.shape[1]
    rows = joined(pieces, q_start)
    if q_start:
        rows_ref[4 * BLOCK :] = rows
    value = matmul(rows, w_ref[:, :quarter]) + bias_ref[bias_row : bias_row + 1]
    q_ref[...] = value.astype(BF16) * BF16(HEAD**-0.5)
    rows = joined(pieces)
    rows_ref[: 4 * BLOCK] = rows
    kv_ref[:, :quarter] = matmul(rows, w_ref[:, quarter : 2 * quarter]).astype(BF16)
    value = matmul(rows, w_ref[:, 2 * quarter :]) + bias_ref[bias_row + 1 : bias_row + 2]
    kv_ref[:, quarter:] = value.astype(BF16)


def project(chain, bias_row, pieces, weight, biases, q_start=0):
    quarter = biases.shape[1]
    rows = 4 * BLOCK
    return call(
        chain,
        functools.partial(project_kernel, bias_row, q_start),
        "project_heads",
        [*pieces, weight, biases],
        [
            jax.ShapeDtypeStruct((rows, quarter), BF16),
            jax.ShapeDtypeStruct((rows, 2 * quarter), BF16),
            jax.ShapeDtypeStruct((rows * (2 if q_start else 1), weight.shape[0]), BF16),
        ],
        flops=2 * rows * weight.size,
    )


def attn_fwd_kernel(form, width, halves, count_ref, q_ref, wo_ref, *refs):
    kv_refs, (kept_ref, lse_ref), out_refs = refs[:halves], refs[halves : halves + 2], refs[halves + 2 : -1]
    ot_ref = refs[-1]
    quarter = q_ref.shape[1]
    kept_ref[:, :quarter] = q_ref[...]
    for j, ref in enumerate(kv_refs):
        kept_ref[:, (2 + 2 * j) * quarter : (4 + 2 * j) * quarter] = ref[...]
    keys = sum(ref.shape[0] for ref in kv_refs)
    for chunk in range(q_ref.shape[0] // width):
        rows = slice(chunk * width, (chunk + 1) * width)
        mask = allowed_mask(form, count_ref, chunk * width, width, keys)
        for head in range(quarter // HEAD):
            cols = slice(head * HEAD, (head + 1) * HEAD)
            wide = slice(quarter + head * HEAD, quarter + (head + 1) * HEAD)
            key = jnp.concatenate([ref[:, cols] for ref in kv_refs], axis=0)
            value = jnp.concatenate([ref[:, wide] for ref in kv_refs], axis=0)
            scores = lax.dot_general(key, q_ref[rows, cols], NT, preferred_element_type=F32)
            scores = jnp.where(mask, scores, MASKED)
            peak = jnp.max(scores, axis=0, keepdims=True)
            weights = jnp.exp(scores - peak)
            total = jnp.sum(weights, axis=0, keepdims=True)
            probs = (weights * (1.0 / total)).astype(BF16)
            ot_ref[cols, rows] = lax.dot_general(value, probs, TN, preferred_element_type=F32)
            lse_ref[head : head + 1, rows] = peak + jnp.log(total)
    mixture = ot_ref[...].T.astype(BF16)
    kept_ref[:, quarter : 2 * quarter] = mixture
    spread(matmul(mixture, wo_ref[...]), out_refs)


def attn_forward(chain, form, count, queries, kv, out_weight):
    rows, cols = queries.shape
    length = rows * len(kv)
    width = 256 if length <= 1024 else 128
    work = rows * length * cols
    outs = [
        jax.ShapeDtypeStruct((rows, cols * (2 + 2 * len(kv))), BF16),
        jax.ShapeDtypeStruct((8, rows), F32),
    ]
    kept, lse, *rest = call(
        chain,
        functools.partial(attn_fwd_kernel, form, width, len(kv)),
        "attn_forward",
        [count, queries, out_weight, *kv],
        outs + spread_shapes(out_weight.shape[1]),
        scratch=[(cols, rows)],
        smem=1,
        flops=8 * work,
        trans=work // HEAD,
    )
    return (kept, out_weight, lse), rest


def attn_bwd_kernel(form, width, halves, split, start, count_ref, kept_ref, wo_ref, lse_ref, *refs):
    low_refs, refs = refs[:4], refs[4:]
    quarter = wo_ref.shape[0]

    def kept(first):
        starts = [(2 + 2 * j) * quarter + first for j in range(halves)]
        return jnp.concatenate([kept_ref[:, at : at + HEAD] for at in starts], axis=0)

    dq_ref, dkv_refs, w_refs = refs[0], refs[1 : 1 + halves], refs[1 + halves : -3]
    dqt_ref, do_ref, all_ref = refs[-3:]
    half = kept_ref.shape[0]
    keys = half * halves
    low = joined(low_refs, start)
    do_ref[...] = back_matmul(low, wo_ref[...])
    grad_w = outer_sum(kept_ref[:, quarter : 2 * quarter], low)
    if split:
        all_ref[...] = grad_w.reshape(all_ref.shape)
        put_halves(all_ref, 1, w_refs)
    else:
        w_refs[0][...] = grad_w
    for chunk in range(half // width):
        rows = slice(chunk * width, (chunk + 1) * width)
        mask = allowed_mask(form, count_ref, chunk * width, width, keys)
        for head in range(quarter // HEAD):
            cols = slice(head * HEAD, (head + 1) * HEAD)
            wide = slice(quarter + head * HEAD, quarter + (head + 1) * HEAD)
            key, value = kept(head * HEAD), kept(quarter + head * HEAD)
            query, grad = kept_ref[rows, cols], do_ref[rows, cols].astype(BF16)
            scores = lax.dot_general(key, query, NT, preferred_element_type=F32)
            probs = jnp.where(mask, jnp.exp(scores - lse_ref[head : head + 1, rows]), 0.0)
            grad_probs = lax.dot_general(value, grad, NT, preferred_element_type=F32)
            product = probs * grad_probs
            delta = jnp.sum(product, axis=0, keepdims=True)
            grad_scores = (product - probs * delta).astype(BF16)
            grad_value = matmul(probs.astype(BF16), grad)
            grad_key = matmul(grad_scores, query)
            for j, ref in enumerate(dkv_refs):
                own = slice(j * half, (j + 1) * half)
                if chunk == 0:
                    ref[:, cols] = grad_key[own]
                    ref[:, wide] = grad_value[own]
                else:
                    ref[:, cols] += grad_key[own]
                    ref[:, wide] += grad_value[own]
            dqt_ref[cols, rows] = lax.dot_general(
                key, grad_scores, TN, preferred_element_type=F32
            ) * (HEAD**-0.5)
    dq_ref[...] = dqt_ref[...].T.astype(BF16)


def attn_backward(chain, form, split, count, saved, low, view, start=0):
    kept, out_weight, lse = saved
    rows, cols = kept.shape[0], out_weight.shape[0]
    halves = kept.shape[1] // (2 * cols) - 1
    length = rows * halves
    width = 256 if length <= 1024 else 128
    work = rows * length * cols
    outs = [jax.ShapeDtypeStruct((rows, cols), BF16)]
    outs += [jax.ShapeDtypeStruct((rows, 2 * cols), F32)] * halves
    outs += split_shapes(split, view, 1)
    dq, *rest = call(
        chain,
        functools.partial(attn_bwd_kernel, form, width, halves, split, start),
        "attn_backward",
        [count, kept, out_weight, lse, *low],
        outs,
        scratch=[(cols, rows), (rows, cols), view if split else (8, BLOCK)],
        smem=1,
        flops=20 * work,
        trans=work // HEAD,
    )
    return dq, rest[:halves], rest[halves:]


def project_back_kernel(cross, joins, split, picks, *refs):
    rows_ref, w_ref, dq_ref, own_ref, got_ref = refs[:5]
    refs = refs[5:]
    made = len({source for source, _, _ in picks})
    vec_refs, refs = refs[:made], refs[made:]
    mate_refs, refs = (refs[:3], refs[3:]) if joins else ((), refs)
    own_q_ref, refs = (refs[0], refs[1:]) if cross else (None, refs)
    out_refs, refs = refs[:4], refs[4:]
    bias_ref, w_refs, all_ref = refs[0], refs[1:-1], refs[-1]
    quarter = dq_ref.shape[1]
    dq = dq_ref[...]
    dkv = (own_ref[...] + got_ref[...]).astype(BF16)
    bias_ref[...] = jnp.zeros_like(bias_ref)
    bias_ref[0:1] = jnp.sum(dq.astype(F32), axis=0, keepdims=True)
    bias_ref[1:2] = jnp.sum(dkv[:, quarter:].astype(F32), axis=0, keepdims=True)
    from_q = back_matmul(dq, w_ref[:, :quarter])
    from_kv = back_matmul(dkv, w_ref[:, quarter:])
    if cross:
        spread(from_kv, out_refs)
        spread(from_q, (own_q_ref, *out_refs[1:]), BLOCK)
    else:
        spread(from_q + from_kv, out_refs)
    for ref, out_ref in zip(mate_refs, out_refs[1:], strict=False):
        out_ref[BLOCK:] = ref[...]
    rows_q = rows_kv = rows_ref[: 4 * BLOCK]
    if cross:
        rows_q = rows_ref[4 * BLOCK :]
    grads = (
        (slice(0, quarter), outer_sum(rows_q, dq)),
        (slice(quarter, 3 * quarter), outer_sum(rows_kv, dkv)),
    )
    for cols, grad in grads:
        if split:
            all_ref[..., cols] = grad.reshape(all_ref.shape[:-1] + (grad.shape[-1],))
        else:
            w_refs[0][:, cols] = grad
    if split:
        part = 2 * lax.axis_index("y") + lax.axis_index("x")
        lines = [None] * 8
        for source, row, lane in picks:
            lines[lane] = vec_refs[source][row : row + 1]
        blank = jnp.zeros_like(vec_refs[0][0:1])
        lines = jnp.concatenate([blank if line is None else line for line in lines], axis=0)
        extra = slice(3 * quarter, 3 * quarter + 8)
        all_ref[..., 3 * quarter :] = jnp.zeros_like(all_ref[..., 3 * quarter :])
        all_ref[..., extra] = lines.T.reshape(all_ref.shape[:-1] + (8,))
        heads = slice(3 * quarter, 3 * quarter + 2)
        all_ref[part, :, :, :, heads] = bias_ref[...].T[:, :2].reshape(all_ref.shape[1:-1] + (2,))
        put_halves(all_ref, 2, w_refs)


def project_back(
    chain, split, kept_rows, weight, dq, own, got, view, vecs, picks, mates=()
):
    rows, quarter = dq.shape
    width = weight.shape[0]
    cross = kept_rows.shape[0] > rows
    outs = [jax.ShapeDtypeStruct((BLOCK, width), F32)] if cross else []
    outs += spread_shapes(width, 2 if cross or mates else 1)
    count = len(outs)
    outs += [jax.ShapeDtypeStruct((8, quarter), F32)] + split_shapes(split, view, 2)
    results = call(
        chain,
        functools.partial(project_back_kernel, cross, bool(mates), split, picks),
        "project_back",
        [kept_rows, weight, dq, own, got, *vecs, *mates],
        outs,
        scratch=[view if split else (8, BLOCK)],
        flops=4 * rows * weight.size,
    )
    return results[:count], results[count], results[count + 1 :]


def norm_kernel(bias_row, line, before, start, base_ref, *refs):
    sent_refs, vec_ref, mate_refs, (resid_ref, low_ref) = refs[:4], refs[4], refs[5:-2], refs[-2:]

    def normed(resid, gain_row, shift_row):
        return layer_norm(
            resid, vec_ref[gain_row : gain_row + 1], vec_ref[shift_row : shift_row + 1]
        )

    base = base_ref[...].astype(F32)
    if before is not None:
        base = normed(base, *before)
    resid = base + vec_ref[bias_row : bias_row + 1] + sent_refs[0][...]
    for ref in sent_refs[1:]:
        resid = resid + ref[start : start + BLOCK].astype(F32)
    resid_ref[...] = resid
    at = BLOCK if mate_refs else 0
    for ref in mate_refs:
        low_ref[:BLOCK] = ref[...]
    low_ref[at:] = normed(resid, *line).astype(BF16)


def norm(chain, base, sent, vectors, bias_row, line, before=None, start=0, mate=()):
    rows, width = base.shape
    return call(
        chain,
        functools.partial(norm_kernel, bias_row, line, before, start),
        "layer_norm",
        [base, *sent, vectors, *mate],
        [
            jax.ShapeDtypeStruct((rows, width), F32),
            jax.ShapeDtypeStruct((rows * (1 + len(mate)), width), BF16),
        ],
    )


def norm_back_kernel(gain_row, count, start, *refs):
    grad_refs, (resid_ref, vec_ref), refs = refs[:count], refs[count : count + 2], refs[count + 2 :]
    mate_refs, out_refs = refs[:-3], refs[-3:]
    grad = None
    for ref in grad_refs:
        first = start if ref.shape[0] > BLOCK else 0
        part = ref[first : first + BLOCK].astype(F32)
        grad = part if grad is None else grad + part
    resid = resid_ref[...]
    center = resid - jnp.mean(resid, axis=-1, keepdims=True)
    scale = lax.rsqrt(jnp.mean(center * center, axis=-1, keepdims=True) + EPSILON)
    unit = center * scale
    weighted = grad * vec_ref[gain_row : gain_row + 1]
    both = grad * unit
    first = jnp.mean(weighted, axis=-1, keepdims=True)
    second = jnp.mean(weighted * unit, axis=-1, keepdims=True)
    value = (weighted - first - unit * second) * scale
    low = value.astype(BF16)
    out_refs[0][...] = value
    for ref in mate_refs:
        out_refs[1][:BLOCK] = ref[...]
    out_refs[1][BLOCK if mate_refs else 0 :] = low
    out_refs[2][...] = jnp.zeros_like(out_refs[2])
    for row, terms in enumerate((both, grad, low.astype(F32))):
        out_refs[2][row : row + 1] = jnp.sum(terms, axis=0, keepdims=True)


def norm_back(chain, grads, resid, vectors, gain_row, start=0, mate=()):
    rows, width = resid.shape
    return call(
        chain,
        functools.partial(norm_back_kernel, gain_row, len(grads), start),
        "layer_norm_back",
        [*grads, resid, vectors, *mate],
        [
            jax.ShapeDtypeStruct((rows, width), F32),
            jax.ShapeDtypeStruct((rows * (1 + len(mate)), width), BF16),
            jax.ShapeDtypeStruct((8, width), F32),
        ],
    )


def both_totals_kernel(*refs):
    for at, base_ref, own_ref in ((0, refs[0], refs[1]), (BLOCK, refs[2], refs[3])):
        total = base_ref[...] + own_ref[...]
        for ref in refs[4:7]:
            total = total + ref[at : at + BLOCK].astype(F32)
        refs[8][at : at + BLOCK] = total.astype(BF16)
    refs[8][2 * BLOCK :] = refs[7][...]


def both_totals(chain, parts):
    shape = (3 * BLOCK, parts[0].shape[1])
    (out,) = call(
        chain, both_totals_kernel, "sum_both", list(parts), [jax.ShapeDtypeStruct(shape, BF16)]
    )
    return out


def total_kernel(*refs):
    total = refs[0][...].astype(F32)
    for ref in refs[1:-1]:
        total = total + ref[...].astype(F32)
    refs[-1][...] = total.astype(BF16)


def rounded_total(chain, parts):
    outs = [jax.ShapeDtypeStruct(parts[0].shape, BF16)]
    (out,) = call(chain, total_kernel, "sum_parts", list(parts), outs)
    return out


def normal_cdf(values):
    return 0.5 + 0.5 * lax.erf(values * (0.5**0.5))


def ffn_fwd_kernel(layer, y0, y1, y2, y3, up_ref, bias_ref, down_ref, *refs):
    mate_refs, rows_ref, out_refs = refs[:-5], refs[-5], refs[-4:]
    rows = joined((y0, y1, y2, y3))
    rows_ref[...] = rows
    hidden = up_ref.shape[1]
    total = None
    for cols in (slice(0, hidden // 2), slice(hidden // 2, hidden)):
        pre = matmul(rows, up_ref[:, cols]) + bias_ref[layer : layer + 1, cols]
        act = (pre * normal_cdf(pre)).astype(BF16)
        part = matmul(act, down_ref[cols])
        total = part if total is None else total + part
    spread(total, out_refs)
    for ref, out_ref in zip(mate_refs, out_refs[1:], strict=False):
        out_ref[BLOCK:] = ref[...]


def ffn_forward(chain, layer, pieces, up, biases, down, mates=()):
    rows, *spreads = call(
        chain,
        functools.partial(ffn_fwd_kernel, layer),
        "ffn_forward",
        [*pieces, up, biases, down, *mates],
        [jax.ShapeDtypeStruct((4 * BLOCK, up.shape[0]), BF16)]
        + spread_shapes(down.shape[1], 2 if mates else 1),
        flops=16 * BLOCK * up.size,
        trans=4 * BLOCK * up.shape[1],
    )
    return rows, spreads


def ffn_bwd_kernel(layer, split, *refs):
    rows, low = refs[0][...], joined(refs[1:5])
    up_ref, bias_ref, down_ref = refs[5:8]
    out_refs, refs = refs[8:12], refs[12:]
    up_all, down_all, bias_all = refs[-3:]
    if split:
        bias_refs, up_refs, down_refs = refs[:2], refs[2:4], refs[4:6]
        bias_all[...] = jnp.zeros_like(bias_all)
    else:
        bias_refs, up_refs, down_refs = refs[:1], refs[1:2], refs[2:3]
    hidden = up_ref.shape[1]
    total = None
    for c, cols in enumerate((slice(0, hidden // 2), slice(hidden // 2, hidden))):
        pre = matmul(rows, up_ref[:, cols]) + bias_ref[layer : layer + 1, cols]
        cdf = normal_cdf(pre)
        act = (pre * cdf).astype(BF16)
        slope = cdf + pre * (jnp.exp(-0.5 * pre * pre) * (2.0 * jnp.pi) ** -0.5)
        grad = (back_matmul(low, down_ref[cols]) * slope).astype(BF16)
        grad_bias = jnp.sum(grad.astype(F32), axis=0, keepdims=True)
        grad_down, grad_up = outer_sum(act, low), outer_sum(rows, grad)
        if split:
            down_all[c] = grad_down.reshape(down_all.shape[1:])
            up_all[..., cols] = grad_up.reshape(up_all.shape[:-1] + (hidden // 2,))
            size = down_all.shape[2]
            for z in range(4):
                bias_all[c, z, 0:1, :size] = grad_bias[:, z * size : (z + 1) * size]
        else:
            bias_refs[0][:, cols] = grad_bias
            down_refs[0][cols] = grad_down
            up_refs[0][:, cols] = grad_up
        part = back_matmul(grad, up_ref[:, cols])
        total = part if total is None else total + part
    spread(total, out_refs)
    if split:
        put_halves(up_all, 2, up_refs)
        put_halves(down_all, 0, down_refs)
        put_halves(bias_all, 0, bias_refs)


def ffn_backward(chain, layer, split, rows, low, up, biases, down, up_view, down_view):
    hidden = up.shape[1]
    bias_view = (2, 4, 8, BLOCK) if split else (1, hidden)
    outs = spread_shapes(down.shape[1]) + split_shapes(split, bias_view, 0)
    outs += split_shapes(split, up_view, 2) + split_shapes(split, down_view, 0)
    tiny = (8, BLOCK)
    results = call(
        chain,
        functools.partial(ffn_bwd_kernel, layer, split),
        "ffn_backward",
        [rows, *low, up, biases, down],
        outs,
        scratch=[up_view, down_view, bias_view] if split else [tiny] * 3,
        flops=48 * BLOCK * up.size,
        trans=8 * BLOCK * hidden,
    )
    per = 2 if split else 1
    rest = results[4:]
    return results[:4], rest[:per], rest[per : 2 * per], rest[2 * per :]


def combine_kernel(count, *refs):
    out_ref = refs[-1]
    row = 0
    for keep_ref, got_ref in zip(refs[:count], refs[count:-1], strict=True):
        total = (keep_ref[...] + got_ref[...].astype(F32)).astype(BF16)
        _, size, cols = total.shape
        out_ref[:, row : row + size, :cols] = total
        if cols < out_ref.shape[2]:
            rest = jnp.zeros((total.shape[0], size, out_ref.shape[2] - cols), BF16)
            out_ref[:, row : row + size, cols:] = rest
        row += size


def combine(chain, keeps, gots, width):
    keeps = [x.reshape(x.shape[0], -1, x.shape[-1]) for x in keeps]
    gots = [x.reshape(x.shape[0], -1, x.shape[-1]) for x in gots]
    shape = (4, sum(x.shape[1] for x in keeps), width)
    (out,) = call(
        chain,
        functools.partial(combine_kernel, len(keeps)),
        "combine_gradients",
        [*keeps, *gots],
        [jax.ShapeDtypeStruct(shape, BF16)],
    )
    return out


def turned_kernel(count, *refs):
    group = lax.axis_index("z")
    outs = refs[2 * count :]
    targets = (outs[0], outs[1], outs[2].at[0], outs[2].at[1])
    for target, shift in zip(targets, (0, 2, 1, 3), strict=True):
        z, row = group ^ shift, 0
        for keep_ref, got_ref in zip(refs[:count], refs[count : 2 * count], strict=True):
            total = (keep_ref[z] + got_ref[z].astype(F32)).astype(target.dtype)
            size, cols = total.shape
            target[row : row + size, :cols] = total
            if cols < target.shape[1]:
                target[row : row + size, cols:] = jnp.zeros(
                    (size, target.shape[1] - cols), target.dtype
                )
            row += size


def group_sums(chain, sends, width):
    keeps = [x[0].reshape(4, -1, x[0].shape[-1]) for x in sends]
    gots = [x[1].reshape(4, -1, x[1].shape[-1]) for x in sends]
    shape = (sum(x.shape[1] for x in keeps), width)
    return call(
        chain,
        functools.partial(turned_kernel, len(keeps)),
        "turn_gradients",
        [*keeps, *gots],
        [jax.ShapeDtypeStruct(shape, F32)] * 2 + [jax.ShapeDtypeStruct((2, *shape), BF16)],
    )


def shares_kernel(keep_ref, got_ref, keep_out, got_out, *out_refs):
    group = lax.axis_index("z")
    cols, wide = keep_ref.shape[-1], out_refs[0].shape[-1]
    targets = (out_refs[0], out_refs[1], out_refs[2].at[0], out_refs[2].at[1])
    for ref, shift in zip(targets, (0, 2, 1, 3), strict=True):
        z = group ^ shift
        ref[:4, :, :cols] = (keep_ref[z] + got_ref[z].astype(F32)).astype(ref.dtype)
        ref[:4, :, cols:] = jnp.zeros((4, ref.shape[1], wide - cols), ref.dtype)
        ref[4] = (keep_out[z] + got_out[z].astype(F32)).astype(ref.dtype)


def shares(chain, heads, out, width):
    shape = (5, heads[0].shape[2], width)
    return call(
        chain,
        shares_kernel,
        "group_shares",
        [*heads, *out],
        [jax.ShapeDtypeStruct(shape, F32)] * 2 + [jax.ShapeDtypeStruct((2, *shape), BF16)],
    )


def join_heads(part_ref, col, out_ref):
    quarter = out_ref.shape[-1] // 4
    for j in range(3):
        for p in range(4):
            value = part_ref[p, :, col + j * quarter : col + (j + 1) * quarter]
            out_ref[j, :, p * quarter : (p + 1) * quarter] = value.astype(F32)


def join_up(part_ref, col, out_ref):
    size = out_ref.shape[1] // 32
    for z in range(4):
        for p in range(4):
            for c in range(2):
                start = ((z * 4 + p) * 2 + c) * size
                first = col + (c * 4 + z) * size
                out_ref[:, start : start + size] = part_ref[p, :, first : first + size].astype(F32)


def join_lines(part_ref, col, out_ref):
    total = part_ref[0, :, col : col + BLOCK].astype(F32)
    for p in (1, 2, 3):
        total = total + part_ref[p, :, col : col + BLOCK].astype(F32)
    out_ref[...] = total.T[:8]


def join_last_kernel(heads_out, part_ref, *refs):
    enc_up_ref, self_ref, enc_ref, dec_up_ref, cross_ref = refs[:5]
    lines = dict(zip("sec", refs[-3:], strict=True))
    hidden = enc_up_ref.shape[1] // 4
    wide = part_ref.shape[-1] - 2 * (hidden + heads_out + BLOCK)
    join_up(part_ref, 0, enc_up_ref)
    join_heads(part_ref, hidden, self_ref)
    join_lines(part_ref, hidden + heads_out, lines["s"])
    start = hidden + heads_out + BLOCK
    join_heads(part_ref, start, enc_ref)
    join_lines(part_ref, start + heads_out, lines["e"])
    start += wide
    join_up(part_ref, start, dec_up_ref)
    join_heads(part_ref, start + hidden, cross_ref)
    join_lines(part_ref, start + hidden + heads_out, lines["c"])
    for ref, picks in zip(refs[5:-3], LINES, strict=True):
        for row, (name, line) in enumerate(picks):
            ref[row : row + 1] = lines[name][line : line + 1]


LINES = (
    (("e", 0), ("e", 1), ("e", 2)),
    (("s", 3),),
    (("e", 4), ("s", 6)),
    (("e", 5), ("s", 7)),
    (("s", 0), ("s", 1), ("s", 2)),
    (("c", 0), ("c", 1), ("c", 2)),
    (("c", 3),),
    (("s", 4), ("c", 6), ("c", 4)),
    (("s", 5), ("c", 7), ("c", 5)),
)


def join_last(chain, parts, heads_out):
    _, rows, _ = parts.shape
    heads = jax.ShapeDtypeStruct((3, rows, 32 * rows), F32)
    up = jax.ShapeDtypeStruct((rows, 128 * rows), F32)
    results = call(
        chain,
        functools.partial(join_last_kernel, heads_out),
        "join_gradients",
        [parts],
        [up, heads, heads, up, heads]
        + [jax.ShapeDtypeStruct((len(picks), rows), F32) for picks in LINES],
        scratch=[(8, rows)] * 3,
    )
    return results[:5], results[5:]


def place_kernel(plan, turned, mine_ref, other_ref, *out_refs):
    group, core = lax.axis_index("z"), lax.axis_index("core")
    for piece_ref, c in ((mine_ref, core), (other_ref, 1 - core)):
        for k in range(4):
            z = group ^ k if turned else k
            for (kind, row, col), out_ref in zip(plan, out_refs, strict=True):
                count, cols = out_ref.shape[-2:]
                for p in range(4 if kind == "rows" else 1):
                    first = row + p * count
                    value = piece_ref[k, first : first + count, col : col + cols]
                    if kind == "rows":
                        out_ref[z, p, c] = value
                    elif kind == "down":
                        out_ref[c, z] = value
                    else:
                        out_ref[z, c] = value


def place(chain, plan, shapes, turned, mine, other):
    lead = {"rows": (4, 4, 2), "down": (2, 4), "out": (4, 2)}
    outs = call(
        chain,
        functools.partial(place_kernel, plan, turned),
        "place_weights",
        [mine, other],
        [
            jax.ShapeDtypeStruct(lead[entry[0]] + shape, mine.dtype)
            for entry, shape in zip(plan, shapes, strict=True)
        ],
    )
    outs = [out.reshape(-1, out.shape[-1]) for out in outs]
    return outs


def place_first_kernel(
    cols, count, mine_ref, other_ref, w_ref, out_w_ref, vec_ref, up_ref, part_ref, all_ref
):
    group, core = lax.axis_index("z"), lax.axis_index("core")
    part = 2 * lax.axis_index("y") + lax.axis_index("x")
    for piece_ref, c in ((mine_ref, core), (other_ref, 1 - core)):
        for k, shift in enumerate((0, 2, 1, 3)):
            for p in range(4):
                w_ref[group ^ shift, p, c] = piece_ref[k, p, :, :cols]
                all_ref[group ^ shift, p, c] = piece_ref[k, p, :, cols:].astype(F32)
            out_w_ref[group ^ shift, c] = piece_ref[k, 4]
    rows = all_ref.shape[3]
    rows_ff = 4 * rows
    for z in range(4):
        for p in range(4):
            for c in range(2):
                start = ((z * 4 + p) * 2 + c) * rows
                vec_ref[:, start : start + rows] = all_ref[z, p, c, :, :rows]
    for c in range(2):
        for z in range(4):
            start = (c * 4 + z) * rows_ff
            up_ref[:, start : start + rows_ff] = all_ref[z, part, c, count : count + 2, :rows_ff]
    for p in range(4):
        for c in range(2):
            start = (p * 2 + c) * rows
            part_ref[:, start : start + rows] = all_ref[part, p, c, :, :rows]


def place_first(chain, mine, other, cols, count):
    _, _, rows, wide = mine.shape
    width = 32 * rows
    return call(
        chain,
        functools.partial(place_first_kernel, cols, count),
        "place_first_weights",
        [mine, other],
        [
            jax.ShapeDtypeStruct((4, 4, 2, rows, cols), mine.dtype),
            jax.ShapeDtypeStruct((4, 2, rows, wide), mine.dtype),
            jax.ShapeDtypeStruct((rows, width), F32),
            jax.ShapeDtypeStruct((2, 32 * rows), F32),
            jax.ShapeDtypeStruct((rows, 8 * rows), F32),
        ],
        scratch=[(4, 4, 2, rows, wide - cols)],
    )


def plane_swap(values, shift):
    return lax.ppermute(values, PLANE, [(i, i ^ shift) for i in range(4)])


def z_swap(values, shift):
    groups = lax.axis_size("z")
    return lax.ppermute(values, "z", [(z, z ^ shift) for z in range(groups)])


def core_swap(values):
    return lax.ppermute(values, "core", [(0, 1), (1, 0)])


def plane_gather(values):
    return [values] + [plane_swap(values, k) for k in (1, 2, 3)]


def tie(*values):
    return lax.optimization_barrier(values)


def plane_send(spreads):
    return [spreads[0]] + [plane_swap(spreads[k], k) for k in (1, 2, 3)]


def plane_total(sent):
    total = sent[0]
    for part in sent[1:]:
        total = total + part.astype(F32)
    return total


class Layout:
    def __init__(self, groups, rows):
        self.groups = groups
        self.devices = groups * 8
        self.subs = groups // rows

    def index(self, z, y, x, c):
        return ((z * 2 + y) * 2 + x) * 2 + c

    def token_moves(self):
        moves = []
        for z in range(self.groups):
            for y in range(2):
                for x in range(2):
                    for c in range(2):
                        row, block = 2 * x + c, 2 * z + y
                        group, within = row * self.subs + block // 8, block % 8
                        core, part = within // 4, within % 4
                        moves.append(
                            (self.index(z, y, x, c), self.index(group, part % 2, part // 2, core))
                        )
        return moves

    def back_moves(self):
        return [(b, a) for a, b in self.token_moves()]

    def turn_moves(self):
        moves = []
        for part in range(4):
            for z in range(self.groups):
                owner, user = part * self.groups + z, z * 4 + part
                moves.append((owner, user))
        return moves


def on_device(lay, core, part, sub, params, tokens):
    (
        enc_qkv,
        enc_out_w,
        enc_attn_bias,
        enc_up,
        enc_up_bias,
        enc_down,
        enc_down_bias,
        enc_gains,
        enc_shifts,
        self_qkv,
        self_out,
        self_bias,
        cross_qkv,
        cross_out,
        cross_bias,
        dec_up,
        dec_up_bias,
        dec_down,
        dec_down_bias,
        dec_gains,
        dec_shifts,
    ) = params
    src, tgt, src_seg, tgt_seg, out_grad = tokens
    groups = lay.groups
    width = src.shape[1]
    rows = enc_out_w.shape[0]
    rows_ff = enc_down.shape[0]
    quarter = width // 4
    hidden = rows_ff * groups * 2
    heads_out = enc_qkv.shape[0] * quarter

    chain = Chain()
    split = groups == 4
    ids = jnp.concatenate([src_seg, tgt_seg]).astype(BF16)
    ids = jnp.pad(ids[None], ((0, 7), (0, width - 2 * BLOCK)))
    packed = jnp.concatenate([src, ids, tgt, out_grad], axis=0)
    packed = lax.ppermute(packed, AXES, lay.token_moves())

    def heads_split(qkv):
        parts = qkv.reshape(3, rows, 4, quarter)
        return parts.transpose(2, 1, 0, 3).reshape(4, rows, heads_out)

    def up_split(up):
        parts = up.reshape(rows, groups, 4, 2, rows_ff)
        return parts.transpose(2, 0, 3, 1, 4).reshape(4, rows, hidden)

    def both_cores(mine, axis):
        other = core_swap(mine)
        shape = [1] * (mine.ndim + 1)
        shape[axis] = 2
        which = lax.broadcasted_iota(jnp.int32, shape, axis) == core
        return jnp.where(which, jnp.expand_dims(mine, axis), jnp.expand_dims(other, axis))

    def whole(kind, piece):
        cols = piece.shape[-1]
        piece = lax.all_gather(piece, "z", axis=0)
        return both_cores(piece, {"rows": 2, "down": 0, "out": 1}[kind]).reshape(-1, cols)

    def plane_turn(values):
        return lax.all_to_all(values, PLANE, split_axis=0, concat_axis=0, tiled=True)

    def out_turn(values):
        return lax.ppermute(values, ("z", "y", "x"), lay.turn_moves())

    vectors = jnp.concatenate(
        [
            enc_attn_bias,
            self_bias,
            cross_bias,
            enc_down_bias[None],
            dec_down_bias[None],
            enc_gains,
            dec_gains,
            enc_shifts,
            dec_shifts,
        ],
        axis=0,
    )
    vector_count = vectors.shape[0]
    if split:
        wide = width - heads_out
        extra = jnp.concatenate(
            [
                jnp.pad(vectors, ((0, 0), (0, wide - rows))),
                jnp.pad(jnp.stack([enc_up_bias, dec_up_bias]), ((0, 1), (0, wide - rows_ff))),
            ],
            axis=0,
        )
        extra = jnp.broadcast_to(extra[None], (4, rows, wide))
        first = plane_turn(jnp.concatenate([heads_split(enc_qkv), extra], axis=2))
        rest = jnp.concatenate(
            [heads_split(self_qkv), heads_split(cross_qkv), up_split(enc_up), up_split(dec_up)],
            axis=2,
        )
        first, rest = tie(first, rest)
        rest = plane_turn(rest).reshape(4 * rows, -1)
        outs = out_turn(jnp.concatenate([enc_out_w, self_out, cross_out], axis=0))
        turned, outs = outs[:rows], outs[rows:]
        first, packed = tie(first, packed)
        first = jnp.concatenate([first, turned[None]], axis=0)
        far = z_swap(first, 2)
        blocks = plane_gather(packed[: BLOCK + 8])
        far, blocks, rest = tie(far, blocks, rest)
        first = jnp.stack([first, far])
        first = jnp.concatenate([first, z_swap(first, 1)], axis=0)
        narrow = ((0, 0), (0, width - heads_out))
        w_self = jnp.pad(rest[:, :heads_out], narrow)
        w_cross = jnp.pad(rest[:, heads_out : 2 * heads_out], narrow)
        up = rest[:, 2 * heads_out : 2 * heads_out + hidden]
        one = jnp.concatenate([up, enc_down, outs, w_self], axis=0)
        one = lax.all_gather(one, "z", axis=0)
        up = rest[:, 2 * heads_out + hidden :]
        two = jnp.concatenate([up, dec_down, w_cross], axis=0)
        two = lax.all_gather(two, "z", axis=0)
        ffn_plan = [("rows", 0, 0), ("down", 4 * rows, 0)]
        ffn_shapes = [(rows, hidden), (rows_ff, width)]
        row = 4 * rows + rows_ff

    start = BLOCK + 8
    src, tgt, out_grad = packed[:BLOCK], packed[start : start + BLOCK], packed[start + BLOCK :]
    if not split:
        blocks = plane_gather(packed[:start])
    src_rows = [block[:BLOCK] for block in blocks]
    doc = jnp.concatenate([block[BLOCK : BLOCK + 1] for block in blocks], axis=0)
    doc = doc[:, : 2 * BLOCK].astype(F32).reshape(4, 2, BLOCK)
    count = jnp.stack(
        [
            jnp.sum((doc < 0.5).astype(F32), axis=(0, 2)),
            jnp.sum((doc < 1.5).astype(F32), axis=(0, 2)),
        ]
    )
    count = jnp.pad(count, ((0, 6), (0, BLOCK - 2)))
    count = count + core_swap(count)
    total = count
    for j in range(1, lay.subs):
        total = total + z_swap(count, j)
    count = total.astype(jnp.int32)

    if split:
        w_enc, wo_enc, vectors, ups, mine = place_first(
            chain, first, core_swap(first), heads_out, vector_count
        )
        w_enc, wo_enc = w_enc.reshape(width, heads_out), wo_enc.reshape(quarter, width)
    else:
        w_enc = whole("rows", plane_turn(heads_split(enc_qkv)))
        vectors = jnp.concatenate([vectors.reshape(-1), enc_up_bias, dec_up_bias])[None]
        vectors = lax.all_gather(vectors, AXES, axis=0, tiled=True).astype(F32)
        ups = vectors[:, vector_count * rows :].reshape(groups, 4, 2, 2, rows_ff)
        ups = lax.dynamic_index_in_dim(ups, part, axis=1, keepdims=False)
        ups = ups.transpose(2, 1, 0, 3).reshape(2, hidden)
        vectors = vectors[:, : vector_count * rows].reshape(lay.devices, vector_count, rows)
        vectors = vectors.transpose(1, 0, 2).reshape(vector_count, width)
        mine = lax.dynamic_slice_in_dim(vectors, part * quarter, quarter, axis=1)
        w_self = whole("rows", plane_turn(heads_split(self_qkv)))
        outs = out_turn(jnp.concatenate([enc_out_w, self_out, cross_out], axis=1))
        outs = whole("out", outs)
        wo_enc, wo_self, wo_cross = (outs[:, k * width : (k + 1) * width] for k in range(3))
        w_up_enc = whole("rows", plane_turn(up_split(enc_up)))
        w_down_enc = whole("down", enc_down)
        w_cross = whole("rows", plane_turn(heads_split(cross_qkv)))
        w_up_dec = whole("rows", plane_turn(up_split(dec_up)))
        w_down_dec = whole("down", dec_down)

    row_view = (4, 4, 2, rows)

    def with_others(kv):
        kv = [kv, core_swap(kv)]
        return kv + [z_swap(half, j) for j in range(1, lay.subs) for half in kv]

    def own_part(halves):
        own, other = halves[:2]
        for j in range(1, lay.subs):
            own = own + z_swap(halves[2 * j], j)
            other = other + z_swap(halves[2 * j + 1], j)
        return own, core_swap(other)

    enc_form, self_form, cross_form = (0, 0, False), (1, 1, True), (1, 0, False)
    q_enc, kv_enc, src_rows = project(chain, 0, src_rows, w_enc, mine)
    kv_enc = with_others(kv_enc)
    enc_saved, sent = attn_forward(chain, enc_form, count, q_enc, kv_enc, wo_enc)
    tgt_rows = plane_gather(tgt)
    sent = plane_send(sent)
    r_enc1, e1_low = norm(chain, src, sent, vectors, 2, (11, 16))
    e1_rows = plane_gather(e1_low)
    if split:
        e1_rows, one = tie(e1_rows, one)
        w_up_enc, w_down_enc, wo_self, wo_cross, w_self = place(
            chain,
            ffn_plan + [("out", row, 0), ("out", row + rows, 0), ("rows", row + 2 * rows, 0)],
            ffn_shapes + [(rows, width)] * 2 + [(rows, heads_out)],
            False,
            one,
            core_swap(one),
        )
    q_self, kv_self, tgt_rows = project(chain, 3, tgt_rows, w_self, mine)
    kv_self = with_others(kv_self)
    self_saved, mates = attn_forward(chain, self_form, count, q_self, kv_self, wo_self)
    e1_rows, sent = ffn_forward(chain, 0, e1_rows, w_up_enc, ups, w_down_enc, mates[1:])
    sent = plane_send(sent)
    r_enc2, encoded_low = norm(chain, r_enc1, sent, vectors, 9, (12, 17), (11, 16))
    sent = [mates[0], *sent[1:]]
    r_dec1, both_low = norm(
        chain, tgt, sent, vectors, 5, (13, 18), start=BLOCK, mate=(encoded_low,)
    )
    if split:
        both_low, two = tie(both_low, two)
    both_rows = plane_gather(both_low)
    if split:
        w_up_dec, w_down_dec, w_cross = place(
            chain,
            ffn_plan + [("rows", row, 0)],
            ffn_shapes + [(rows, heads_out)],
            False,
            two,
            core_swap(two),
        )
    q_cross, kv_cross, both_rows = project(chain, 6, both_rows, w_cross, mine, q_start=BLOCK)
    kv_cross = with_others(kv_cross)
    cross_saved, sent = attn_forward(chain, cross_form, count, q_cross, kv_cross, wo_cross)
    sent = plane_send(sent)
    r_dec2, t2_low = norm(chain, r_dec1, sent, vectors, 8, (14, 19), (13, 18))
    t2_rows = plane_gather(t2_low)
    t2_rows, sent = ffn_forward(chain, 1, t2_rows, w_up_dec, ups, w_down_dec)
    sent = plane_send(sent)
    r_dec3, t3_low = norm(chain, r_dec2, sent, vectors, 10, (15, 20), (14, 19))

    heads_view = row_view + (heads_out + BLOCK,)
    up_view = row_view + (hidden,)
    down_view = (2, 4, rows_ff, width)
    out_view = (4, 2, rows, width)
    if not split:
        heads_view, up_view = (width, heads_out), (width, hidden)
        down_view, out_view = (hidden, width), (quarter, width)

    def core_send(grad, kind):
        if split:
            return grad[0], core_swap(grad[1])
        axis = {"rows": 2, "down": 0, "out": 1}[kind]
        shape = {
            "rows": (groups, 4, 2, rows, -1),
            "down": (2, groups, rows_ff, width),
            "out": (groups, 2, rows, width),
        }[kind]
        grad = grad[0].reshape(shape)
        zero = lax.index_in_dim(grad, 0, axis, keepdims=False)
        one = lax.index_in_dim(grad, 1, axis, keepdims=False)
        send = jnp.where(core == 0, one, zero).astype(BF16)
        return jnp.where(core == 0, zero, one), core_swap(send)

    def stacked(*sends):
        keeps, gots = [x[0] for x in sends], [x[1] for x in sends]
        if split:
            return combine(chain, keeps, gots, width)
        sums = []
        for keep, got in zip(keeps, gots, strict=True):
            total = (keep + got.astype(F32)).astype(BF16)
            total = total.reshape(groups, -1, total.shape[-1])
            sums.append(jnp.pad(total, ((0, 0), (0, 0), (0, width - total.shape[-1]))))
        return jnp.concatenate(sums, axis=1)

    def z_reduce(grad):
        return lax.psum_scatter(grad, "z", scatter_dimension=0, tiled=False)

    def home(values):
        return lax.ppermute(values, AXES, lay.back_moves())

    def ffn_sends(bias, up, down):
        sends = [core_send(up, "rows"), core_send(down, "down")]
        if split:
            sends.append(core_send(bias, "bias"))
        return sends

    d_r3, low3, sums3 = norm_back(chain, [out_grad], r_dec3, vectors, 15)
    spreads, *grads = ffn_backward(
        chain, 1, split, t2_rows, plane_gather(low3), w_up_dec, ups, w_down_dec, up_view, down_view
    )
    upb_dec = grads[0]
    sent = plane_send(spreads)
    sends = ffn_sends(*grads)
    sent, sends = tie(sent, sends)
    d_r2, low2, sums2 = norm_back(chain, [d_r3, *sent], r_dec2, vectors, 14)

    low2_rows = plane_gather(low2)
    dec_sends = sends
    dq, dkv, g_wo_cross = attn_backward(
        chain, cross_form, split, count, cross_saved, low2_rows, out_view
    )
    spreads, g_bias_cross, g_cross = project_back(
        chain,
        split,
        both_rows,
        w_cross,
        dq,
        *own_part(dkv),
        heads_view,
        [sums2, sums3],
        ((0, 2, 2), (1, 2, 3), (1, 0, 4), (1, 1, 5), (0, 0, 6), (0, 1, 7)),
    )
    sent = plane_send(spreads[1:])
    sends = [core_send(g_cross, "rows"), core_send(g_wo_cross, "out")]
    sent, sends = tie(sent, sends)

    d_e2, low_e2, sums_e2 = norm_back(chain, sent, r_enc2, vectors, 12)
    d_r1, both_low, sums1 = norm_back(
        chain, [d_r2, spreads[0], *sent[1:]], r_dec1, vectors, 13, start=BLOCK, mate=(low_e2,)
    )
    both_grads = plane_gather(both_low)
    decoder = z_reduce(stacked(*dec_sends, *sends))
    spreads, *grads = ffn_backward(
        chain, 0, split, e1_rows, both_grads, w_up_enc, ups, w_down_enc, up_view, down_view
    )
    upb_enc = grads[0]
    sent = plane_send(spreads)
    sends = ffn_sends(*grads)
    dq_self, dkv_self, g_wo_self = attn_backward(
        chain, self_form, split, count, self_saved, both_grads, out_view, start=BLOCK
    )
    enc_sends = sends
    if split:
        enc_own, enc_far, enc_near = group_sums(chain, enc_sends, width)
        enc_near = z_swap(enc_near, 1)
    d_r1e, low_e1, sums_e1 = norm_back(chain, [d_e2, *sent], r_enc1, vectors, 11)

    low_e1_rows = plane_gather(low_e1)
    if split:
        enc_far = z_swap(rounded_total(chain, [enc_far, enc_near[1]]), 2)
    spreads_self, g_bias_self, g_self = project_back(
        chain,
        split,
        tgt_rows,
        w_self,
        dq_self,
        *own_part(dkv_self),
        heads_view,
        [sums1, sums_e2],
        ((0, 2, 2), (1, 2, 3), (0, 0, 4), (0, 1, 5), (1, 0, 6), (1, 1, 7)),
    )
    self_sends = [core_send(g_self, "rows"), core_send(g_wo_self, "out")]
    if split:
        low_e1_rows, enc_far = tie(low_e1_rows, enc_far)
    own_self, decoder = tie(stacked(*self_sends), decoder)
    own_self = z_reduce(own_self)
    tall = decoder.shape[0] - 5 * rows
    dec_ffn, cross = decoder[:tall], decoder[tall:]
    dq_enc, dkv_enc, g_wo_enc = attn_backward(
        chain, enc_form, split, count, enc_saved, low_e1_rows, out_view
    )
    spreads, g_bias_enc, g_enc = project_back(
        chain,
        split,
        src_rows,
        w_enc,
        dq_enc,
        *own_part(dkv_enc),
        heads_view,
        [sums_e1],
        ((0, 2, 2), (0, 0, 4), (0, 1, 5)),
        mates=spreads_self[1:],
    )
    g_enc, g_wo_enc = core_send(g_enc, "rows"), core_send(g_wo_enc, "out")
    sent = plane_send(spreads)

    if split:
        own_sum, far_sum, near = shares(chain, g_enc, g_wo_enc, width)
        near = z_swap(near, 1)
        near, decoder = tie(near, decoder)
        dec_ffn, cross = decoder[:tall], decoder[tall:]
        enc_ffn = rounded_total(chain, [enc_own, enc_near[0], enc_far])
        far_sum = z_swap(rounded_total(chain, [far_sum, near[1]]), 2)
        homes = both_totals(chain, [d_r1e, sent[0], d_r1, spreads_self[0], *sent[1:], t3_low])
        last = rounded_total(chain, [own_sum, near[0], far_sum])
        parts = jnp.concatenate(
            [
                enc_ffn[: 4 * rows].reshape(4, rows, hidden),
                own_self[: 4 * rows, : heads_out + BLOCK].reshape(4, rows, heads_out + BLOCK),
                last[:4],
                dec_ffn[: 4 * rows].reshape(4, rows, hidden),
                cross[: 4 * rows, : heads_out + BLOCK].reshape(4, rows, heads_out + BLOCK),
            ],
            axis=2,
        )
        parts = plane_turn(parts)
        outs = jnp.concatenate([last[4], own_self[4 * rows :], cross[4 * rows :]], axis=0)
        outs = lax.ppermute(outs, ("z", "y", "x"), [(b, a) for a, b in lay.turn_moves()])
        outs = outs.astype(F32)
        grads, small = join_last(chain, parts, heads_out)
        g_enc_up, g_self_qkv, g_enc_qkv, g_dec_up, g_cross_qkv = grads
        small = [x[0] if x.shape[0] == 1 else x for x in small]
        tail = 4 * rows + rows_ff
        g_upb_enc, g_upb_dec = (x[tail, :rows_ff].astype(F32) for x in (enc_ffn, dec_ffn))
        g_enc_down, g_dec_down = (x[4 * rows : tail].astype(F32) for x in (enc_ffn, dec_ffn))
    else:

        def heads_join(parts):
            parts = plane_turn(parts[:, :heads_out].reshape(4, rows, heads_out))
            parts = parts.reshape(4, rows, 3, quarter).transpose(2, 1, 0, 3)
            return parts.reshape(3, rows, width).astype(F32)

        def up_join(parts):
            parts = plane_turn(parts.reshape(4, rows, hidden))
            parts = parts.reshape(4, rows, 2, groups, rows_ff).transpose(1, 3, 0, 2, 4)
            return parts.reshape(rows, -1).astype(F32)

        homes = both_totals(chain, [d_r1e, sent[0], d_r1, spreads_self[0], *sent[1:], t3_low])
        last = z_reduce(stacked(g_enc, g_wo_enc))
        enc_ffn = z_reduce(stacked(*enc_sends))
        g_dec_up, g_enc_up = up_join(dec_ffn[: 4 * rows]), up_join(enc_ffn[: 4 * rows])
        g_enc_down, g_dec_down = (x[4 * rows :].astype(F32) for x in (enc_ffn, dec_ffn))
        g_cross_qkv, g_self_qkv, g_enc_qkv = (
            heads_join(x[: 4 * rows]) for x in (cross, own_self, last)
        )
        outs = jnp.concatenate([x[4 * rows :] for x in (last, own_self, cross)], axis=0)
        outs = lax.ppermute(outs, ("z", "y", "x"), [(b, a) for a, b in lay.turn_moves()])
        outs = outs.astype(F32)
        placed = jnp.concatenate([g_bias_enc[:2], g_bias_self[:2], g_bias_cross[:2]], axis=0)
        placed = lax.dynamic_update_slice(
            jnp.zeros((6, width), F32), placed, (jnp.int32(0), part * quarter)
        )
        lines = jnp.concatenate(
            [placed, sums_e1[:3], sums_e2[:3], sums1[:3], sums2[:3], sums3[:3]], axis=0
        )
        line_count = lines.shape[0]
        lines = lines.reshape(line_count, lay.devices, rows).transpose(1, 0, 2)
        lines = lines.reshape(lay.devices, line_count * rows)
        upb = jnp.concatenate([upb_enc[0], upb_dec[0]]).reshape(2, 2, groups, rows_ff)
        upb = lax.dynamic_update_slice(
            jnp.zeros((groups, 4, 2, 2, rows_ff), F32),
            upb.transpose(2, 1, 0, 3)[:, None],
            (jnp.int32(0), part, jnp.int32(0), jnp.int32(0), jnp.int32(0)),
        )
        lines = jnp.concatenate([lines, upb.reshape(lay.devices, 2 * rows_ff)], axis=1)
        lines = lax.all_to_all(lines, AXES, split_axis=0, concat_axis=0, tiled=True)
        lines = jnp.sum(lines, axis=0)
        upb = lines[line_count * rows :]
        g_upb_enc, g_upb_dec = upb[:rows_ff], upb[rows_ff:]
        lines = lines[: line_count * rows].reshape(line_count, rows)
        small = [
            jnp.stack([lines[0], lines[1], lines[8]]),
            lines[11],
            jnp.stack([lines[6], lines[9]]),
            jnp.stack([lines[7], lines[10]]),
            jnp.stack([lines[2], lines[3], lines[14]]),
            jnp.stack([lines[4], lines[5], lines[17]]),
            lines[20],
            jnp.stack([lines[12], lines[15], lines[18]]),
            jnp.stack([lines[13], lines[16], lines[19]]),
        ]
    g_enc_out, g_self_out, g_cross_out = outs[:rows], outs[rows : 2 * rows], outs[2 * rows :]

    homes = home(homes)
    bias_enc, down_enc, gains_enc, shifts_enc = small[:4]
    bias_self, bias_cross, down_dec, gains_dec, shifts_dec = small[4:]
    return (
        homes[None, 2 * BLOCK :],
        homes[None, :BLOCK].astype(F32),
        homes[None, BLOCK : 2 * BLOCK].astype(F32),
        g_enc_qkv,
        g_enc_out,
        bias_enc,
        g_enc_up,
        g_upb_enc,
        g_enc_down,
        down_enc,
        gains_enc,
        shifts_enc,
        g_self_qkv,
        g_self_out,
        bias_self,
        g_cross_qkv,
        g_cross_out,
        bias_cross,
        g_dec_up,
        g_upb_dec,
        g_dec_down,
        down_dec,
        gains_dec,
        shifts_dec,
    )


def solution(mesh):
    groups = mesh.shape["seq"] // 2
    rows = mesh.shape["dp"]
    lay = Layout(groups, rows)
    fine = Mesh(mesh.devices.reshape(groups, 2, 2, 2), AXES)
    seq, dp = ("z", "y"), ("x", "core")

    def run(
        src,
        tgt,
        src_seg,
        tgt_seg,
        enc_qkv,
        enc_out_w,
        enc_attn_bias,
        enc_up,
        enc_up_bias,
        enc_down,
        enc_down_bias,
        enc_gains,
        enc_shifts,
        self_qkv,
        self_out,
        self_bias,
        cross_qkv,
        cross_out,
        cross_bias,
        dec_up,
        dec_up_bias,
        dec_down,
        dec_down_bias,
        dec_gains,
        dec_shifts,
        out_grad,
    ):
        core = lax.axis_index("core")
        part = 2 * lax.axis_index("y") + lax.axis_index("x")
        sub = lax.axis_index("z") % lay.subs
        params = (
            enc_qkv,
            enc_out_w,
            enc_attn_bias,
            enc_up,
            enc_up_bias,
            enc_down,
            enc_down_bias,
            enc_gains,
            enc_shifts,
            self_qkv,
            self_out,
            self_bias,
            cross_qkv,
            cross_out,
            cross_bias,
            dec_up,
            dec_up_bias,
            dec_down,
            dec_down_bias,
            dec_gains,
            dec_shifts,
        )
        return on_device(
            lay, core, part, sub, params, (src[0], tgt[0], src_seg[0], tgt_seg[0], out_grad[0])
        )

    token = P(dp, seq, None)
    ids = P(dp, seq)
    stack = P(None, AXES, None)
    mat = P(AXES, None)
    vecs = P(None, AXES)
    vec = P(AXES)
    in_specs = (
        (token, token, ids, ids)
        + (stack, mat, vecs, mat, vec, mat, vec, vecs, vecs)
        + (stack, mat, vecs, stack, mat, vecs, mat, vec, mat, vec, vecs, vecs)
        + (token,)
    )
    out_specs = (
        (token, token, token)
        + (stack, mat, vecs, mat, vec, mat, vec, vecs, vecs)
        + (stack, mat, vecs, stack, mat, vecs, mat, vec, mat, vec, vecs, vecs)
    )
    return jax.shard_map(run, mesh=fine, in_specs=in_specs, out_specs=out_specs, check_vma=False)
```

```python
import functools

import jax
import jax.numpy as jnp
from jax import lax
from jax.experimental import pallas as pl
from jax.experimental.pallas import tpu as pltpu
from jax.sharding import Mesh
from jax.sharding import PartitionSpec as P

HEADS = 12
HEAD = 64
EPSILON = 1e-05
MASKED = -1e30
BLOCK = 128
F32 = jnp.float32
BF16 = jnp.bfloat16
AXES = ("z", "y", "x", "core")
PLANE = ("y", "x")
NT = (((1,), (1,)), ((), ()))
TN = (((0,), (0,)), ((), ()))


def matmul(left, right):
    return jnp.dot(left, right, preferred_element_type=F32)


def outer_sum(left, right):
    return lax.dot_general(left, right, TN, preferred_element_type=F32)


def back_matmul(left, right):
    return lax.dot_general(left, right, NT, preferred_element_type=F32)


def layer_norm(resid, gain, shift):
    center = resid - jnp.mean(resid, axis=-1, keepdims=True)
    second = jnp.mean(center * center, axis=-1, keepdims=True)
    return center * lax.rsqrt(second + EPSILON) * gain + shift


def positions(subs, index):
    core = lax.axis_index("core")
    part = 2 * lax.axis_index("x") + lax.axis_index("y")
    sub = lax.axis_index("z") & (subs - 1)
    group = lax.shift_right_logical(index, 10)
    half = lax.shift_right_logical(index, 9) & 1
    block = lax.shift_right_logical(index, 7) & 3
    block = ((block & 1) << 1) | lax.shift_right_logical(block, 1)
    return ((sub ^ group) << 10) + ((core ^ half) << 9) + ((part ^ block) << 7) + (index & 127)


def allowed_mask(form, count_ref, start, width, keys):
    query_kind, key_kind, causal = form
    subs = keys // (8 * BLOCK)
    query = positions(subs, lax.broadcasted_iota(jnp.int32, (1, width), 1) + start)
    key = positions(subs, lax.broadcasted_iota(jnp.int32, (keys, 1), 0))
    one, two = count_ref[0, key_kind], count_ref[1, key_kind]
    first = query >= count_ref[0, query_kind]
    second = query >= count_ref[1, query_kind]
    low = jnp.where(second, two, jnp.where(first, one, 0))
    high = jnp.where(second, keys, jnp.where(first, two, one))
    if causal:
        high = jnp.minimum(high, query + 1)
    return (key >= low) & (key < high)


def joined(refs, start=0):
    return jnp.concatenate([ref[start : start + BLOCK] for ref in refs], axis=0)


def spread(value, out_refs, start=0):
    out_refs[0][...] = value[:BLOCK]
    for k in (1, 2, 3):
        block = value[k * BLOCK : (k + 1) * BLOCK]
        out_refs[k][start : start + BLOCK] = block.astype(BF16)


def spread_shapes(width, blocks=1):
    return [jax.ShapeDtypeStruct((BLOCK, width), F32)] + [
        jax.ShapeDtypeStruct((blocks * BLOCK, width), BF16)
    ] * 3


def split_shapes(split, shape, core_axis):
    if not split:
        rows = 1
        for size in shape[:-1]:
            rows *= size
        return [jax.ShapeDtypeStruct((rows, shape[-1]), F32)]
    half = shape[:core_axis] + shape[core_axis + 1 :]
    return [jax.ShapeDtypeStruct(half, F32), jax.ShapeDtypeStruct(half, BF16)]


def put_halves(all_ref, core_axis, out_refs):
    core = lax.axis_index("core")
    lead = (slice(None),) * core_axis
    out_refs[0][...] = all_ref[lead + (core,)]
    out_refs[1][...] = all_ref[lead + (1 - core,)].astype(BF16)


class Chain:
    def __init__(self):
        self.token = jnp.zeros((8, BLOCK), F32)

    def tie(self, *values):
        self.token, *values = lax.optimization_barrier((self.token, *values))
        return values


def call(chain, kernel, name, ins, outs, scratch=(), smem=0, flops=0, trans=0):
    size = sum(x.size * x.dtype.itemsize for x in ins)
    size += sum(x.size * jnp.dtype(x.dtype).itemsize for x in outs)
    count, made = len(ins), len(outs)

    def body(*refs):
        refs[count + 1 + made][...] = refs[count][...]
        kernel(*refs[:count], *refs[count + 1 : count + 1 + made], *refs[count + 2 + made :])

    results = pl.pallas_call(
        body,
        out_shape=(*outs, jax.ShapeDtypeStruct((8, BLOCK), F32)),
        in_specs=[pl.BlockSpec(memory_space=pltpu.SMEM)] * smem + vmem_specs(count - smem + 1),
        out_specs=tuple(vmem_specs(made + 1)),
        scratch_shapes=[pltpu.VMEM(shape, F32) for shape in scratch],
        compiler_params=pltpu.CompilerParams(vmem_limit_bytes=24 << 20),
        cost_estimate=pl.CostEstimate(flops=flops, transcendentals=trans, bytes_accessed=size),
        name=name,
    )(*ins, chain.token)
    chain.token = results[-1]
    return results[:-1]


def vmem_specs(count):
    return [pl.BlockSpec(memory_space=pltpu.VMEM)] * count


def project_kernel(bias_row, q_start, x0, x1, x2, x3, w_ref, bias_ref, q_ref, kv_ref, rows_ref):
    pieces = (x0, x1, x2, x3)
    quarter = bias_ref.shape[1]
    rows = joined(pieces, q_start)
    if q_start:
        rows_ref[4 * BLOCK :] = rows
    value = matmul(rows, w_ref[:, :quarter]) + bias_ref[bias_row : bias_row + 1]
    q_ref[...] = value.astype(BF16) * BF16(HEAD**-0.5)
    rows = joined(pieces)
    rows_ref[: 4 * BLOCK] = rows
    kv_ref[:, :quarter] = matmul(rows, w_ref[:, quarter : 2 * quarter]).astype(BF16)
    value = matmul(rows, w_ref[:, 2 * quarter :]) + bias_ref[bias_row + 1 : bias_row + 2]
    kv_ref[:, quarter:] = value.astype(BF16)


def project(chain, bias_row, pieces, weight, biases, q_start=0):
    quarter = biases.shape[1]
    rows = 4 * BLOCK
    return call(
        chain,
        functools.partial(project_kernel, bias_row, q_start),
        "project_heads",
        [*pieces, weight, biases],
        [
            jax.ShapeDtypeStruct((rows, quarter), BF16),
            jax.ShapeDtypeStruct((rows, 2 * quarter), BF16),
            jax.ShapeDtypeStruct((rows * (2 if q_start else 1), weight.shape[0]), BF16),
        ],
        flops=2 * rows * weight.size,
    )


def attn_fwd_kernel(form, width, halves, count_ref, q_ref, wo_ref, *refs):
    kv_refs, (kept_ref, lse_ref), out_refs = refs[:halves], refs[halves : halves + 2], refs[halves + 2 : -1]
    ot_ref = refs[-1]
    quarter = q_ref.shape[1]
    kept_ref[:, :quarter] = q_ref[...]
    for j, ref in enumerate(kv_refs):
        kept_ref[:, (2 + 2 * j) * quarter : (4 + 2 * j) * quarter] = ref[...]
    keys = sum(ref.shape[0] for ref in kv_refs)
    for chunk in range(q_ref.shape[0] // width):
        rows = slice(chunk * width, (chunk + 1) * width)
        mask = allowed_mask(form, count_ref, chunk * width, width, keys)
        for head in range(quarter // HEAD):
            cols = slice(head * HEAD, (head + 1) * HEAD)
            wide = slice(quarter + head * HEAD, quarter + (head + 1) * HEAD)
            key = jnp.concatenate([ref[:, cols] for ref in kv_refs], axis=0)
            value = jnp.concatenate([ref[:, wide] for ref in kv_refs], axis=0)
            scores = lax.dot_general(key, q_ref[rows, cols], NT, preferred_element_type=F32)
            scores = jnp.where(mask, scores, MASKED)
            peak = jnp.max(scores, axis=0, keepdims=True)
            weights = jnp.exp(scores - peak)
            total = jnp.sum(weights, axis=0, keepdims=True)
            probs = (weights * (1.0 / total)).astype(BF16)
            ot_ref[cols, rows] = lax.dot_general(value, probs, TN, preferred_element_type=F32)
            lse_ref[head : head + 1, rows] = peak + jnp.log(total)
    mixture = ot_ref[...].T.astype(BF16)
    kept_ref[:, quarter : 2 * quarter] = mixture
    spread(matmul(mixture, wo_ref[...]), out_refs)


def attn_forward(chain, form, count, queries, kv, out_weight):
    rows, cols = queries.shape
    length = rows * len(kv)
    width = 256 if length <= 1024 else 128
    work = rows * length * cols
    outs = [
        jax.ShapeDtypeStruct((rows, cols * (2 + 2 * len(kv))), BF16),
        jax.ShapeDtypeStruct((8, rows), F32),
    ]
    kept, lse, *rest = call(
        chain,
        functools.partial(attn_fwd_kernel, form, width, len(kv)),
        "attn_forward",
        [count, queries, out_weight, *kv],
        outs + spread_shapes(out_weight.shape[1]),
        scratch=[(cols, rows)],
        smem=1,
        flops=8 * work,
        trans=work // HEAD,
    )
    return (kept, out_weight, lse), rest


def attn_bwd_kernel(form, width, halves, split, start, count_ref, kept_ref, wo_ref, lse_ref, *refs):
    low_refs, refs = refs[:4], refs[4:]
    quarter = wo_ref.shape[0]

    def kept(first):
        starts = [(2 + 2 * j) * quarter + first for j in range(halves)]
        return jnp.concatenate([kept_ref[:, at : at + HEAD] for at in starts], axis=0)

    dq_ref, dkv_refs, w_refs = refs[0], refs[1 : 1 + halves], refs[1 + halves : -3]
    dqt_ref, do_ref, all_ref = refs[-3:]
    half = kept_ref.shape[0]
    keys = half * halves
    low = joined(low_refs, start)
    do_ref[...] = back_matmul(low, wo_ref[...])
    grad_w = outer_sum(kept_ref[:, quarter : 2 * quarter], low)
    if split:
        all_ref[...] = grad_w.reshape(all_ref.shape)
        put_halves(all_ref, 1, w_refs)
    else:
        w_refs[0][...] = grad_w
    for chunk in range(half // width):
        rows = slice(chunk * width, (chunk + 1) * width)
        mask = allowed_mask(form, count_ref, chunk * width, width, keys)
        for head in range(quarter // HEAD):
            cols = slice(head * HEAD, (head + 1) * HEAD)
            wide = slice(quarter + head * HEAD, quarter + (head + 1) * HEAD)
            key, value = kept(head * HEAD), kept(quarter + head * HEAD)
            query, grad = kept_ref[rows, cols], do_ref[rows, cols].astype(BF16)
            scores = lax.dot_general(key, query, NT, preferred_element_type=F32)
            probs = jnp.where(mask, jnp.exp(scores - lse_ref[head : head + 1, rows]), 0.0)
            grad_probs = lax.dot_general(value, grad, NT, preferred_element_type=F32)
            product = probs * grad_probs
            delta = jnp.sum(product, axis=0, keepdims=True)
            grad_scores = (product - probs * delta).astype(BF16)
            grad_value = matmul(probs.astype(BF16), grad)
            grad_key = matmul(grad_scores, query)
            for j, ref in enumerate(dkv_refs):
                own = slice(j * half, (j + 1) * half)
                if chunk == 0:
                    ref[:, cols] = grad_key[own]
                    ref[:, wide] = grad_value[own]
                else:
                    ref[:, cols] += grad_key[own]
                    ref[:, wide] += grad_value[own]
            dqt_ref[cols, rows] = lax.dot_general(
                key, grad_scores, TN, preferred_element_type=F32
            ) * (HEAD**-0.5)
    dq_ref[...] = dqt_ref[...].T.astype(BF16)


def attn_backward(chain, form, split, count, saved, low, view, start=0):
    kept, out_weight, lse = saved
    rows, cols = kept.shape[0], out_weight.shape[0]
    halves = kept.shape[1] // (2 * cols) - 1
    length = rows * halves
    width = 256 if length <= 1024 else 128
    work = rows * length * cols
    outs = [jax.ShapeDtypeStruct((rows, cols), BF16)]
    outs += [jax.ShapeDtypeStruct((rows, 2 * cols), F32)] * halves
    outs += split_shapes(split, view, 1)
    dq, *rest = call(
        chain,
        functools.partial(attn_bwd_kernel, form, width, halves, split, start),
        "attn_backward",
        [count, kept, out_weight, lse, *low],
        outs,
        scratch=[(cols, rows), (rows, cols), view if split else (8, BLOCK)],
        smem=1,
        flops=20 * work,
        trans=work // HEAD,
    )
    return dq, rest[:halves], rest[halves:]


def project_back_kernel(cross, joins, split, picks, *refs):
    rows_ref, w_ref, dq_ref, own_ref, got_ref = refs[:5]
    refs = refs[5:]
    made = len({source for source, _, _ in picks})
    vec_refs, refs = refs[:made], refs[made:]
    mate_refs, refs = (refs[:3], refs[3:]) if joins else ((), refs)
    own_q_ref, refs = (refs[0], refs[1:]) if cross else (None, refs)
    out_refs, refs = refs[:4], refs[4:]
    bias_ref, w_refs, all_ref = refs[0], refs[1:-1], refs[-1]
    quarter = dq_ref.shape[1]
    dq = dq_ref[...]
    dkv = (own_ref[...] + got_ref[...]).astype(BF16)
    bias_ref[...] = jnp.zeros_like(bias_ref)
    bias_ref[0:1] = jnp.sum(dq.astype(F32), axis=0, keepdims=True)
    bias_ref[1:2] = jnp.sum(dkv[:, quarter:].astype(F32), axis=0, keepdims=True)
    from_q = back_matmul(dq, w_ref[:, :quarter])
    from_kv = back_matmul(dkv, w_ref[:, quarter:])
    if cross:
        spread(from_kv, out_refs)
        spread(from_q, (own_q_ref, *out_refs[1:]), BLOCK)
    else:
        spread(from_q + from_kv, out_refs)
    for ref, out_ref in zip(mate_refs, out_refs[1:], strict=False):
        out_ref[BLOCK:] = ref[...]
    rows_q = rows_kv = rows_ref[: 4 * BLOCK]
    if cross:
        rows_q = rows_ref[4 * BLOCK :]
    grads = (
        (slice(0, quarter), outer_sum(rows_q, dq)),
        (slice(quarter, 3 * quarter), outer_sum(rows_kv, dkv)),
    )
    for cols, grad in grads:
        if split:
            all_ref[..., cols] = grad.reshape(all_ref.shape[:-1] + (grad.shape[-1],))
        else:
            w_refs[0][:, cols] = grad
    if split:
        part = 2 * lax.axis_index("y") + lax.axis_index("x")
        lines = [None] * 8
        for source, row, lane in picks:
            lines[lane] = vec_refs[source][row : row + 1]
        blank = jnp.zeros_like(vec_refs[0][0:1])
        lines = jnp.concatenate([blank if line is None else line for line in lines], axis=0)
        extra = slice(3 * quarter, 3 * quarter + 8)
        all_ref[..., 3 * quarter :] = jnp.zeros_like(all_ref[..., 3 * quarter :])
        all_ref[..., extra] = lines.T.reshape(all_ref.shape[:-1] + (8,))
        heads = slice(3 * quarter, 3 * quarter + 2)
        all_ref[part, :, :, :, heads] = bias_ref[...].T[:, :2].reshape(all_ref.shape[1:-1] + (2,))
        put_halves(all_ref, 2, w_refs)


def project_back(
    chain, split, kept_rows, weight, dq, own, got, view, vecs, picks, mates=()
):
    rows, quarter = dq.shape
    width = weight.shape[0]
    cross = kept_rows.shape[0] > rows
    outs = [jax.ShapeDtypeStruct((BLOCK, width), F32)] if cross else []
    outs += spread_shapes(width, 2 if cross or mates else 1)
    count = len(outs)
    outs += [jax.ShapeDtypeStruct((8, quarter), F32)] + split_shapes(split, view, 2)
    results = call(
        chain,
        functools.partial(project_back_kernel, cross, bool(mates), split, picks),
        "project_back",
        [kept_rows, weight, dq, own, got, *vecs, *mates],
        outs,
        scratch=[view if split else (8, BLOCK)],
        flops=4 * rows * weight.size,
    )
    return results[:count], results[count], results[count + 1 :]


def norm_kernel(bias_row, line, before, start, base_ref, *refs):
    sent_refs, vec_ref, mate_refs, (resid_ref, low_ref) = refs[:4], refs[4], refs[5:-2], refs[-2:]

    def normed(resid, gain_row, shift_row):
        return layer_norm(
            resid, vec_ref[gain_row : gain_row + 1], vec_ref[shift_row : shift_row + 1]
        )

    base = base_ref[...].astype(F32)
    if before is not None:
        base = normed(base, *before)
    resid = base + vec_ref[bias_row : bias_row + 1] + sent_refs[0][...]
    for ref in sent_refs[1:]:
        resid = resid + ref[start : start + BLOCK].astype(F32)
    resid_ref[...] = resid
    at = BLOCK if mate_refs else 0
    for ref in mate_refs:
        low_ref[:BLOCK] = ref[...]
    low_ref[at:] = normed(resid, *line).astype(BF16)


def norm(chain, base, sent, vectors, bias_row, line, before=None, start=0, mate=()):
    rows, width = base.shape
    return call(
        chain,
        functools.partial(norm_kernel, bias_row, line, before, start),
        "layer_norm",
        [base, *sent, vectors, *mate],
        [
            jax.ShapeDtypeStruct((rows, width), F32),
            jax.ShapeDtypeStruct((rows * (1 + len(mate)), width), BF16),
        ],
    )


def norm_back_kernel(gain_row, count, start, *refs):
    grad_refs, (resid_ref, vec_ref), refs = refs[:count], refs[count : count + 2], refs[count + 2 :]
    mate_refs, out_refs = refs[:-3], refs[-3:]
    grad = None
    for ref in grad_refs:
        first = start if ref.shape[0] > BLOCK else 0
        part = ref[first : first + BLOCK].astype(F32)
        grad = part if grad is None else grad + part
    resid = resid_ref[...]
    center = resid - jnp.mean(resid, axis=-1, keepdims=True)
    scale = lax.rsqrt(jnp.mean(center * center, axis=-1, keepdims=True) + EPSILON)
    unit = center * scale
    weighted = grad * vec_ref[gain_row : gain_row + 1]
    both = grad * unit
    first = jnp.mean(weighted, axis=-1, keepdims=True)
    second = jnp.mean(weighted * unit, axis=-1, keepdims=True)
    value = (weighted - first - unit * second) * scale
    low = value.astype(BF16)
    out_refs[0][...] = value
    for ref in mate_refs:
        out_refs[1][:BLOCK] = ref[...]
    out_refs[1][BLOCK if mate_refs else 0 :] = low
    out_refs[2][...] = jnp.zeros_like(out_refs[2])
    for row, terms in enumerate((both, grad, low.astype(F32))):
        out_refs[2][row : row + 1] = jnp.sum(terms, axis=0, keepdims=True)


def norm_back(chain, grads, resid, vectors, gain_row, start=0, mate=()):
    rows, width = resid.shape
    return call(
        chain,
        functools.partial(norm_back_kernel, gain_row, len(grads), start),
        "layer_norm_back",
        [*grads, resid, vectors, *mate],
        [
            jax.ShapeDtypeStruct((rows, width), F32),
            jax.ShapeDtypeStruct((rows * (1 + len(mate)), width), BF16),
            jax.ShapeDtypeStruct((8, width), F32),
        ],
    )


def both_totals_kernel(*refs):
    for at, base_ref, own_ref in ((0, refs[0], refs[1]), (BLOCK, refs[2], refs[3])):
        total = base_ref[...] + own_ref[...]
        for ref in refs[4:7]:
            total = total + ref[at : at + BLOCK].astype(F32)
        refs[7][at : at + BLOCK] = total.astype(BF16)


def both_totals(chain, parts):
    shape = (2 * BLOCK, parts[0].shape[1])
    (out,) = call(
        chain, both_totals_kernel, "sum_both", list(parts), [jax.ShapeDtypeStruct(shape, BF16)]
    )
    return out


def total_kernel(*refs):
    total = refs[0][...].astype(F32)
    for ref in refs[1:-1]:
        total = total + ref[...].astype(F32)
    refs[-1][...] = total.astype(BF16)


def rounded_total(chain, parts):
    outs = [jax.ShapeDtypeStruct(parts[0].shape, BF16)]
    (out,) = call(chain, total_kernel, "sum_parts", list(parts), outs)
    return out


def normal_cdf(values):
    return 0.5 + 0.5 * lax.erf(values * (0.5**0.5))


def ffn_fwd_kernel(layer, y0, y1, y2, y3, up_ref, bias_ref, down_ref, *refs):
    mate_refs, rows_ref, out_refs = refs[:-5], refs[-5], refs[-4:]
    rows = joined((y0, y1, y2, y3))
    rows_ref[...] = rows
    hidden = up_ref.shape[1]
    total = None
    for cols in (slice(0, hidden // 2), slice(hidden // 2, hidden)):
        pre = matmul(rows, up_ref[:, cols]) + bias_ref[layer : layer + 1, cols]
        act = (pre * normal_cdf(pre)).astype(BF16)
        part = matmul(act, down_ref[cols])
        total = part if total is None else total + part
    spread(total, out_refs)
    for ref, out_ref in zip(mate_refs, out_refs[1:], strict=False):
        out_ref[BLOCK:] = ref[...]


def ffn_forward(chain, layer, pieces, up, biases, down, mates=()):
    rows, *spreads = call(
        chain,
        functools.partial(ffn_fwd_kernel, layer),
        "ffn_forward",
        [*pieces, up, biases, down, *mates],
        [jax.ShapeDtypeStruct((4 * BLOCK, up.shape[0]), BF16)]
        + spread_shapes(down.shape[1], 2 if mates else 1),
        flops=16 * BLOCK * up.size,
        trans=4 * BLOCK * up.shape[1],
    )
    return rows, spreads


def ffn_bwd_kernel(layer, split, *refs):
    rows, low = refs[0][...], joined(refs[1:5])
    up_ref, bias_ref, down_ref = refs[5:8]
    out_refs, refs = refs[8:12], refs[12:]
    up_all, down_all, bias_all = refs[-3:]
    if split:
        bias_refs, up_refs, down_refs = refs[:2], refs[2:4], refs[4:6]
        bias_all[...] = jnp.zeros_like(bias_all)
    else:
        bias_refs, up_refs, down_refs = refs[:1], refs[1:2], refs[2:3]
    hidden = up_ref.shape[1]
    total = None
    for c, cols in enumerate((slice(0, hidden // 2), slice(hidden // 2, hidden))):
        pre = matmul(rows, up_ref[:, cols]) + bias_ref[layer : layer + 1, cols]
        cdf = normal_cdf(pre)
        act = (pre * cdf).astype(BF16)
        slope = cdf + pre * (jnp.exp(-0.5 * pre * pre) * (2.0 * jnp.pi) ** -0.5)
        grad = (back_matmul(low, down_ref[cols]) * slope).astype(BF16)
        grad_bias = jnp.sum(grad.astype(F32), axis=0, keepdims=True)
        grad_down, grad_up = outer_sum(act, low), outer_sum(rows, grad)
        if split:
            down_all[c] = grad_down.reshape(down_all.shape[1:])
            up_all[..., cols] = grad_up.reshape(up_all.shape[:-1] + (hidden // 2,))
            size = down_all.shape[2]
            for z in range(4):
                bias_all[c, z, 0:1, :size] = grad_bias[:, z * size : (z + 1) * size]
        else:
            bias_refs[0][:, cols] = grad_bias
            down_refs[0][cols] = grad_down
            up_refs[0][:, cols] = grad_up
        part = back_matmul(grad, up_ref[:, cols])
        total = part if total is None else total + part
    spread(total, out_refs)
    if split:
        put_halves(up_all, 2, up_refs)
        put_halves(down_all, 0, down_refs)
        put_halves(bias_all, 0, bias_refs)


def ffn_backward(chain, layer, split, rows, low, up, biases, down, up_view, down_view):
    hidden = up.shape[1]
    bias_view = (2, 4, 8, BLOCK) if split else (1, hidden)
    outs = spread_shapes(down.shape[1]) + split_shapes(split, bias_view, 0)
    outs += split_shapes(split, up_view, 2) + split_shapes(split, down_view, 0)
    tiny = (8, BLOCK)
    results = call(
        chain,
        functools.partial(ffn_bwd_kernel, layer, split),
        "ffn_backward",
        [rows, *low, up, biases, down],
        outs,
        scratch=[up_view, down_view, bias_view] if split else [tiny] * 3,
        flops=48 * BLOCK * up.size,
        trans=8 * BLOCK * hidden,
    )
    per = 2 if split else 1
    rest = results[4:]
    return results[:4], rest[:per], rest[per : 2 * per], rest[2 * per :]


def combine_kernel(count, *refs):
    out_ref = refs[-1]
    row = 0
    for keep_ref, got_ref in zip(refs[:count], refs[count:-1], strict=True):
        total = (keep_ref[...] + got_ref[...].astype(F32)).astype(BF16)
        _, size, cols = total.shape
        out_ref[:, row : row + size, :cols] = total
        if cols < out_ref.shape[2]:
            rest = jnp.zeros((total.shape[0], size, out_ref.shape[2] - cols), BF16)
            out_ref[:, row : row + size, cols:] = rest
        row += size


def combine(chain, keeps, gots, width):
    keeps = [x.reshape(x.shape[0], -1, x.shape[-1]) for x in keeps]
    gots = [x.reshape(x.shape[0], -1, x.shape[-1]) for x in gots]
    shape = (4, sum(x.shape[1] for x in keeps), width)
    (out,) = call(
        chain,
        functools.partial(combine_kernel, len(keeps)),
        "combine_gradients",
        [*keeps, *gots],
        [jax.ShapeDtypeStruct(shape, BF16)],
    )
    return out


def turned_kernel(count, *refs):
    group = lax.axis_index("z")
    outs = refs[2 * count :]
    targets = (outs[0], outs[1], outs[2].at[0], outs[2].at[1])
    for target, shift in zip(targets, (0, 2, 1, 3), strict=True):
        z, row = group ^ shift, 0
        for keep_ref, got_ref in zip(refs[:count], refs[count : 2 * count], strict=True):
            total = (keep_ref[z] + got_ref[z].astype(F32)).astype(target.dtype)
            size, cols = total.shape
            target[row : row + size, :cols] = total
            if cols < target.shape[1]:
                target[row : row + size, cols:] = jnp.zeros(
                    (size, target.shape[1] - cols), target.dtype
                )
            row += size


def group_sums(chain, sends, width):
    keeps = [x[0].reshape(4, -1, x[0].shape[-1]) for x in sends]
    gots = [x[1].reshape(4, -1, x[1].shape[-1]) for x in sends]
    shape = (sum(x.shape[1] for x in keeps), width)
    return call(
        chain,
        functools.partial(turned_kernel, len(keeps)),
        "turn_gradients",
        [*keeps, *gots],
        [jax.ShapeDtypeStruct(shape, F32)] * 2 + [jax.ShapeDtypeStruct((2, *shape), BF16)],
    )


def shares_kernel(keep_ref, got_ref, keep_out, got_out, *out_refs):
    group = lax.axis_index("z")
    cols, wide = keep_ref.shape[-1], out_refs[0].shape[-1]
    targets = (out_refs[0], out_refs[1], out_refs[2].at[0], out_refs[2].at[1])
    for ref, shift in zip(targets, (0, 2, 1, 3), strict=True):
        z = group ^ shift
        ref[:4, :, :cols] = (keep_ref[z] + got_ref[z].astype(F32)).astype(ref.dtype)
        ref[:4, :, cols:] = jnp.zeros((4, ref.shape[1], wide - cols), ref.dtype)
        ref[4] = (keep_out[z] + got_out[z].astype(F32)).astype(ref.dtype)


def shares(chain, heads, out, width):
    shape = (5, heads[0].shape[2], width)
    return call(
        chain,
        shares_kernel,
        "group_shares",
        [*heads, *out],
        [jax.ShapeDtypeStruct(shape, F32)] * 2 + [jax.ShapeDtypeStruct((2, *shape), BF16)],
    )


def join_heads(part_ref, col, out_ref):
    quarter = out_ref.shape[-1] // 4
    for j in range(3):
        for p in range(4):
            value = part_ref[p, :, col + j * quarter : col + (j + 1) * quarter]
            out_ref[j, :, p * quarter : (p + 1) * quarter] = value.astype(F32)


def join_up(part_ref, col, out_ref):
    size = out_ref.shape[1] // 32
    for z in range(4):
        for p in range(4):
            for c in range(2):
                start = ((z * 4 + p) * 2 + c) * size
                first = col + (c * 4 + z) * size
                out_ref[:, start : start + size] = part_ref[p, :, first : first + size].astype(F32)


def join_lines(part_ref, col, out_ref):
    total = part_ref[0, :, col : col + BLOCK].astype(F32)
    for p in (1, 2, 3):
        total = total + part_ref[p, :, col : col + BLOCK].astype(F32)
    out_ref[...] = total.T[:8]


def join_layer_kernel(heads_out, part_ref, up_ref, heads_ref, line_ref):
    hidden = part_ref.shape[-1] - heads_out - BLOCK
    join_up(part_ref, 0, up_ref)
    join_heads(part_ref, hidden, heads_ref)
    join_lines(part_ref, hidden + heads_out, line_ref)


def join_layer(chain, parts, heads_out):
    _, rows, _ = parts.shape
    return call(
        chain,
        functools.partial(join_layer_kernel, heads_out),
        "join_gradients",
        [parts],
        [
            jax.ShapeDtypeStruct((rows, 128 * rows), F32),
            jax.ShapeDtypeStruct((3, rows, 32 * rows), F32),
            jax.ShapeDtypeStruct((8, rows), F32),
        ],
    )


def join_last_kernel(heads_out, part_ref, cross_ref, enc_up_ref, self_ref, enc_ref, *refs):
    lines = {"s": refs[-2], "e": refs[-1], "c": cross_ref}
    hidden = enc_up_ref.shape[1] // 4
    join_up(part_ref, 0, enc_up_ref)
    join_heads(part_ref, hidden, self_ref)
    join_lines(part_ref, hidden + heads_out, lines["s"])
    start = hidden + heads_out + BLOCK
    join_heads(part_ref, start, enc_ref)
    join_lines(part_ref, start + heads_out, lines["e"])
    for ref, picks in zip(refs[:-2], LINES, strict=True):
        for row, (name, line) in enumerate(picks):
            ref[row : row + 1] = lines[name][line : line + 1]


LINES = (
    (("e", 0), ("e", 1), ("e", 2)),
    (("s", 3),),
    (("e", 4), ("s", 6)),
    (("e", 5), ("s", 7)),
    (("s", 0), ("s", 1), ("s", 2)),
    (("c", 0), ("c", 1), ("c", 2)),
    (("c", 3),),
    (("s", 4), ("c", 6), ("c", 4)),
    (("s", 5), ("c", 7), ("c", 5)),
)


def join_last(chain, parts, cross_lines, heads_out):
    _, rows, _ = parts.shape
    heads = jax.ShapeDtypeStruct((3, rows, 32 * rows), F32)
    up = jax.ShapeDtypeStruct((rows, 128 * rows), F32)
    results = call(
        chain,
        functools.partial(join_last_kernel, heads_out),
        "join_gradients",
        [parts, cross_lines],
        [up, heads, heads] + [jax.ShapeDtypeStruct((len(picks), rows), F32) for picks in LINES],
        scratch=[(8, rows)] * 2,
    )
    return results[:3], results[3:]


def place_kernel(plan, turned, mine_ref, other_ref, *out_refs):
    group, core = lax.axis_index("z"), lax.axis_index("core")
    for piece_ref, c in ((mine_ref, core), (other_ref, 1 - core)):
        for k in range(4):
            z = group ^ k if turned else k
            for (kind, row, col), out_ref in zip(plan, out_refs, strict=True):
                count, cols = out_ref.shape[-2:]
                for p in range(4 if kind == "rows" else 1):
                    first = row + p * count
                    value = piece_ref[k, first : first + count, col : col + cols]
                    if kind == "rows":
                        out_ref[z, p, c] = value
                    elif kind == "down":
                        out_ref[c, z] = value
                    else:
                        out_ref[z, c] = value


def place(chain, plan, shapes, turned, mine, other):
    lead = {"rows": (4, 4, 2), "down": (2, 4), "out": (4, 2)}
    outs = call(
        chain,
        functools.partial(place_kernel, plan, turned),
        "place_weights",
        [mine, other],
        [
            jax.ShapeDtypeStruct(lead[entry[0]] + shape, mine.dtype)
            for entry, shape in zip(plan, shapes, strict=True)
        ],
    )
    outs = [out.reshape(-1, out.shape[-1]) for out in outs]
    return outs


def place_first_kernel(
    cols, count, mine_ref, other_ref, w_ref, out_w_ref, vec_ref, up_ref, part_ref, all_ref
):
    group, core = lax.axis_index("z"), lax.axis_index("core")
    part = 2 * lax.axis_index("y") + lax.axis_index("x")
    for piece_ref, c in ((mine_ref, core), (other_ref, 1 - core)):
        for k, shift in enumerate((0, 2, 1, 3)):
            for p in range(4):
                w_ref[group ^ shift, p, c] = piece_ref[k, p, :, :cols]
                all_ref[group ^ shift, p, c] = piece_ref[k, p, :, cols:].astype(F32)
            out_w_ref[group ^ shift, c] = piece_ref[k, 4]
    rows = all_ref.shape[3]
    rows_ff = 4 * rows
    for z in range(4):
        for p in range(4):
            for c in range(2):
                start = ((z * 4 + p) * 2 + c) * rows
                vec_ref[:, start : start + rows] = all_ref[z, p, c, :, :rows]
    for c in range(2):
        for z in range(4):
            start = (c * 4 + z) * rows_ff
            up_ref[:, start : start + rows_ff] = all_ref[z, part, c, count : count + 2, :rows_ff]
    for p in range(4):
        for c in range(2):
            start = (p * 2 + c) * rows
            part_ref[:, start : start + rows] = all_ref[part, p, c, :, :rows]


def place_first(chain, mine, other, cols, count):
    _, _, rows, wide = mine.shape
    width = 32 * rows
    return call(
        chain,
        functools.partial(place_first_kernel, cols, count),
        "place_first_weights",
        [mine, other],
        [
            jax.ShapeDtypeStruct((4, 4, 2, rows, cols), mine.dtype),
            jax.ShapeDtypeStruct((4, 2, rows, wide), mine.dtype),
            jax.ShapeDtypeStruct((rows, width), F32),
            jax.ShapeDtypeStruct((2, 32 * rows), F32),
            jax.ShapeDtypeStruct((rows, 8 * rows), F32),
        ],
        scratch=[(4, 4, 2, rows, wide - cols)],
    )


def plane_swap(values, shift):
    return lax.ppermute(values, PLANE, [(i, i ^ shift) for i in range(4)])


def z_swap(values, shift):
    groups = lax.axis_size("z")
    return lax.ppermute(values, "z", [(z, z ^ shift) for z in range(groups)])


def core_swap(values):
    return lax.ppermute(values, "core", [(0, 1), (1, 0)])


def plane_gather(values):
    return [values] + [plane_swap(values, k) for k in (1, 2, 3)]


def tie(*values):
    return lax.optimization_barrier(values)


def plane_send(spreads):
    return [spreads[0]] + [plane_swap(spreads[k], k) for k in (1, 2, 3)]


def plane_total(sent):
    total = sent[0]
    for part in sent[1:]:
        total = total + part.astype(F32)
    return total


class Layout:
    def __init__(self, groups, rows):
        self.groups = groups
        self.devices = groups * 8
        self.subs = groups // rows

    def index(self, z, y, x, c):
        return ((z * 2 + y) * 2 + x) * 2 + c

    def token_moves(self):
        moves = []
        for z in range(self.groups):
            for y in range(2):
                for x in range(2):
                    for c in range(2):
                        row, block = 2 * x + c, 2 * z + y
                        group, within = row * self.subs + block // 8, block % 8
                        core, part = within // 4, within % 4
                        moves.append(
                            (self.index(z, y, x, c), self.index(group, part % 2, part // 2, core))
                        )
        return moves

    def back_moves(self):
        return [(b, a) for a, b in self.token_moves()]

    def turn_moves(self):
        moves = []
        for part in range(4):
            for z in range(self.groups):
                owner, user = part * self.groups + z, z * 4 + part
                moves.append((owner, user))
        return moves


def on_device(lay, core, part, sub, params, tokens):
    (
        enc_qkv,
        enc_out_w,
        enc_attn_bias,
        enc_up,
        enc_up_bias,
        enc_down,
        enc_down_bias,
        enc_gains,
        enc_shifts,
        self_qkv,
        self_out,
        self_bias,
        cross_qkv,
        cross_out,
        cross_bias,
        dec_up,
        dec_up_bias,
        dec_down,
        dec_down_bias,
        dec_gains,
        dec_shifts,
    ) = params
    src, tgt, src_seg, tgt_seg, out_grad = tokens
    groups = lay.groups
    width = src.shape[1]
    rows = enc_out_w.shape[0]
    rows_ff = enc_down.shape[0]
    quarter = width // 4
    hidden = rows_ff * groups * 2
    heads_out = enc_qkv.shape[0] * quarter

    chain = Chain()
    split = groups == 4
    ids = jnp.concatenate([src_seg, tgt_seg]).astype(BF16)
    ids = jnp.pad(ids[None], ((0, 7), (0, width - 2 * BLOCK)))
    packed = jnp.concatenate([src, ids, tgt, out_grad], axis=0)
    packed = lax.ppermute(packed, AXES, lay.token_moves())

    def heads_split(qkv):
        parts = qkv.reshape(3, rows, 4, quarter)
        return parts.transpose(2, 1, 0, 3).reshape(4, rows, heads_out)

    def up_split(up):
        parts = up.reshape(rows, groups, 4, 2, rows_ff)
        return parts.transpose(2, 0, 3, 1, 4).reshape(4, rows, hidden)

    def both_cores(mine, axis):
        other = core_swap(mine)
        shape = [1] * (mine.ndim + 1)
        shape[axis] = 2
        which = lax.broadcasted_iota(jnp.int32, shape, axis) == core
        return jnp.where(which, jnp.expand_dims(mine, axis), jnp.expand_dims(other, axis))

    def whole(kind, piece):
        cols = piece.shape[-1]
        piece = lax.all_gather(piece, "z", axis=0)
        return both_cores(piece, {"rows": 2, "down": 0, "out": 1}[kind]).reshape(-1, cols)

    def plane_turn(values):
        return lax.all_to_all(values, PLANE, split_axis=0, concat_axis=0, tiled=True)

    def out_turn(values):
        return lax.ppermute(values, ("z", "y", "x"), lay.turn_moves())

    vectors = jnp.concatenate(
        [
            enc_attn_bias,
            self_bias,
            cross_bias,
            enc_down_bias[None],
            dec_down_bias[None],
            enc_gains,
            dec_gains,
            enc_shifts,
            dec_shifts,
        ],
        axis=0,
    )
    vector_count = vectors.shape[0]
    if split:
        wide = width - heads_out
        extra = jnp.concatenate(
            [
                jnp.pad(vectors, ((0, 0), (0, wide - rows))),
                jnp.pad(jnp.stack([enc_up_bias, dec_up_bias]), ((0, 1), (0, wide - rows_ff))),
            ],
            axis=0,
        )
        extra = jnp.broadcast_to(extra[None], (4, rows, wide))
        first = plane_turn(jnp.concatenate([heads_split(enc_qkv), extra], axis=2))
        rest = jnp.concatenate(
            [heads_split(self_qkv), heads_split(cross_qkv), up_split(enc_up), up_split(dec_up)],
            axis=2,
        )
        first, rest = tie(first, rest)
        rest = plane_turn(rest).reshape(4 * rows, -1)
        outs = out_turn(jnp.concatenate([enc_out_w, self_out, cross_out], axis=0))
        turned, outs = outs[:rows], outs[rows:]
        first, packed = tie(first, packed)
        first = jnp.concatenate([first, turned[None]], axis=0)
        far = z_swap(first, 2)
        blocks = plane_gather(packed[: BLOCK + 8])
        far, blocks, rest = tie(far, blocks, rest)
        first = jnp.stack([first, far])
        first = jnp.concatenate([first, z_swap(first, 1)], axis=0)
        narrow = ((0, 0), (0, width - heads_out))
        w_self = jnp.pad(rest[:, :heads_out], narrow)
        w_cross = jnp.pad(rest[:, heads_out : 2 * heads_out], narrow)
        up = rest[:, 2 * heads_out : 2 * heads_out + hidden]
        one = jnp.concatenate([up, enc_down, outs, w_self], axis=0)
        one = lax.all_gather(one, "z", axis=0)
        up = rest[:, 2 * heads_out + hidden :]
        two = jnp.concatenate([up, dec_down, w_cross], axis=0)
        two = lax.all_gather(two, "z", axis=0)
        ffn_plan = [("rows", 0, 0), ("down", 4 * rows, 0)]
        ffn_shapes = [(rows, hidden), (rows_ff, width)]
        row = 4 * rows + rows_ff

    start = BLOCK + 8
    src, tgt, out_grad = packed[:BLOCK], packed[start : start + BLOCK], packed[start + BLOCK :]
    if not split:
        blocks = plane_gather(packed[:start])
    src_rows = [block[:BLOCK] for block in blocks]
    doc = jnp.concatenate([block[BLOCK : BLOCK + 1] for block in blocks], axis=0)
    doc = doc[:, : 2 * BLOCK].astype(F32).reshape(4, 2, BLOCK)
    count = jnp.stack(
        [
            jnp.sum((doc < 0.5).astype(F32), axis=(0, 2)),
            jnp.sum((doc < 1.5).astype(F32), axis=(0, 2)),
        ]
    )
    count = jnp.pad(count, ((0, 6), (0, BLOCK - 2)))
    count = count + core_swap(count)
    total = count
    for j in range(1, lay.subs):
        total = total + z_swap(count, j)
    count = total.astype(jnp.int32)

    if split:
        w_enc, wo_enc, vectors, ups, mine = place_first(
            chain, first, core_swap(first), heads_out, vector_count
        )
        w_enc, wo_enc = w_enc.reshape(width, heads_out), wo_enc.reshape(quarter, width)
    else:
        w_enc = whole("rows", plane_turn(heads_split(enc_qkv)))
        vectors = jnp.concatenate([vectors.reshape(-1), enc_up_bias, dec_up_bias])[None]
        vectors = lax.all_gather(vectors, AXES, axis=0, tiled=True).astype(F32)
        ups = vectors[:, vector_count * rows :].reshape(groups, 4, 2, 2, rows_ff)
        ups = lax.dynamic_index_in_dim(ups, part, axis=1, keepdims=False)
        ups = ups.transpose(2, 1, 0, 3).reshape(2, hidden)
        vectors = vectors[:, : vector_count * rows].reshape(lay.devices, vector_count, rows)
        vectors = vectors.transpose(1, 0, 2).reshape(vector_count, width)
        mine = lax.dynamic_slice_in_dim(vectors, part * quarter, quarter, axis=1)
        w_self = whole("rows", plane_turn(heads_split(self_qkv)))
        outs = out_turn(jnp.concatenate([enc_out_w, self_out, cross_out], axis=1))
        outs = whole("out", outs)
        wo_enc, wo_self, wo_cross = (outs[:, k * width : (k + 1) * width] for k in range(3))
        w_up_enc = whole("rows", plane_turn(up_split(enc_up)))
        w_down_enc = whole("down", enc_down)
        w_cross = whole("rows", plane_turn(heads_split(cross_qkv)))
        w_up_dec = whole("rows", plane_turn(up_split(dec_up)))
        w_down_dec = whole("down", dec_down)

    row_view = (4, 4, 2, rows)

    def with_others(kv):
        kv = [kv, core_swap(kv)]
        return kv + [z_swap(half, j) for j in range(1, lay.subs) for half in kv]

    def own_part(halves):
        own, other = halves[:2]
        for j in range(1, lay.subs):
            own = own + z_swap(halves[2 * j], j)
            other = other + z_swap(halves[2 * j + 1], j)
        return own, core_swap(other)

    enc_form, self_form, cross_form = (0, 0, False), (1, 1, True), (1, 0, False)
    q_enc, kv_enc, src_rows = project(chain, 0, src_rows, w_enc, mine)
    kv_enc = with_others(kv_enc)
    enc_saved, sent = attn_forward(chain, enc_form, count, q_enc, kv_enc, wo_enc)
    tgt_rows = plane_gather(tgt)
    sent = plane_send(sent)
    r_enc1, e1_low = norm(chain, src, sent, vectors, 2, (11, 16))
    e1_rows = plane_gather(e1_low)
    if split:
        e1_rows, one = tie(e1_rows, one)
        w_up_enc, w_down_enc, wo_self, wo_cross, w_self = place(
            chain,
            ffn_plan + [("out", row, 0), ("out", row + rows, 0), ("rows", row + 2 * rows, 0)],
            ffn_shapes + [(rows, width)] * 2 + [(rows, heads_out)],
            False,
            one,
            core_swap(one),
        )
    q_self, kv_self, tgt_rows = project(chain, 3, tgt_rows, w_self, mine)
    kv_self = with_others(kv_self)
    self_saved, mates = attn_forward(chain, self_form, count, q_self, kv_self, wo_self)
    e1_rows, sent = ffn_forward(chain, 0, e1_rows, w_up_enc, ups, w_down_enc, mates[1:])
    sent = plane_send(sent)
    r_enc2, encoded_low = norm(chain, r_enc1, sent, vectors, 9, (12, 17), (11, 16))
    sent = [mates[0], *sent[1:]]
    r_dec1, both_low = norm(
        chain, tgt, sent, vectors, 5, (13, 18), start=BLOCK, mate=(encoded_low,)
    )
    if split:
        both_low, two = tie(both_low, two)
    both_rows = plane_gather(both_low)
    if split:
        w_up_dec, w_down_dec, w_cross = place(
            chain,
            ffn_plan + [("rows", row, 0)],
            ffn_shapes + [(rows, heads_out)],
            False,
            two,
            core_swap(two),
        )
    q_cross, kv_cross, both_rows = project(chain, 6, both_rows, w_cross, mine, q_start=BLOCK)
    kv_cross = with_others(kv_cross)
    cross_saved, sent = attn_forward(chain, cross_form, count, q_cross, kv_cross, wo_cross)
    sent = plane_send(sent)
    r_dec2, t2_low = norm(chain, r_dec1, sent, vectors, 8, (14, 19), (13, 18))
    t2_rows = plane_gather(t2_low)
    t2_rows, sent = ffn_forward(chain, 1, t2_rows, w_up_dec, ups, w_down_dec)
    sent = plane_send(sent)
    r_dec3, t3_low = norm(chain, r_dec2, sent, vectors, 10, (15, 20), (14, 19))

    heads_view = row_view + (heads_out + BLOCK,)
    up_view = row_view + (hidden,)
    down_view = (2, 4, rows_ff, width)
    out_view = (4, 2, rows, width)
    if not split:
        heads_view, up_view = (width, heads_out), (width, hidden)
        down_view, out_view = (hidden, width), (quarter, width)

    def core_send(grad, kind):
        if split:
            return grad[0], core_swap(grad[1])
        axis = {"rows": 2, "down": 0, "out": 1}[kind]
        shape = {
            "rows": (groups, 4, 2, rows, -1),
            "down": (2, groups, rows_ff, width),
            "out": (groups, 2, rows, width),
        }[kind]
        grad = grad[0].reshape(shape)
        zero = lax.index_in_dim(grad, 0, axis, keepdims=False)
        one = lax.index_in_dim(grad, 1, axis, keepdims=False)
        send = jnp.where(core == 0, one, zero).astype(BF16)
        return jnp.where(core == 0, zero, one), core_swap(send)

    def stacked(*sends):
        keeps, gots = [x[0] for x in sends], [x[1] for x in sends]
        if split:
            return combine(chain, keeps, gots, width)
        sums = []
        for keep, got in zip(keeps, gots, strict=True):
            total = (keep + got.astype(F32)).astype(BF16)
            total = total.reshape(groups, -1, total.shape[-1])
            sums.append(jnp.pad(total, ((0, 0), (0, 0), (0, width - total.shape[-1]))))
        return jnp.concatenate(sums, axis=1)

    def z_reduce(grad):
        return lax.psum_scatter(grad, "z", scatter_dimension=0, tiled=False)

    def home(values):
        return lax.ppermute(values, AXES, lay.back_moves())

    def ffn_sends(bias, up, down):
        sends = [core_send(up, "rows"), core_send(down, "down")]
        if split:
            sends.append(core_send(bias, "bias"))
        return sends

    d_r3, low3, sums3 = norm_back(chain, [out_grad], r_dec3, vectors, 15)
    spreads, *grads = ffn_backward(
        chain, 1, split, t2_rows, plane_gather(low3), w_up_dec, ups, w_down_dec, up_view, down_view
    )
    upb_dec = grads[0]
    sent = plane_send(spreads)
    sends = ffn_sends(*grads)
    sent, sends = tie(sent, sends)
    d_r2, low2, sums2 = norm_back(chain, [d_r3, *sent], r_dec2, vectors, 14)

    low2_rows = plane_gather(low2)
    dec_sends = sends
    dq, dkv, g_wo_cross = attn_backward(
        chain, cross_form, split, count, cross_saved, low2_rows, out_view
    )
    spreads, g_bias_cross, g_cross = project_back(
        chain,
        split,
        both_rows,
        w_cross,
        dq,
        *own_part(dkv),
        heads_view,
        [sums2, sums3],
        ((0, 2, 2), (1, 2, 3), (1, 0, 4), (1, 1, 5), (0, 0, 6), (0, 1, 7)),
    )
    sent = plane_send(spreads[1:])
    sends = [core_send(g_cross, "rows"), core_send(g_wo_cross, "out")]
    decoded = home(t3_low)
    sent, sends, decoded = tie(sent, sends, decoded)

    d_e2, low_e2, sums_e2 = norm_back(chain, sent, r_enc2, vectors, 12)
    d_r1, both_low, sums1 = norm_back(
        chain, [d_r2, spreads[0], *sent[1:]], r_dec1, vectors, 13, start=BLOCK, mate=(low_e2,)
    )
    both_grads = plane_gather(both_low)
    decoder = z_reduce(stacked(*dec_sends, *sends))
    spreads, *grads = ffn_backward(
        chain, 0, split, e1_rows, both_grads, w_up_enc, ups, w_down_enc, up_view, down_view
    )
    upb_enc = grads[0]
    sent = plane_send(spreads)
    sends = ffn_sends(*grads)
    dq_self, dkv_self, g_wo_self = attn_backward(
        chain, self_form, split, count, self_saved, both_grads, out_view, start=BLOCK
    )
    enc_sends = sends
    if split:
        enc_own, enc_far, enc_near = group_sums(chain, enc_sends, width)
        enc_near = z_swap(enc_near, 1)
    d_r1e, low_e1, sums_e1 = norm_back(chain, [d_e2, *sent], r_enc1, vectors, 11)

    low_e1_rows = plane_gather(low_e1)
    if split:
        enc_far = z_swap(rounded_total(chain, [enc_far, enc_near[1]]), 2)
    spreads_self, g_bias_self, g_self = project_back(
        chain,
        split,
        tgt_rows,
        w_self,
        dq_self,
        *own_part(dkv_self),
        heads_view,
        [sums1, sums_e2],
        ((0, 2, 2), (1, 2, 3), (0, 0, 4), (0, 1, 5), (1, 0, 6), (1, 1, 7)),
    )
    self_sends = [core_send(g_self, "rows"), core_send(g_wo_self, "out")]
    if split:
        low_e1_rows, enc_far = tie(low_e1_rows, enc_far)
    own_self, decoder = tie(stacked(*self_sends), decoder)
    own_self = z_reduce(own_self)
    tall = decoder.shape[0] - 5 * rows
    dec_ffn, cross = decoder[:tall], decoder[tall:]
    dq_enc, dkv_enc, g_wo_enc = attn_backward(
        chain, enc_form, split, count, enc_saved, low_e1_rows, out_view
    )
    spreads, g_bias_enc, g_enc = project_back(
        chain,
        split,
        src_rows,
        w_enc,
        dq_enc,
        *own_part(dkv_enc),
        heads_view,
        [sums_e1],
        ((0, 2, 2), (0, 0, 4), (0, 1, 5)),
        mates=spreads_self[1:],
    )
    g_enc, g_wo_enc = core_send(g_enc, "rows"), core_send(g_wo_enc, "out")
    sent = plane_send(spreads)

    if split:
        own_sum, far_sum, near = shares(chain, g_enc, g_wo_enc, width)
        near = z_swap(near, 1)
        near, decoder = tie(near, decoder)
        dec_ffn, cross = decoder[:tall], decoder[tall:]
        enc_ffn = rounded_total(chain, [enc_own, enc_near[0], enc_far])
        far_sum = z_swap(rounded_total(chain, [far_sum, near[1]]), 2)
        homes = both_totals(chain, [d_r1e, sent[0], d_r1, spreads_self[0], *sent[1:]])
        parts = jnp.concatenate(
            [
                dec_ffn[: 4 * rows].reshape(4, rows, hidden),
                cross[: 4 * rows, : heads_out + BLOCK].reshape(4, rows, heads_out + BLOCK),
            ],
            axis=2,
        )
        g_dec_up, g_cross_qkv, cross_lines = join_layer(chain, plane_turn(parts), heads_out)
        last = rounded_total(chain, [own_sum, near[0], far_sum])
        parts = jnp.concatenate(
            [
                enc_ffn[: 4 * rows].reshape(4, rows, hidden),
                own_self[: 4 * rows, : heads_out + BLOCK].reshape(4, rows, heads_out + BLOCK),
                last[:4],
            ],
            axis=2,
        )
        parts = plane_turn(parts)
        outs = jnp.concatenate([last[4], own_self[4 * rows :], cross[4 * rows :]], axis=0)
        outs = lax.ppermute(outs, ("z", "y", "x"), [(b, a) for a, b in lay.turn_moves()])
        outs = outs.astype(F32)
        grads, small = join_last(chain, parts, cross_lines, heads_out)
        g_enc_up, g_self_qkv, g_enc_qkv = grads
        small = [x[0] if x.shape[0] == 1 else x for x in small]
        tail = 4 * rows + rows_ff
        g_upb_enc, g_upb_dec = (x[tail, :rows_ff].astype(F32) for x in (enc_ffn, dec_ffn))
        g_enc_down, g_dec_down = (x[4 * rows : tail].astype(F32) for x in (enc_ffn, dec_ffn))
    else:

        def heads_join(parts):
            parts = plane_turn(parts[:, :heads_out].reshape(4, rows, heads_out))
            parts = parts.reshape(4, rows, 3, quarter).transpose(2, 1, 0, 3)
            return parts.reshape(3, rows, width).astype(F32)

        def up_join(parts):
            parts = plane_turn(parts.reshape(4, rows, hidden))
            parts = parts.reshape(4, rows, 2, groups, rows_ff).transpose(1, 3, 0, 2, 4)
            return parts.reshape(rows, -1).astype(F32)

        homes = both_totals(chain, [d_r1e, sent[0], d_r1, spreads_self[0], *sent[1:]])
        last = z_reduce(stacked(g_enc, g_wo_enc))
        enc_ffn = z_reduce(stacked(*enc_sends))
        g_dec_up, g_enc_up = up_join(dec_ffn[: 4 * rows]), up_join(enc_ffn[: 4 * rows])
        g_enc_down, g_dec_down = (x[4 * rows :].astype(F32) for x in (enc_ffn, dec_ffn))
        g_cross_qkv, g_self_qkv, g_enc_qkv = (
            heads_join(x[: 4 * rows]) for x in (cross, own_self, last)
        )
        outs = jnp.concatenate([x[4 * rows :] for x in (last, own_self, cross)], axis=0)
        outs = lax.ppermute(outs, ("z", "y", "x"), [(b, a) for a, b in lay.turn_moves()])
        outs = outs.astype(F32)
        placed = jnp.concatenate([g_bias_enc[:2], g_bias_self[:2], g_bias_cross[:2]], axis=0)
        placed = lax.dynamic_update_slice(
            jnp.zeros((6, width), F32), placed, (jnp.int32(0), part * quarter)
        )
        lines = jnp.concatenate(
            [placed, sums_e1[:3], sums_e2[:3], sums1[:3], sums2[:3], sums3[:3]], axis=0
        )
        line_count = lines.shape[0]
        lines = lines.reshape(line_count, lay.devices, rows).transpose(1, 0, 2)
        lines = lines.reshape(lay.devices, line_count * rows)
        upb = jnp.concatenate([upb_enc[0], upb_dec[0]]).reshape(2, 2, groups, rows_ff)
        upb = lax.dynamic_update_slice(
            jnp.zeros((groups, 4, 2, 2, rows_ff), F32),
            upb.transpose(2, 1, 0, 3)[:, None],
            (jnp.int32(0), part, jnp.int32(0), jnp.int32(0), jnp.int32(0)),
        )
        lines = jnp.concatenate([lines, upb.reshape(lay.devices, 2 * rows_ff)], axis=1)
        lines = lax.all_to_all(lines, AXES, split_axis=0, concat_axis=0, tiled=True)
        lines = jnp.sum(lines, axis=0)
        upb = lines[line_count * rows :]
        g_upb_enc, g_upb_dec = upb[:rows_ff], upb[rows_ff:]
        lines = lines[: line_count * rows].reshape(line_count, rows)
        small = [
            jnp.stack([lines[0], lines[1], lines[8]]),
            lines[11],
            jnp.stack([lines[6], lines[9]]),
            jnp.stack([lines[7], lines[10]]),
            jnp.stack([lines[2], lines[3], lines[14]]),
            jnp.stack([lines[4], lines[5], lines[17]]),
            lines[20],
            jnp.stack([lines[12], lines[15], lines[18]]),
            jnp.stack([lines[13], lines[16], lines[19]]),
        ]
    g_enc_out, g_self_out, g_cross_out = outs[:rows], outs[rows : 2 * rows], outs[2 * rows :]

    homes = home(homes)
    bias_enc, down_enc, gains_enc, shifts_enc = small[:4]
    bias_self, bias_cross, down_dec, gains_dec, shifts_dec = small[4:]
    return (
        decoded[None],
        homes[None, :BLOCK].astype(F32),
        homes[None, BLOCK:].astype(F32),
        g_enc_qkv,
        g_enc_out,
        bias_enc,
        g_enc_up,
        g_upb_enc,
        g_enc_down,
        down_enc,
        gains_enc,
        shifts_enc,
        g_self_qkv,
        g_self_out,
        bias_self,
        g_cross_qkv,
        g_cross_out,
        bias_cross,
        g_dec_up,
        g_upb_dec,
        g_dec_down,
        down_dec,
        gains_dec,
        shifts_dec,
    )


def solution(mesh):
    groups = mesh.shape["seq"] // 2
    rows = mesh.shape["dp"]
    lay = Layout(groups, rows)
    fine = Mesh(mesh.devices.reshape(groups, 2, 2, 2), AXES)
    seq, dp = ("z", "y"), ("x", "core")

    def run(
        src,
        tgt,
        src_seg,
        tgt_seg,
        enc_qkv,
        enc_out_w,
        enc_attn_bias,
        enc_up,
        enc_up_bias,
        enc_down,
        enc_down_bias,
        enc_gains,
        enc_shifts,
        self_qkv,
        self_out,
        self_bias,
        cross_qkv,
        cross_out,
        cross_bias,
        dec_up,
        dec_up_bias,
        dec_down,
        dec_down_bias,
        dec_gains,
        dec_shifts,
        out_grad,
    ):
        core = lax.axis_index("core")
        part = 2 * lax.axis_index("y") + lax.axis_index("x")
        sub = lax.axis_index("z") % lay.subs
        params = (
            enc_qkv,
            enc_out_w,
            enc_attn_bias,
            enc_up,
            enc_up_bias,
            enc_down,
            enc_down_bias,
            enc_gains,
            enc_shifts,
            self_qkv,
            self_out,
            self_bias,
            cross_qkv,
            cross_out,
            cross_bias,
            dec_up,
            dec_up_bias,
            dec_down,
            dec_down_bias,
            dec_gains,
            dec_shifts,
        )
        return on_device(
            lay, core, part, sub, params, (src[0], tgt[0], src_seg[0], tgt_seg[0], out_grad[0])
        )

    token = P(dp, seq, None)
    ids = P(dp, seq)
    stack = P(None, AXES, None)
    mat = P(AXES, None)
    vecs = P(None, AXES)
    vec = P(AXES)
    in_specs = (
        (token, token, ids, ids)
        + (stack, mat, vecs, mat, vec, mat, vec, vecs, vecs)
        + (stack, mat, vecs, stack, mat, vecs, mat, vec, mat, vec, vecs, vecs)
        + (token,)
    )
    out_specs = (
        (token, token, token)
        + (stack, mat, vecs, mat, vec, mat, vec, vecs, vecs)
        + (stack, mat, vecs, stack, mat, vecs, mat, vec, mat, vec, vecs, vecs)
    )
    return jax.shard_map(run, mesh=fine, in_specs=in_specs, out_specs=out_specs, check_vma=False)
```
